32 devices in a mesh: dp: 8 (over z, x), fsdp: 4 (over y, core).
Axes of the slice: x: 2, y: 2, z: 4, core: 2. Of those that a mesh axis runs over, the one named last changes fastest.
Arguments:
- tokens: bfloat16 [8192, 2048], P(('dp', 'fsdp')), may hold values from -6 to 6
- segments: int32 [8192], P(('dp', 'fsdp')), may hold values from 0 to 3, as said below
- gain_attn: float32 [2048], P('dp'), may hold values from 0.1 to 1.9
- w_query: float32 [2048, 2048], P('dp', 'fsdp'), may hold values from -0.125 to 0.125
- w_key: float32 [2048, 256], P('dp', 'fsdp'), may hold values from -0.125 to 0.125
- w_value: float32 [2048, 256], P('dp', 'fsdp'), may hold values from -0.125 to 0.125
- w_out: float32 [2048, 2048], P('fsdp', 'dp'), may hold values from -0.75 to 0.75
- gain_mlp: float32 [2048], P('dp'), may hold values from 0.1 to 1.9
- w_gate: float32 [2048, 5632], P('dp', 'fsdp'), may hold values from -0.125 to 0.125
- w_up: float32 [2048, 5632], P('dp', 'fsdp'), may hold values from -0.125 to 0.125
- w_down: float32 [5632, 2048], P('fsdp', 'dp'), may hold values from -0.078125 to 0.078125
- cotangent: bfloat16 [8192, 2048], P(('dp', 'fsdp')), may hold values from -6 to 6
Outputs:
- layer_out: bfloat16 [8192, 2048], P(('dp', 'fsdp'))
- grad_tokens: bfloat16 [8192, 2048], P(('dp', 'fsdp'))
- grad_gain_attn: float32 [2048], P('dp')
- grad_w_query: float32 [2048, 2048], P('dp', 'fsdp')
- grad_w_key: float32 [2048, 256], P('dp', 'fsdp')
- grad_w_value: float32 [2048, 256], P('dp', 'fsdp')
- grad_w_out: float32 [2048, 2048], P('fsdp', 'dp')
- grad_gain_mlp: float32 [2048], P('dp')
- grad_w_gate: float32 [2048, 5632], P('dp', 'fsdp')
- grad_w_up: float32 [2048, 5632], P('dp', 'fsdp')
- grad_w_down: float32 [5632, 2048], P('fsdp', 'dp')
The draws below stay inside these ranges and needn't reach their ends.
Inputs may be any that keep to these rules, and one draw needn't show every extreme that they name: `segments`: on each device's 256 tokens the ids number 1 to 4 whole sequences from 0 up, never falling; every sequence has 64, 128 or 256 tokens; some device holds one sequence and some four.
All inputs are finite; a program needn't handle non-finite values.
Results may differ from the reference program's by a relative error of at most 0.02.
Values may be sent and summed in bfloat16 or wider, within the bound.
No kernel may reach another device: no remote copies, remote signals or barrier semaphores. Data moves between devices by JAX's collectives and lax.ppermute only.
A program may use at most 448 MiB of HBM per device.

```python
import math
import jax
import jax.numpy as jnp
from jax import lax

D = 2048
HEADS = 32
KV_HEADS = 4
HEAD_DIM = 64
FF = 5632
TOK_DEV = 256
TOKENS = 8192


def draw_segments(key, part):
    devices_count = TOKENS // TOK_DEV
    layouts = jnp.array([[0, 0, 0, 0], [0, 0, 1, 1], [0, 0, 1, 2], [0, 1, 1, 2], [0, 1, 2, 2], [0, 1, 2, 3]], dtype=jnp.int32)
    picks = jax.random.randint(jax.random.fold_in(key, 11), (devices_count,), 0, 6)
    order = jax.random.permutation(jax.random.fold_in(key, 12), devices_count)
    picks = picks.at[order[0]].set(0).at[order[1]].set(5)
    units = layouts[picks]
    return jnp.repeat(units, TOK_DEV // 4, axis=1).reshape(TOKENS).astype(jnp.int32)


def strengthened(drawn, own_key, source, target, shards_of, factor):
    owner, partner = [(jnp.arange(drawn.shape[dim]) // (drawn.shape[dim] // shards_of)).reshape([-1 if axis == dim else 1 for axis in range(drawn.ndim)]) for dim in (source, target)]
    chosen = jax.random.permutation(own_key, shards_of)[partner]
    strong = (owner == chosen) | (owner == (partner + shards_of // 2) % shards_of)
    return jnp.where(strong, factor * drawn, drawn)


def level_of(key, dims, shards, least, largest):
    level = 1.0
    for position, shards_of in shards:
        heights = jax.random.uniform(jax.random.fold_in(jax.random.fold_in(key, 6), position), (shards_of,), jnp.float32, least / len(shards), largest / len(shards))
        level = level * jnp.repeat(jnp.exp(heights), dims[position] // shards_of).reshape((-1,) + (1,) * (len(dims) - 1 - position))
    return level


def normal_values(stream_key, extent, deviation, most, cuts=(), kind=jnp.bfloat16):
    entries = deviation * jax.random.normal(stream_key, extent, jnp.float32)
    if cuts:
        entries = entries * level_of(stream_key, extent, cuts, -0.22, 0.18)
    return jnp.clip(entries, -most, most).astype(kind)


def gaussian_with(rng, dims, scale, limit, split, heavy, held_as=jnp.bfloat16):
    entries = scale * jax.random.normal(rng, dims, jnp.float32)
    if split:
        entries = entries * level_of(rng, dims, split, -0.22, 0.18)
    return jnp.clip(strengthened(entries, jax.random.fold_in(rng, 3), *heavy), -limit, limit).astype(held_as)


def setup_inputs(seed: int = 0) -> dict:
    key_list = jax.random.split(jax.random.key(seed), 13)
    return {
        "tokens": gaussian_with(key_list[0], (TOKENS, D), 1.0, 6.0, ((0, 32),), (0, 1, 32, 2.75)),
        "segments": draw_segments(jax.random.fold_in(key_list[12], 71), 0),
        "gain_attn": jnp.clip(1.0 + 0.18 * jax.random.normal(key_list[2], (D,), jnp.float32), 0.1, 1.9),
        "w_query": normal_values(key_list[3], (D, D), D ** -0.5, 0.125, ((0, 8), (1, 4)), jnp.float32),
        "w_key": normal_values(key_list[4], (D, KV_HEADS * HEAD_DIM), D ** -0.5, 0.125, ((0, 8), (1, 4)), jnp.float32),
        "w_value": normal_values(key_list[5], (D, KV_HEADS * HEAD_DIM), D ** -0.5, 0.125, ((0, 8), (1, 4)), jnp.float32),
        "w_out": normal_values(key_list[6], (D, D), (D // 32) ** -0.5, 0.75, ((0, 4), (1, 8)), jnp.float32),
        "gain_mlp": jnp.clip(1.0 + 0.18 * jax.random.normal(key_list[7], (D,), jnp.float32), 0.1, 1.9),
        "w_gate": normal_values(key_list[8], (D, FF), D ** -0.5, 0.125, ((0, 8), (1, 4)), jnp.float32),
        "w_up": normal_values(key_list[9], (D, FF), D ** -0.5, 0.125, ((0, 8), (1, 4)), jnp.float32),
        "w_down": normal_values(key_list[10], (FF, D), FF ** -0.5, 0.078125, ((0, 4), (1, 8)), jnp.float32),
        "cotangent": gaussian_with(key_list[11], (TOKENS, D), 1.0, 6.0, ((0, 32),), (0, 1, 32, 2.75)),
    }


EPSILON = 1e-05
rope_base = 10000.0

@jax.custom_vjp
def low(v):
    return lax.optimization_barrier(v.astype(jnp.bfloat16)).astype(jnp.float32)

@jax.custom_vjp
def low_back(v):
    return v

def low_keep(v):
    return (low(v), None)

def low_pass(kept, grad):
    return (grad,)

def back_keep(v):
    return (v, None)

def back_low(kept, grad):
    return (low(grad),)
low.defvjp(low_keep, low_pass)
low_back.defvjp(back_keep, back_low)

def tables(segment_block):
    rows_here = segment_block.shape[0]
    places = jnp.arange(rows_here, dtype=jnp.int32)
    same_segment = segment_block[:, None] == segment_block[None, :]
    first_index = lax.optimization_barrier(jnp.min(jnp.where(same_segment, places[None, :], rows_here), axis=1)).astype(jnp.int32)
    offsets = (places - first_index).astype(jnp.float32)
    half_dim = HEAD_DIM // 2
    frequencies = jnp.exp(jnp.arange(half_dim, dtype=jnp.float32) * (-2.0 * math.log(rope_base) / HEAD_DIM))
    angles = offsets[:, None] * frequencies[None, :]
    cosine = jnp.concatenate([jnp.cos(angles), jnp.cos(angles)], axis=1)[:, None, :]
    sine_part = jnp.concatenate([jnp.sin(angles), jnp.sin(angles)], axis=1)[:, None, :]
    allowed = same_segment & (places[:, None] >= places[None, :])
    return (cosine, sine_part, allowed)

def rotate(values, cosine, sine_part):
    half_dim = values.shape[-1] // 2
    turned = jnp.concatenate([-values[..., half_dim:], values[..., :half_dim]], axis=-1)
    return values * cosine + turned * sine_part

def layer(tokens, gain_attn, w_query, w_key, w_value, w_out, gain_mlp, w_gate, w_up, w_down, cosine, sine_part, allowed):
    highest = lax.Precision.HIGHEST
    rows_here = tokens.shape[0]
    group_size = HEADS // KV_HEADS
    inv_first = lax.rsqrt(lax.optimization_barrier(jnp.mean(tokens * tokens, axis=-1, keepdims=True)) + EPSILON)
    normed = low(tokens * inv_first * low(gain_attn))
    query_proj = low_back(jnp.dot(normed, low(w_query), precision=highest)).reshape(rows_here, HEADS, HEAD_DIM)
    keys_proj = low_back(jnp.dot(normed, low(w_key), precision=highest)).reshape(rows_here, KV_HEADS, HEAD_DIM)
    values = low(low_back(jnp.dot(normed, low(w_value), precision=highest))).reshape(rows_here, KV_HEADS, HEAD_DIM)
    query_rot = low(rotate(query_proj, cosine, sine_part)).reshape(rows_here, KV_HEADS, group_size, HEAD_DIM)
    keys_rot = low(rotate(keys_proj, cosine, sine_part))
    scores = low_back(jnp.einsum('tgrd,ugd->grtu', query_rot, keys_rot, precision=highest) * HEAD_DIM ** (-0.5))
    masked = jnp.where(allowed[None, None], scores, -1e+30)
    row_peak = lax.optimization_barrier(jnp.max(masked, axis=-1, keepdims=True))
    exponent = jnp.exp(masked - row_peak)
    weights_soft = exponent / lax.optimization_barrier(jnp.sum(exponent, axis=-1, keepdims=True))
    mixed_heads = jnp.einsum('grtu,ugd->tgrd', low(weights_soft), values, precision=highest).reshape(rows_here, HEADS * HEAD_DIM)
    mixed_heads = low(low_back(mixed_heads))
    branch = low_back(jnp.dot(mixed_heads, low(w_out), precision=highest))
    hidden = tokens + branch
    inv_second = lax.rsqrt(lax.optimization_barrier(jnp.mean(hidden * hidden, axis=-1, keepdims=True)) + EPSILON)
    normed_mlp = low(hidden * inv_second * low(gain_mlp))
    gate_proj = low_back(jnp.dot(normed_mlp, low(w_gate), precision=highest))
    upward = low_back(jnp.dot(normed_mlp, low(w_up), precision=highest))
    activation = low(jax.nn.silu(gate_proj) * upward)
    return hidden + jnp.dot(activation, low(w_down), precision=highest)

def reference(tokens, segments, gain_attn, w_query, w_key, w_value, w_out, gain_mlp, w_gate, w_up, w_down, cotangent):
    blocks = TOKENS // TOK_DEV
    token_blocks = tokens.astype(jnp.float32).reshape(blocks, TOK_DEV, D)
    cotangent_blocks = cotangent.astype(jnp.float32).reshape(blocks, TOK_DEV, D)
    segment_blocks = segments.reshape(blocks, TOK_DEV)
    weights = (gain_attn, w_query, w_key, w_value, w_out, gain_mlp, w_gate, w_up, w_down)

    def block_step(totals, inputs):
        token_block, segment_block, cotangent_block = inputs
        cosine, sine_part, allowed = tables(segment_block)

        def forward(token_input, *parameters):
            return layer(token_input, *parameters, cosine, sine_part, allowed)
        output, pullback = jax.vjp(forward, token_block, *weights)
        gradients = pullback(cotangent_block)
        totals = tuple((total_part + grad_part for total_part, grad_part in zip(totals, gradients[1:])))
        return (totals, (output.astype(jnp.bfloat16), gradients[0].astype(jnp.bfloat16)))
    initial = tuple((jnp.zeros_like(weight) for weight in weights))
    totals, outputs = lax.scan(block_step, initial, (token_blocks, segment_blocks, cotangent_blocks))
    layer_out = outputs[0].reshape(TOKENS, D)
    grad_tokens = outputs[1].reshape(TOKENS, D)
    return (layer_out, grad_tokens, totals[0], totals[1], totals[2], totals[3], totals[4], totals[5], totals[6], totals[7], totals[8])
```

```python
import math

import jax
import jax.numpy as jnp
from jax import lax
from jax.experimental import pallas as pl
from jax.experimental.pallas import tpu as pltpu
from jax.sharding import PartitionSpec as P

HEAD_DIM = 64
EPSILON = 1e-05
ROPE_BASE = 10000.0
LOW = jnp.bfloat16
WIDE = jnp.float32
LANES = 128


def ring_order(n):
    return list(range(0, n, 2)) + list(range(n - 1, 0, -2))


def ring_perms(n):
    order = ring_order(n)
    forward = [(order[i], order[(i + 1) % n]) for i in range(n)]
    return forward, [(b, a) for a, b in forward]


def place_of(index, n):
    return jnp.where(index % 2 == 0, index // 2, n - (index + 1) // 2)


def index_at(place, n):
    return jnp.where(place < n // 2, 2 * place, 2 * (n - place) - 1)


def ring_gather(own, n):
    forward, backward = ring_perms(n)
    half = own.shape[0] // 2
    chunks = [None] * n
    chunks[0] = own
    ahead = behind = own
    for hop in range(1, n // 2):
        ahead = lax.ppermute(ahead, "dp", forward)
        behind = lax.ppermute(behind, "dp", backward)
        chunks[n - hop] = ahead
        chunks[hop] = behind
    top = lax.ppermute(ahead[:half], "dp", forward)
    bottom = lax.ppermute(behind[half:], "dp", backward)
    chunks[n // 2] = jnp.concatenate([top, bottom], axis=0)
    return chunks


def ring_reduce(parts, n):
    forward, backward = ring_perms(n)
    half = parts[0].shape[0] // 2
    far = parts[n // 2]
    ahead = lax.ppermute(far[:half], "dp", forward)
    behind = lax.ppermute(far[half:], "dp", backward)
    for hop in range(n // 2 - 1, 0, -1):
        mine_ahead, mine_behind = parts[hop], parts[n - hop]
        if hop == n // 2 - 1:
            ahead = jnp.concatenate([mine_ahead[:half] + ahead, mine_ahead[half:]], axis=0)
            behind = jnp.concatenate([mine_behind[:half], mine_behind[half:] + behind], axis=0)
        else:
            ahead = mine_ahead + ahead
            behind = mine_behind + behind
        ahead = lax.ppermute(ahead, "dp", forward)
        behind = lax.ppermute(behind, "dp", backward)
    return parts[0].astype(WIDE) + ahead.astype(WIDE) + behind.astype(WIDE)


def swap_core(value):
    return lax.ppermute(value, "fsdp", [(i, i ^ 1) for i in range(4)])


def swap_pair(value):
    return lax.ppermute(value, "fsdp", [(i, i ^ 2) for i in range(4)])


def group_gather(own):
    pair = swap_pair(own)
    core = swap_core(own)
    return [own, core, pair, swap_core(pair)]


def group_reduce(partial, rows):
    block = [partial[i * rows : (i + 1) * rows] for i in range(4)]
    far = swap_core(block[3])
    near = swap_core(block[1])
    sent = swap_pair(block[2] + far)
    return block[0].astype(WIDE) + near.astype(WIDE) + sent.astype(WIDE)


def turn(values, first_half):
    width = values.shape[-1]
    left = pltpu.roll(values, width - HEAD_DIM // 2, 1)
    right = pltpu.roll(values, HEAD_DIM // 2, 1)
    return jnp.where(first_half, -left, right)


def lane_ids(rows, width):
    return lax.broadcasted_iota(jnp.int32, (rows, width), 1)


def allowed_pairs(column, row):
    rows = column.shape[0]
    later = lax.broadcasted_iota(jnp.int32, (rows, rows), 0)
    earlier = lax.broadcasted_iota(jnp.int32, (rows, rows), 1)
    return (column == row) & (later >= earlier)


def dot_rows(a, b):
    return lax.dot_general(a, b, (((1,), (1,)), ((), ())), preferred_element_type=WIDE)


def dot_firsts(a, b):
    return lax.dot_general(a, b, (((0,), (0,)), ((), ())), preferred_element_type=WIDE)


def attention_forward(qkv_ref, cos_ref, sin_ref, col_ref, row_ref, q_ref, kv_ref, o_ref, lse_ref):
    rows, width = q_ref.shape
    pairs = width // LANES
    cosine, sine = cos_ref[...], sin_ref[...]
    lanes = lane_ids(rows, LANES)
    even = lanes < HEAD_DIM
    first = (lanes % HEAD_DIM) < HEAD_DIM // 2
    keyval = qkv_ref[:, width:]
    keyval_rot = keyval * cosine + turn(keyval, first) * sine
    keyval = jnp.where(even, keyval_rot, keyval)
    kv_ref[...] = keyval.astype(LOW)
    other = pltpu.roll(keyval, HEAD_DIM, 1)
    keys = jnp.where(even, keyval, other).astype(LOW)
    vals = jnp.where(even, other, keyval).astype(LOW)
    allowed = allowed_pairs(col_ref[...], row_ref[0])
    log_sums = jnp.zeros((rows, LANES), WIDE)
    for pair in range(pairs):
        piece = qkv_ref[:, pair * LANES : (pair + 1) * LANES]
        piece = (piece * cosine + turn(piece, first) * sine).astype(LOW)
        q_ref[:, pair * LANES : (pair + 1) * LANES] = piece
        mixed = []
        for side in range(2):
            chosen = jnp.where(even if side == 0 else ~even, piece, jnp.zeros_like(piece))
            scores = dot_rows(chosen, keys) * (HEAD_DIM ** -0.5)
            scores = jnp.where(allowed, scores, -1e30)
            peak = jnp.max(scores, axis=1, keepdims=True)
            powers = jnp.exp(scores - peak)
            total = jnp.sum(powers, axis=1, keepdims=True)
            soft = (powers / total).astype(LOW)
            mixed.append(jnp.dot(soft, vals, preferred_element_type=WIDE))
            log_sums = jnp.where(lanes == 2 * pair + side, peak + jnp.log(total), log_sums)
        o_ref[:, pair * LANES : (pair + 1) * LANES] = jnp.where(even, mixed[0], mixed[1]).astype(LOW)
    lse_ref[...] = log_sums


def attention_backward(q_ref, kv_ref, lse_ref, do_ref, cos_ref, sin_ref, col_ref, row_ref, out_ref):
    rows, width = q_ref.shape
    pairs = width // LANES
    scale = HEAD_DIM ** -0.5
    cosine, sine = cos_ref[...], sin_ref[...]
    lanes = lane_ids(rows, LANES)
    even = lanes < HEAD_DIM
    first = (lanes % HEAD_DIM) < HEAD_DIM // 2
    keyval = kv_ref[...].astype(WIDE)
    other = pltpu.roll(keyval, HEAD_DIM, 1)
    keys = jnp.where(even, keyval, other).astype(LOW)
    vals = jnp.where(even, other, keyval).astype(LOW)
    allowed = allowed_pairs(col_ref[...], row_ref[0])
    log_sums = lse_ref[...]
    grad_keys = jnp.zeros((rows, LANES), WIDE)
    grad_vals = jnp.zeros((rows, LANES), WIDE)
    for pair in range(pairs):
        piece = q_ref[:, pair * LANES : (pair + 1) * LANES]
        grads = do_ref[:, pair * LANES : (pair + 1) * LANES]
        turned = []
        for side in range(2):
            mine = even if side == 0 else ~even
            chosen = jnp.where(mine, piece, jnp.zeros_like(piece))
            chosen_grad = jnp.where(mine, grads, jnp.zeros_like(grads))
            head = 2 * pair + side
            log_sum = log_sums[:, head : head + 1]
            scores = jnp.where(allowed, dot_rows(chosen, keys) * scale, -1e30)
            soft = jnp.exp(scores - log_sum)
            grad_soft = dot_rows(chosen_grad, vals)
            delta = jnp.sum(soft * grad_soft, axis=1, keepdims=True)
            grad_scores = (soft * (grad_soft - delta)).astype(LOW)
            grad_vals = grad_vals + dot_firsts(soft.astype(LOW), chosen_grad)
            grad_keys = grad_keys + dot_firsts(grad_scores, chosen)
            turned.append(jnp.dot(grad_scores, keys, preferred_element_type=WIDE))
        grad_q = jnp.where(even, turned[0], turned[1]) * scale
        grad_q = grad_q * cosine - turn(grad_q, first) * sine
        out_ref[:, pair * LANES : (pair + 1) * LANES] = grad_q.astype(LOW)
    grad_keys = (grad_keys + pltpu.roll(grad_keys, HEAD_DIM, 1)) * scale
    grad_keys = grad_keys * cosine - turn(grad_keys, first) * sine
    grad_vals = grad_vals + pltpu.roll(grad_vals, HEAD_DIM, 1)
    out_ref[:, width:] = jnp.where(even, grad_keys, grad_vals).astype(LOW)


def by_rows(rows, width):
    return pl.BlockSpec((rows, width), lambda i: (i, 0))


def attend(qkv, cosine, sine, column, row, rows):
    total, wide = qkv.shape
    width = wide - LANES
    blocks = total // rows
    return pl.pallas_call(
        attention_forward,
        grid=(blocks,),
        in_specs=[
            by_rows(rows, wide),
            by_rows(rows, LANES),
            by_rows(rows, LANES),
            by_rows(rows, 1),
            pl.BlockSpec((1, 1, rows), lambda i: (i, 0, 0)),
        ],
        out_specs=[by_rows(rows, width), by_rows(rows, LANES), by_rows(rows, width), by_rows(rows, LANES)],
        out_shape=[
            jax.ShapeDtypeStruct((total, width), LOW),
            jax.ShapeDtypeStruct((total, LANES), LOW),
            jax.ShapeDtypeStruct((total, width), LOW),
            jax.ShapeDtypeStruct((total, LANES), WIDE),
        ],
        name="attend",
    )(qkv, cosine, sine, column, row)


def attend_back(query, keyval, log_sums, grads, cosine, sine, column, row, rows):
    total, width = query.shape
    blocks = total // rows
    return pl.pallas_call(
        attention_backward,
        grid=(blocks,),
        in_specs=[
            by_rows(rows, width),
            by_rows(rows, LANES),
            by_rows(rows, LANES),
            by_rows(rows, width),
            by_rows(rows, LANES),
            by_rows(rows, LANES),
            by_rows(rows, 1),
            pl.BlockSpec((1, 1, rows), lambda i: (i, 0, 0)),
        ],
        out_specs=by_rows(rows, width + LANES),
        out_shape=jax.ShapeDtypeStruct((total, width + LANES), LOW),
        name="attend_back",
    )(query, keyval, log_sums, grads, cosine, sine, column, row)


def tables(segment_block):
    rows = segment_block.shape[0]
    places = jnp.arange(rows, dtype=jnp.int32)
    same = segment_block[:, None] == segment_block[None, :]
    first_index = jnp.min(jnp.where(same, places[None, :], rows), axis=1)
    offsets = (places - first_index).astype(WIDE)
    half = HEAD_DIM // 2
    frequencies = jnp.exp(jnp.arange(half, dtype=WIDE) * (-2.0 * math.log(ROPE_BASE) / HEAD_DIM))
    angles = offsets[:, None] * frequencies[None, :]
    cosine, sine = jnp.cos(angles), jnp.sin(angles)
    return jnp.concatenate([cosine] * 4, axis=1), jnp.concatenate([sine] * 4, axis=1)


def mul(a, b):
    return jnp.dot(a, b, preferred_element_type=WIDE)


def on_device(
    tokens, segments, gain_attn, w_query, w_key, w_value, w_out, gain_mlp, w_gate, w_up, w_down, cotangent
):
    n = lax.axis_size("dp")
    rows, depth = tokens.shape
    part = depth // n
    me = lax.axis_index("dp")
    place = place_of(me, n)
    sources = [index_at((place + s) % n, n) for s in range(n)]
    offsets = [(place_of(jnp.int32(j), n) - place) % n for j in range(n)]

    def pick(value, starts):
        return jnp.concatenate(
            [lax.dynamic_slice(value, (0, at * part), (value.shape[0], part)) for at in starts], axis=1
        )

    attn_own = jnp.concatenate([w_query, w_key, w_value, w_out.T], axis=1).astype(LOW)
    gate_up_own = jnp.concatenate([w_gate, w_up], axis=1).astype(LOW)
    down_own = w_down.T.astype(LOW)
    heads_wide = w_query.shape[1]
    qkv_wide = heads_wide + w_key.shape[1] + w_value.shape[1]
    hidden_wide = w_gate.shape[1]

    attn_chunks = ring_gather(attn_own, n)
    gate_up_chunks = ring_gather(gate_up_own, n)
    down_chunks = ring_gather(down_own, n)
    gains = lax.all_gather(jnp.stack([gain_attn, gain_mlp]).astype(LOW), "dp", axis=1, tiled=True)
    gains = pick(gains, sources).astype(WIDE)
    gain_one, gain_two = gains[0:1], gains[1:2]

    own_tokens = pick(tokens, sources)
    own_grads = pick(cotangent, sources)
    token_all = jnp.concatenate(group_gather(own_tokens), axis=0)
    segment_blocks = jnp.stack(group_gather(segments))
    grads_all = jnp.concatenate(group_gather(own_grads), axis=0)
    cosine, sine = jax.vmap(tables)(segment_blocks)
    cosine, sine = cosine.reshape(-1, LANES), sine.reshape(-1, LANES)
    column, row = segment_blocks.reshape(-1, 1), segment_blocks[:, None, :]

    query_key_value = jnp.concatenate([c[:, :qkv_wide] for c in attn_chunks], axis=0)
    out_turned = jnp.concatenate([c[:, qkv_wide:] for c in attn_chunks], axis=0)
    gate = jnp.concatenate([c[:, :hidden_wide] for c in gate_up_chunks], axis=0)
    up = jnp.concatenate([c[:, hidden_wide:] for c in gate_up_chunks], axis=0)
    down_turned = jnp.concatenate(down_chunks, axis=0)

    wide_all = token_all.astype(WIDE)
    inv_all = lax.rsqrt(jnp.mean(wide_all * wide_all, axis=-1, keepdims=True) + EPSILON)
    normed = (wide_all * inv_all * gain_one).astype(LOW)
    qkv = mul(normed, query_key_value)
    query, keyval, mixed, log_sums = attend(qkv, cosine, sine, column, row, rows)
    own_wide = own_tokens.astype(WIDE)
    branch = dot_rows(mixed, out_turned).astype(LOW)
    hidden = own_wide + group_reduce(branch, rows)

    inv_second = lax.rsqrt(jnp.mean(hidden * hidden, axis=-1, keepdims=True) + EPSILON)
    unit_mlp = hidden * inv_second
    normed_mlp = jnp.concatenate(group_gather((unit_mlp * gain_two).astype(LOW)), axis=0)
    gate_proj = mul(normed_mlp, gate)
    upward = mul(normed_mlp, up)
    sigmoid = jax.nn.sigmoid(gate_proj)
    activation = (gate_proj * sigmoid * upward).astype(LOW)
    layer_own = hidden + group_reduce(dot_rows(activation, down_turned).astype(LOW), rows)

    def parts_of(value):
        return [value[s * part : (s + 1) * part] for s in range(n)]

    grad_down = ring_reduce(parts_of(dot_firsts(grads_all, activation).astype(LOW)), n)
    grad_act = mul(grads_all, down_turned)
    grad_gate = (grad_act * upward * sigmoid * (1.0 + gate_proj * (1.0 - sigmoid))).astype(LOW)
    grad_up = (grad_act * gate_proj * sigmoid).astype(LOW)
    grad_w_gate = ring_reduce(parts_of(dot_firsts(normed_mlp, grad_gate).astype(LOW)), n)
    grad_w_up = ring_reduce(parts_of(dot_firsts(normed_mlp, grad_up).astype(LOW)), n)
    grad_normed_mlp = group_reduce((dot_rows(grad_gate, gate) + dot_rows(grad_up, up)).astype(LOW), rows)
    gain_mlp_terms = jnp.sum(grad_normed_mlp * unit_mlp, axis=0, keepdims=True)
    scaled = grad_normed_mlp * gain_two
    grad_hidden = own_grads.astype(WIDE) + inv_second * (
        scaled - unit_mlp * jnp.mean(scaled * unit_mlp, axis=-1, keepdims=True)
    )

    grad_branch = jnp.concatenate(group_gather(grad_hidden.astype(LOW)), axis=0)
    grad_mixed = mul(grad_branch, out_turned).astype(LOW)
    grad_qkv = attend_back(query, keyval, log_sums, grad_mixed, cosine, sine, column, row, rows)
    attn_terms = jnp.concatenate(
        [dot_firsts(normed, grad_qkv).astype(LOW), dot_firsts(grad_branch, mixed).astype(LOW)], axis=1
    )
    grad_attn = ring_reduce(parts_of(attn_terms), n)
    grad_normed = group_reduce(dot_rows(grad_qkv, query_key_value).astype(LOW), rows)
    inv_first = lax.rsqrt(jnp.mean(own_wide * own_wide, axis=-1, keepdims=True) + EPSILON)
    unit_attn = own_wide * inv_first
    gain_attn_terms = jnp.sum(grad_normed * unit_attn, axis=0, keepdims=True)
    scaled = grad_normed * gain_one
    grad_inputs = grad_hidden + inv_first * (
        scaled - unit_attn * jnp.mean(scaled * unit_attn, axis=-1, keepdims=True)
    )

    gain_terms = pick(jnp.concatenate([gain_attn_terms, gain_mlp_terms], axis=0), offsets)
    bit = 1
    while bit < 4:
        gain_terms = gain_terms + lax.ppermute(gain_terms, "fsdp", [(i, i ^ bit) for i in range(4)])
        bit *= 2
    bit = 1
    while bit < n:
        gain_terms = gain_terms + lax.ppermute(gain_terms, "dp", [(i, i ^ bit) for i in range(n)])
        bit *= 2
    gain_own = lax.dynamic_slice(gain_terms, (0, me * part), (2, part))

    key_at, value_at = heads_wide, heads_wide + w_key.shape[1]
    return (
        pick(layer_own.astype(LOW), offsets),
        pick(grad_inputs.astype(LOW), offsets),
        gain_own[0],
        grad_attn[:, :key_at],
        grad_attn[:, key_at:value_at],
        grad_attn[:, value_at:qkv_wide],
        grad_attn[:, qkv_wide:].T,
        gain_own[1],
        grad_w_gate,
        grad_w_up,
        grad_down.T,
    )


def solution(mesh):
    placed = (
        P(("dp", "fsdp"), None),
        P(("dp", "fsdp")),
        P("dp"),
        P("dp", "fsdp"),
        P("dp", "fsdp"),
        P("dp", "fsdp"),
        P("fsdp", "dp"),
        P("dp"),
        P("dp", "fsdp"),
        P("dp", "fsdp"),
        P("fsdp", "dp"),
        P(("dp", "fsdp"), None),
    )
    return jax.shard_map(
        on_device,
        mesh=mesh,
        in_specs=placed,
        out_specs=(
            P(("dp", "fsdp"), None),
            P(("dp", "fsdp"), None),
            P("dp"),
            P("dp", "fsdp"),
            P("dp", "fsdp"),
            P("dp", "fsdp"),
            P("fsdp", "dp"),
            P("dp"),
            P("dp", "fsdp"),
            P("dp", "fsdp"),
            P("fsdp", "dp"),
        ),
        check_vma=False,
    )
```

```python
import functools
import math

import jax
import jax.numpy as jnp
import numpy as np
from jax import lax
from jax.experimental import pallas as pl
from jax.experimental.pallas import tpu as pltpu
from jax.sharding import PartitionSpec as P

HEAD_DIM = 64
EPSILON = 1e-05
ROPE_BASE = 10000.0
LOW = jnp.bfloat16
WIDE = jnp.float32
LANES = 128


def ring_order(n):
    return list(range(0, n, 2)) + list(range(n - 1, 0, -2))


def ring_perms(n):
    order = ring_order(n)
    forward = [(order[i], order[(i + 1) % n]) for i in range(n)]
    return forward, [(b, a) for a, b in forward]


def ring_tables(n):
    order = ring_order(n)
    place = [order.index(j) for j in range(n)]
    sources = [[order[(place[i] + s) % n] for s in range(n)] for i in range(n)]
    offsets = [[(place[j] - place[i]) % n for j in range(n)] for i in range(n)]
    return np.array(sources, np.int32), np.array(offsets, np.int32)


class Line:
    def __init__(self, token):
        self.token = token

    def after(self, *values):
        out = lax.optimization_barrier((*values, self.token))
        return out[0] if len(values) == 1 else out[:-1]

    def passed(self, *values):
        out = lax.optimization_barrier((*values, self.token))
        self.token = out[-1]
        return out[0] if len(values) == 1 else out[:-1]

    def run(self, work, *values):
        result = work(*lax.optimization_barrier((*values, self.token))[:-1])
        if isinstance(result, (tuple, list)):
            return self.passed(*result)
        return self.passed(result)

    def send(self, value, axis, pairs):
        return lax.ppermute(self.after(value), axis, pairs)


class RingGather:
    def __init__(self, line, own, n, split):
        self.line, self.n, self.split = line, n, split
        self.chunks = {0: own}
        self.flying = None

    def start(self, hop):
        n, pairs = self.n, ring_perms(self.n)
        ahead, behind = self.chunks[(n - hop + 1) % n], self.chunks[hop - 1]
        if hop == n // 2:
            ahead, behind = ahead[:, : self.split], behind[:, self.split :]
        self.flying = (self.line.send(ahead, "dp", pairs[0]), self.line.send(behind, "dp", pairs[1]))

    def wait(self, hop):
        ahead, behind = self.line.passed(*self.flying)
        if hop == self.n // 2:
            self.far = (ahead, behind)
        else:
            self.chunks[self.n - hop], self.chunks[hop] = ahead, behind

    def panel(self):
        n = self.n
        near = [self.chunks[s] for s in range(n) if s != n // 2]
        if near[0].shape[0] % LANES == 0:
            return [*near, *self.far]
        far = jnp.concatenate(self.far, axis=1)
        return [jnp.concatenate([*near[: n // 2], far, *near[n // 2 :]], axis=0)]


class RingReduce:
    def __init__(self, line, product, n, split):
        self.line, self.product, self.n, self.split = line, product, n, split
        self.came = ()

    def start(self, hop):
        n, pairs = self.n, ring_perms(self.n)
        part = self.product.shape[0] // n
        if hop == 1:
            far = self.product[n // 2 * part : (n // 2 + 1) * part]
            ahead, behind = far[:, : self.split], far[:, self.split :]
        else:
            ahead, behind = self.line.run(
                lambda v, *c: grow(v, c, n, n // 2 - hop + 1, self.split), self.product, *self.came
            )
        self.came = (self.line.send(ahead, "dp", pairs[0]), self.line.send(behind, "dp", pairs[1]))

    def wait(self, hop):
        self.came = self.line.passed(*self.came)

    def total(self):
        return self.line.run(lambda v, *c: grow(v, c, self.n, 0, self.split), self.product, *self.came)


CORE = [(i, i ^ 1) for i in range(4)]
PAIR = [(i, i ^ 2) for i in range(4)]


class GroupGather:
    def __init__(self, line, own):
        self.line, self.own = line, own
        self.pair = line.send(own, "fsdp", PAIR)
        self.core = line.send(own, "fsdp", CORE)

    def relay(self):
        self.pair, self.core = self.line.passed(self.pair, self.core)
        self.diagonal = self.line.send(self.pair, "fsdp", CORE)

    def blocks(self):
        return [self.own, self.pair, self.core, self.line.passed(self.diagonal)]


class GroupReduce:
    def __init__(self, line, blocks):
        self.line, self.blocks = line, blocks
        self.far = line.send(blocks[3], "fsdp", CORE)
        self.near = line.send(blocks[2], "fsdp", CORE)

    def relay(self):
        far, self.near = self.line.passed(self.far, self.near)
        self.sent = self.line.send(self.line.run(plus, self.blocks[1], far), "fsdp", PAIR)

    def terms(self):
        return self.blocks[0], self.near, self.line.passed(self.sent)


def dot(a, b):
    return jnp.dot(a, b, preferred_element_type=WIDE)


def dot_rows(a, b):
    return lax.dot_general(a, b, (((1,), (1,)), ((), ())), preferred_element_type=WIDE)


def dot_firsts(a, b):
    return lax.dot_general(a, b, (((0,), (0,)), ((), ())), preferred_element_type=WIDE)


def by_rows(rows, width):
    return pl.BlockSpec((rows, width), lambda i: (i, 0))


def whole(value):
    zeros = (0,) * value.ndim
    return pl.BlockSpec(value.shape, lambda i: zeros, pipeline_mode=pl.Buffered(1))


def shaped(shape, kind):
    return jax.ShapeDtypeStruct(shape, kind)


def times_chunks(value, chunks):
    total, at = None, 0
    for chunk in chunks:
        size = chunk.shape[0]
        term = dot(value[:, at : at + size], chunk[...])
        total = term if total is None else total + term
        at += size
    return total


def into_chunks(out_ref, values, chunk_sets):
    at = 0
    for row in zip(*chunk_sets):
        size = row[0].shape[0]
        total = None
        for value, chunk in zip(values, row):
            term = dot_rows(value, chunk[...])
            total = term if total is None else total + term
        out_ref[:, at : at + size] = total.astype(out_ref.dtype)
        at += size


def pieces_of(panel, split):
    if len(panel) == 1:
        chunk = panel[0]
        return [chunk.at[:, :split]], [chunk.at[:, split:]]
    near, far = panel[:-2], panel[-2:]
    left = [chunk.at[:, :split] for chunk in near]
    right = [chunk.at[:, split:] for chunk in near]
    at = (len(near) + 1) // 2
    return left[:at] + [far[0]] + left[at:], right[:at] + [far[1]] + right[at:]


def turn(values, first_half):
    width = values.shape[-1]
    left = pltpu.roll(values, width - HEAD_DIM // 2, 1)
    right = pltpu.roll(values, HEAD_DIM // 2, 1)
    return jnp.where(first_half, -left, right)


def lane_ids(rows, width):
    return lax.broadcasted_iota(jnp.int32, (rows, width), 1)


def allowed_pairs(column, row):
    rows = column.shape[0]
    later = lax.broadcasted_iota(jnp.int32, (rows, rows), 0)
    earlier = lax.broadcasted_iota(jnp.int32, (rows, rows), 1)
    return (column == row) & (later >= earlier)


def normalize(hidden, gain):
    inverse = lax.rsqrt(jnp.mean(hidden * hidden, axis=-1, keepdims=True) + EPSILON)
    return (hidden * inverse * gain).astype(LOW)


def attention_forward(count, *refs):
    x_ref, gain_ref, cos_ref, sin_ref, col_ref, row_ref = refs[:6]
    turned_ref, q_ref, kv_ref, o_ref, lse_ref = refs[6 + count : 11 + count]
    branch_refs, qkv_ref = refs[11 + count : 15 + count], refs[15 + count]
    q_chunks, o_chunks = pieces_of(refs[6 : 6 + count], qkv_ref.shape[1])
    depth = gain_ref.shape[1]
    rows, width = q_ref.shape
    pairs = width // LANES
    normed = normalize(x_ref[:, :depth].astype(WIDE), gain_ref[...])
    turned_ref[...] = normed.T
    qkv_ref[...] = times_chunks(normed, q_chunks)
    cosine, sine = cos_ref[...], sin_ref[...]
    lanes = lane_ids(rows, LANES)
    even = lanes < HEAD_DIM
    first = (lanes % HEAD_DIM) < HEAD_DIM // 2
    keyval = qkv_ref[:, width:]
    keyval_rot = keyval * cosine + turn(keyval, first) * sine
    keyval = jnp.where(even, keyval_rot, keyval)
    kv_ref[...] = keyval.astype(LOW)
    other = pltpu.roll(keyval, HEAD_DIM, 1)
    keys = jnp.where(even, keyval, other).astype(LOW)
    vals = jnp.where(even, other, keyval).astype(LOW)
    allowed = allowed_pairs(col_ref[...], row_ref[0])
    log_sums = jnp.zeros((rows, LANES), WIDE)
    for pair in range(pairs):
        piece = qkv_ref[:, pair * LANES : (pair + 1) * LANES]
        piece = (piece * cosine + turn(piece, first) * sine).astype(LOW)
        q_ref[:, pair * LANES : (pair + 1) * LANES] = piece
        mixed = []
        for side in range(2):
            chosen = jnp.where(even if side == 0 else ~even, piece, jnp.zeros_like(piece))
            scores = dot_rows(chosen, keys) * (HEAD_DIM ** -0.5)
            scores = jnp.where(allowed, scores, -1e30)
            peak = jnp.max(scores, axis=1, keepdims=True)
            powers = jnp.exp(scores - peak)
            total = jnp.sum(powers, axis=1, keepdims=True)
            soft = (powers / total).astype(LOW)
            mixed.append(dot(soft, vals))
            log_sums = jnp.where(lanes == 2 * pair + side, peak + jnp.log(total), log_sums)
        o_ref[:, pair * LANES : (pair + 1) * LANES] = jnp.where(even, mixed[0], mixed[1]).astype(LOW)
    lse_ref[...] = log_sums
    for block, branch_ref in enumerate(branch_refs):

        @pl.when(pl.program_id(0) == block)
        def _(branch_ref=branch_ref):
            into_chunks(branch_ref, [o_ref[...]], [o_chunks])


def fixed(rows, width):
    return pl.BlockSpec((rows, width), lambda i: (0, 0))


def attend(x, gain, cosine, sine, column, row, panel, width, rows):
    total, depth = x.shape[0], gain.shape[1]
    return pl.pallas_call(
        functools.partial(attention_forward, len(panel)),
        grid=(total // rows,),
        in_specs=[
            by_rows(rows, x.shape[1]),
            whole(gain),
            by_rows(rows, LANES),
            by_rows(rows, LANES),
            by_rows(rows, 1),
            pl.BlockSpec((1, 1, rows), lambda i: (i, 0, 0)),
        ]
        + [whole(v) for v in panel],
        out_specs=[
            pl.BlockSpec((depth, rows), lambda i: (0, i)),
            by_rows(rows, width),
            by_rows(rows, LANES),
            by_rows(rows, width),
            by_rows(rows, LANES),
        ]
        + [fixed(rows, depth)] * 4,
        out_shape=[
            shaped((depth, total), LOW),
            shaped((total, width), LOW),
            shaped((total, LANES), LOW),
            shaped((total, width), LOW),
            shaped((total, LANES), WIDE),
        ]
        + [shaped((rows, depth), LOW)] * 4,
        scratch_shapes=[pltpu.VMEM((rows, width + LANES), WIDE)],
        name="attend",
    )(x, gain, cosine, sine, column, row, *panel)


def attention_backward(count, *refs):
    dh_ref, q_ref, kv_ref, lse_ref, cos_ref, sin_ref, col_ref, row_ref = refs[:8]
    grad_ref, part_refs, do_ref = refs[8 + count], refs[9 + count : 13 + count], refs[13 + count]
    q_chunks, o_chunks = pieces_of(refs[8 : 8 + count], grad_ref.shape[1])
    rows, width = q_ref.shape
    pairs = width // LANES
    scale = HEAD_DIM ** -0.5
    do_ref[...] = times_chunks(dh_ref, o_chunks).astype(LOW)
    cosine, sine = cos_ref[...], sin_ref[...]
    lanes = lane_ids(rows, LANES)
    even = lanes < HEAD_DIM
    first = (lanes % HEAD_DIM) < HEAD_DIM // 2
    keyval = kv_ref[...].astype(WIDE)
    other = pltpu.roll(keyval, HEAD_DIM, 1)
    keys = jnp.where(even, keyval, other).astype(LOW)
    vals = jnp.where(even, other, keyval).astype(LOW)
    allowed = allowed_pairs(col_ref[...], row_ref[0])
    log_sums = lse_ref[...]
    grad_keys = jnp.zeros((rows, LANES), WIDE)
    grad_vals = jnp.zeros((rows, LANES), WIDE)
    for pair in range(pairs):
        piece = q_ref[:, pair * LANES : (pair + 1) * LANES]
        grads = do_ref[:, pair * LANES : (pair + 1) * LANES]
        turned = []
        for side in range(2):
            mine = even if side == 0 else ~even
            chosen = jnp.where(mine, piece, jnp.zeros_like(piece))
            chosen_grad = jnp.where(mine, grads, jnp.zeros_like(grads))
            head = 2 * pair + side
            log_sum = log_sums[:, head : head + 1]
            scores = jnp.where(allowed, dot_rows(chosen, keys) * scale, -1e30)
            soft = jnp.exp(scores - log_sum)
            grad_soft = dot_rows(chosen_grad, vals)
            delta = jnp.sum(soft * grad_soft, axis=1, keepdims=True)
            grad_scores = (soft * (grad_soft - delta)).astype(LOW)
            grad_vals = grad_vals + dot_firsts(soft.astype(LOW), chosen_grad)
            grad_keys = grad_keys + dot_firsts(grad_scores, chosen)
            turned.append(dot(grad_scores, keys))
        grad_q = jnp.where(even, turned[0], turned[1]) * scale
        grad_q = grad_q * cosine - turn(grad_q, first) * sine
        grad_ref[:, pair * LANES : (pair + 1) * LANES] = grad_q.astype(LOW)
    grad_keys = (grad_keys + pltpu.roll(grad_keys, HEAD_DIM, 1)) * scale
    grad_keys = grad_keys * cosine - turn(grad_keys, first) * sine
    grad_vals = grad_vals + pltpu.roll(grad_vals, HEAD_DIM, 1)
    grad_ref[:, width:] = jnp.where(even, grad_keys, grad_vals).astype(LOW)
    for block, part_ref in enumerate(part_refs):

        @pl.when(pl.program_id(0) == block)
        def _(part_ref=part_ref):
            into_chunks(part_ref, [grad_ref[...]], [q_chunks])


def attend_back(grads, query, keyval, log_sums, cosine, sine, column, row, panel, rows):
    total, depth = grads.shape
    width = query.shape[1]
    return pl.pallas_call(
        functools.partial(attention_backward, len(panel)),
        grid=(total // rows,),
        in_specs=[
            by_rows(rows, depth),
            by_rows(rows, width),
            by_rows(rows, LANES),
            by_rows(rows, LANES),
            by_rows(rows, LANES),
            by_rows(rows, LANES),
            by_rows(rows, 1),
            pl.BlockSpec((1, 1, rows), lambda i: (i, 0, 0)),
        ]
        + [whole(v) for v in panel],
        out_specs=[by_rows(rows, width + LANES)] + [fixed(rows, depth)] * 4,
        out_shape=[shaped((total, width + LANES), LOW)] + [shaped((rows, depth), LOW)] * 4,
        scratch_shapes=[pltpu.VMEM((rows, width), LOW)],
        name="attend_back",
    )(grads, query, keyval, log_sums, cosine, sine, column, row, *panel)


def plus_kernel(a_ref, b_ref, out_ref):
    out_ref[...] = a_ref[...] + b_ref[...]


def plus(a, b):
    rows, depth = a.shape
    step = rows // 2
    return pl.pallas_call(
        plus_kernel,
        grid=(2,),
        in_specs=[by_rows(step, depth)] * 2,
        out_specs=by_rows(step, depth),
        out_shape=shaped(a.shape, a.dtype),
        name="plus",
    )(a, b)


def gathered_kernel(own_ref, pair_ref, core_ref, diagonal_ref, all_ref, turned_ref=None):
    for block, ref in enumerate((own_ref, pair_ref, core_ref, diagonal_ref)):

        @pl.when(pl.program_id(0) == block)
        def _(ref=ref):
            value = ref[...]
            all_ref[...] = value
            if turned_ref is not None:
                turned_ref[...] = value.T


def gathered(blocks, with_turned):
    rows, depth = blocks[0].shape
    out_specs, out_shape = [by_rows(rows, depth)], [shaped((4 * rows, depth), LOW)]
    if with_turned:
        out_specs.append(pl.BlockSpec((depth, rows), lambda i: (0, i)))
        out_shape.append(shaped((depth, 4 * rows), LOW))
    out = pl.pallas_call(
        gathered_kernel,
        grid=(4,),
        in_specs=[whole(v) for v in blocks],
        out_specs=out_specs,
        out_shape=out_shape,
        name="gathered",
    )(*blocks)
    return tuple(out) if with_turned else out[0]


def added(refs):
    total = refs[0][...].astype(WIDE)
    for ref in refs[1:]:
        total = total + ref[...].astype(WIDE)
    return total


def join_kernel(x_ref, own_ref, near_ref, sent_ref, gain_ref, hidden_ref, normed_ref):
    hidden = added((x_ref, own_ref, near_ref, sent_ref))
    hidden_ref[...] = hidden
    normed_ref[...] = normalize(hidden, gain_ref[...])


def join(x, gain, *parts):
    rows, depth = x.shape
    step = rows // 2
    return pl.pallas_call(
        join_kernel,
        grid=(2,),
        in_specs=[by_rows(step, depth)] * 4 + [whole(gain)],
        out_specs=[by_rows(step, depth)] * 2,
        out_shape=[shaped((rows, depth), WIDE), shaped((rows, depth), LOW)],
        name="join",
    )(x, *parts, gain)


def feed_kernel(count, *refs):
    x_ref = refs[0]
    act_ref, slope_ref, silu_ref = refs[1 + count :]
    g_chunks, u_chunks = pieces_of(refs[1 : 1 + count], act_ref.shape[1])
    gate = times_chunks(x_ref, g_chunks)
    up = times_chunks(x_ref, u_chunks)
    sigmoid = 1.0 / (1.0 + jnp.exp(-gate))
    silu = gate * sigmoid
    act_ref[...] = (silu * up).astype(LOW)
    silu_ref[...] = silu.astype(LOW)
    slope_ref[...] = (up * sigmoid * (1.0 + gate * (1.0 - sigmoid))).astype(LOW)


def feed(x, panel, wide):
    total, depth = x.shape
    step = total // 4
    return pl.pallas_call(
        functools.partial(feed_kernel, len(panel)),
        grid=(4,),
        in_specs=[by_rows(step, depth)] + [whole(v) for v in panel],
        out_specs=[by_rows(step, wide)] * 3,
        out_shape=[shaped((total, wide), LOW)] * 3,
        name="feed",
    )(x, *panel)


def feed_back_kernel(count, split, *refs):
    dy_ref, slope_ref, silu_ref = refs[:3]
    (out_ref,) = refs[3 + count :]
    wide = slope_ref.shape[1]
    at = 0
    for chunks in pieces_of(refs[3 : 3 + count], split):
        end = at + chunks[0].shape[1]
        grads = times_chunks(dy_ref, chunks)
        out_ref[:, at:end] = (grads * slope_ref[:, at:end].astype(WIDE)).astype(LOW)
        out_ref[:, wide + at : wide + end] = (grads * silu_ref[:, at:end].astype(WIDE)).astype(LOW)
        at = end


def feed_back(grads, slope, silu, panel, split):
    total, depth = grads.shape
    wide = slope.shape[1]
    step = total // 4
    return pl.pallas_call(
        functools.partial(feed_back_kernel, len(panel), split),
        grid=(4,),
        in_specs=[by_rows(step, depth), by_rows(step, wide), by_rows(step, wide)]
        + [whole(v) for v in panel],
        out_specs=by_rows(step, 2 * wide),
        out_shape=shaped((total, 2 * wide), LOW),
        name="feed_back",
    )(grads, slope, silu, *panel)


def spread_kernel(count, split, *refs):
    value, out_refs = refs[0], refs[1 + count :]
    left, right = pieces_of(refs[1 : 1 + count], split)
    rows = out_refs[0].shape[0]
    each = value.shape[0] // rows
    for block, out_ref in enumerate(out_refs):
        inside = block % each

        @pl.when(pl.program_id(0) == block // each)
        def _(out_ref=out_ref, at=inside * rows):
            pieces = [value[at : at + rows, :split], value[at : at + rows, split:]]
            into_chunks(out_ref, pieces, [left, right])


def spread(value, panel, split, rows):
    total, wide = value.shape
    n = len(panel)
    depth = panel[0].shape[0] * max(1, n - 1)
    return pl.pallas_call(
        functools.partial(spread_kernel, n, split),
        grid=(4,),
        in_specs=[by_rows(total // 4, wide)] + [whole(c) for c in panel],
        out_specs=[fixed(rows, depth)] * 4,
        out_shape=[shaped((rows, depth), LOW)] * 4,
        name="spread",
    )(value, *panel)


def product_kernel(count, *refs):
    out_ref = refs[-1]
    at = 0
    for left, right in zip(refs[:count], refs[count : 2 * count]):
        end = at + right.shape[1]
        out_ref[:, at:end] = dot(left[...], right[...]).astype(LOW)
        at = end


def product(lefts, rights):
    depth, total = lefts[0].shape
    wide = sum(v.shape[1] for v in rights)
    step = depth // 8
    return pl.pallas_call(
        functools.partial(product_kernel, len(lefts)),
        grid=(8,),
        in_specs=[by_rows(step, total) for _ in lefts] + [whole(v) for v in rights],
        out_specs=by_rows(step, wide),
        out_shape=shaped((depth, wide), LOW),
        name="product",
    )(*lefts, *rights)


def grow_kernel(split, narrow, *refs):
    ahead_term, behind_term, ahead, behind, ahead_out, behind_out = refs
    if narrow:
        ahead_out[:, :split] = ahead_term[:, :split] + ahead[...]
        ahead_out[:, split:] = ahead_term[:, split:]
        behind_out[:, :split] = behind_term[:, :split]
        behind_out[:, split:] = behind_term[:, split:] + behind[...]
    else:
        ahead_out[...] = ahead_term[...] + ahead[...]
        behind_out[...] = behind_term[...] + behind[...]


def last_kernel(term, ahead, behind, out):
    out[...] = term[...].astype(WIDE) + ahead[...].astype(WIDE) + behind[...].astype(WIDE)


def grow(product, came, n, away, split):
    part, wide = product.shape[0] // n, product.shape[1]
    narrow = away == n // 2 - 1
    step = part // 2
    sizes = [v.shape[1] for v in came]
    came_specs = [by_rows(step, size) for size in sizes]

    def rows_at(offset):
        return pl.BlockSpec((step, wide), lambda i: (2 * offset + i, 0))

    if away == 0:
        return pl.pallas_call(
            last_kernel,
            grid=(2,),
            in_specs=[rows_at(0)] + came_specs,
            out_specs=by_rows(step, wide),
            out_shape=shaped((part, wide), WIDE),
            name="last",
        )(product, *came)
    return tuple(
        pl.pallas_call(
            functools.partial(grow_kernel, split, narrow),
            grid=(2,),
            in_specs=[rows_at(away), rows_at(n - away)] + came_specs,
            out_specs=[by_rows(step, wide)] * 2,
            out_shape=[shaped((part, wide), LOW)] * 2,
            name="grow",
        )(product, product, *came)
    )


def norm_back_kernel(hidden_ref, gain_ref, rest_ref, own_ref, near_ref, sent_ref, grads_ref, low_ref, terms_ref):
    hidden = hidden_ref[...].astype(WIDE)
    grad_normed = added((own_ref, near_ref, sent_ref))
    inverse = lax.rsqrt(jnp.mean(hidden * hidden, axis=-1, keepdims=True) + EPSILON)
    unit = hidden * inverse
    scaled = grad_normed * gain_ref[...]
    grads = rest_ref[...].astype(WIDE) + inverse * (
        scaled - unit * jnp.mean(scaled * unit, axis=-1, keepdims=True)
    )
    grads_ref[...] = grads
    low_ref[...] = grads.astype(LOW)

    @pl.when(pl.program_id(0) == 0)
    def _():
        terms_ref[...] = jnp.zeros_like(terms_ref)

    terms_ref[...] += jnp.sum(grad_normed * unit, axis=0, keepdims=True)


def norm_back(hidden, gain, rest, *parts):
    rows, depth = hidden.shape
    step = rows // 2
    return pl.pallas_call(
        norm_back_kernel,
        grid=(2,),
        in_specs=[by_rows(step, depth), whole(gain)] + [by_rows(step, depth)] * 4,
        out_specs=[by_rows(step, depth), by_rows(step, depth), pl.BlockSpec((1, depth), lambda i: (0, 0))],
        out_shape=[shaped((rows, depth), WIDE), shaped((rows, depth), LOW), shaped((1, depth), WIDE)],
        name="norm_back",
    )(hidden, gain, rest, *parts)


def shuffle_kernel(n, order_ref, *refs):
    out_ref = refs[-1]
    part = out_ref.shape[1] // n
    for s in range(n):
        at = pl.multiple_of(order_ref[s] * part, part)
        if len(refs) == 2:
            piece = refs[0][:, pl.ds(at, part)]
        else:
            piece = refs[0][:, pl.ds(at, part)]
            for ref in refs[1:-1]:
                piece = piece + ref[:, pl.ds(at, part)].astype(WIDE)
        out_ref[:, s * part : (s + 1) * part] = piece.astype(out_ref.dtype)


def shuffle(order, n, *values):
    rows, depth = values[0].shape
    part = depth // n
    if part % LANES:
        total = values[0]
        for v in values[1:]:
            total = total + v.astype(WIDE)
        pieces = [lax.dynamic_slice(total, (0, order[s] * part), (rows, part)) for s in range(n)]
        return jnp.concatenate(pieces, axis=1).astype(LOW)
    step = rows // 2
    return pl.pallas_call(
        functools.partial(shuffle_kernel, n),
        grid_spec=pltpu.PrefetchScalarGridSpec(
            num_scalar_prefetch=1,
            grid=(2,),
            in_specs=[pl.BlockSpec((step, depth), lambda i, order: (i, 0))] * len(values),
            out_specs=pl.BlockSpec((step, depth), lambda i, order: (i, 0)),
        ),
        out_shape=shaped((rows, depth), LOW),
        name="shuffle",
    )(order, *values)


def tables(segment_block):
    rows = segment_block.shape[0]
    places = jnp.arange(rows, dtype=jnp.int32)
    same = segment_block[:, None] == segment_block[None, :]
    first_index = jnp.min(jnp.where(same, places[None, :], rows), axis=1)
    offsets = (places - first_index).astype(WIDE)
    half = HEAD_DIM // 2
    frequencies = jnp.exp(jnp.arange(half, dtype=WIDE) * (-2.0 * math.log(ROPE_BASE) / HEAD_DIM))
    angles = offsets[:, None] * frequencies[None, :]
    cosine, sine = jnp.cos(angles), jnp.sin(angles)
    return jnp.concatenate([cosine] * 4, axis=1), jnp.concatenate([sine] * 4, axis=1)


def on_device(
    tokens, segments, gain_attn, w_query, w_key, w_value, w_out, gain_mlp, w_gate, w_up, w_down, cotangent
):
    n = lax.axis_size("dp")
    rows, depth = tokens.shape
    part = depth // n
    hops = n // 2
    me = lax.axis_index("dp")
    sources, offsets = [lax.dynamic_index_in_dim(jnp.asarray(t), me, keepdims=False) for t in ring_tables(n)]
    line = Line(jnp.zeros((8, LANES), WIDE))

    heads_wide, hidden_wide = w_query.shape[1], w_gate.shape[1]
    qkv_wide = heads_wide + w_key.shape[1] + w_value.shape[1]
    split = -(-hidden_wide // (2 * LANES)) * LANES
    attn = RingGather(line, jnp.concatenate([w_query, w_key, w_value, w_out.T], axis=1).astype(LOW), n, qkv_wide)
    feedw = RingGather(line, jnp.concatenate([w_gate, w_up], axis=1).astype(LOW), n, hidden_wide)
    down = RingGather(line, w_down.T.astype(LOW), n, split)

    attn.start(1)
    own_tokens = shuffle(sources, n, tokens)
    marks = jnp.broadcast_to(segments.astype(LOW)[:, None], (rows, LANES))
    x = GroupGather(line, jnp.concatenate([own_tokens, marks], axis=1))
    gains = jnp.stack([gain_attn, gain_mlp]).astype(LOW)
    bits = [1 << i for i in range((n - 1).bit_length())]

    def gains_from(value, bit):
        other = lax.ppermute(value, "dp", [(i, i ^ bit) for i in range(n)])
        return jnp.concatenate([value, other], axis=1)

    gains = gains_from(gains, bits[0])
    attn.wait(1)
    attn.start(2)
    for bit in bits[1:-1]:
        gains = gains_from(line.passed(gains), bit)
    own_grads = line.run(lambda *v: shuffle(v[0], n, v[1]), sources, cotangent)
    for hop in range(2, hops - 1):
        attn.wait(hop)
        attn.start(hop + 1)
    gains = gains_from(line.passed(gains), bits[-1])
    x.relay()
    attn.wait(hops - 1)
    attn.start(hops)
    token_rows = line.run(lambda *v: gathered(v, False), *x.blocks())
    gains = jnp.take(gains.reshape(2, n, part), sources ^ me, axis=1).reshape(2, depth).astype(WIDE)
    gains = line.passed(gains)
    gain_one, gain_two = gains[0:1], gains[1:2]
    attn.wait(hops)
    feedw.start(1)
    y = GroupGather(line, own_grads)
    segment_blocks = token_rows[:, depth].astype(jnp.int32).reshape(-1, rows)
    column, row = segment_blocks.reshape(-1, 1), segment_blocks[:, None, :]
    cosine, sine = line.run(lambda v: jax.vmap(tables)(v), segment_blocks)
    cosine, sine = cosine.reshape(-1, LANES), sine.reshape(-1, LANES)

    attn_panel = attn.panel()
    normed_turned, query, keyval, mixed, log_sums, *branch = line.run(
        lambda *v: attend(*v[:6], v[6:], heads_wide, rows),
        token_rows, gain_one, cosine, sine, column, row, *attn_panel,
    )
    y.relay()
    feedw.wait(1)
    feedw.start(2)
    branch = GroupReduce(line, branch)
    grads_all, grads_turned = line.run(lambda *v: gathered(v, True), *y.blocks())
    branch.relay()
    for hop in range(2, hops - 1):
        feedw.wait(hop)
        feedw.start(hop + 1)
    hidden, normed_own = line.run(join, own_tokens, gain_two, *branch.terms())
    z = GroupGather(line, normed_own)
    feedw.wait(hops - 1)
    feedw.start(hops)
    z.relay()
    normed_mlp, mlp_turned = line.run(lambda *v: gathered(v, True), *z.blocks())

    feedw.wait(hops)
    down.start(1)
    feed_panel = feedw.panel()
    activation, slope, silu = line.run(lambda a, *v: feed(a, v, hidden_wide), normed_mlp, *feed_panel)
    for hop in range(1, hops):
        down.wait(hop)
        down.start(hop + 1)
        if hop == 1:
            down_terms = line.run(lambda a, b: product([a], [b]), grads_turned, activation)
            r_down = RingReduce(line, down_terms, n, split)
    r_down.start(1)
    down.wait(hops)
    down_panel = down.panel()

    grad_feed = line.run(
        lambda a, b, c, *v: feed_back(a, b, c, v, split), grads_all, slope, silu, *down_panel
    )
    for hop in range(1, hops - 2):
        r_down.wait(hop)
        r_down.start(hop + 1)
    grad_normed = line.run(lambda a, *v: spread(a, v, hidden_wide, rows), grad_feed, *feed_panel)
    r_down.wait(hops - 2)
    r_down.start(hops - 1)
    grad_normed = GroupReduce(line, grad_normed)
    feed_terms = line.run(lambda a, b: product([a], [b]), mlp_turned, grad_feed)
    r_down.wait(hops - 1)
    r_down.start(hops)
    grad_normed.relay()
    layer_part = line.run(lambda a, *v: spread(a, v, split, rows), activation, *down_panel)
    r_down.wait(hops)
    r_feed = RingReduce(line, feed_terms, n, hidden_wide)
    r_feed.start(1)
    grad_down = r_down.total()
    grad_hidden, grad_branch, gain_mlp_terms = line.run(
        norm_back, hidden, gain_two, own_grads, *grad_normed.terms()
    )
    b = GroupGather(line, grad_branch)
    r_feed.wait(1)
    r_feed.start(2)
    b.relay()
    branch_grads, branch_turned = line.run(lambda *v: gathered(v, True), *b.blocks())
    for hop in range(2, hops - 1):
        r_feed.wait(hop)
        r_feed.start(hop + 1)

    grad_qkv, *grad_input_part = line.run(
        lambda *v: attend_back(*v[:8], v[8:], rows),
        branch_grads, query, keyval, log_sums, cosine, sine, column, row, *attn_panel,
    )
    attn_terms = line.run(
        lambda *v: product(v[:2], v[2:]), normed_turned, branch_turned, grad_qkv, mixed
    )
    r_feed.wait(hops - 1)
    r_feed.start(hops)
    grad_input_sum = GroupReduce(line, grad_input_part)
    grad_input_sum.relay()
    r_attn = RingReduce(line, attn_terms, n, qkv_wide)
    r_feed.wait(hops)
    r_attn.start(1)
    layer_sum = GroupReduce(line, layer_part)
    grad_w_feed = r_feed.total()
    r_attn.wait(1)
    r_attn.start(2)
    _, grad_tokens, gain_attn_terms = line.run(
        norm_back, own_tokens, gain_one, grad_hidden, *grad_input_sum.terms()
    )
    layer_sum.relay()
    gain_terms = jnp.concatenate([gain_attn_terms, gain_mlp_terms], axis=0).reshape(2, n, part)
    gain_terms = jnp.take(gain_terms, offsets, axis=1).reshape(2, depth)
    gain_steps = [("fsdp", 4, 1), ("fsdp", 4, 2)] + [("dp", n, bit) for bit in bits]

    def gain_step(value, step):
        axis, size, bit = step
        other = line.passed(line.send(value, axis, [(i, i ^ bit) for i in range(size)]))
        return line.run(jnp.add, value, other)

    for step in gain_steps[:2]:
        gain_terms = gain_step(gain_terms, step)
    grad_tokens = line.run(lambda at, v: shuffle(at, n, v), offsets, grad_tokens)
    for hop in range(2, hops):
        r_attn.wait(hop)
        r_attn.start(hop + 1)
        for step in gain_steps[2 * hop - 2 : 2 * hop]:
            gain_terms = gain_step(gain_terms, step)
    for step in gain_steps[2 * hops - 2 :]:
        gain_terms = gain_step(gain_terms, step)
    layer_own = line.run(lambda at, *v: shuffle(at, n, *v), offsets, hidden, *layer_sum.terms())
    gain_own = lax.dynamic_slice(gain_terms, (0, me * part), (2, part))
    r_attn.wait(hops)
    grad_attn = r_attn.total()

    value_at = heads_wide + w_key.shape[1]
    return (
        layer_own,
        grad_tokens,
        gain_own[0],
        grad_attn[:, :heads_wide],
        grad_attn[:, heads_wide:value_at],
        grad_attn[:, value_at:qkv_wide],
        grad_attn[:, qkv_wide:].T,
        gain_own[1],
        grad_w_feed[:, :hidden_wide],
        grad_w_feed[:, hidden_wide:],
        grad_down.T,
    )


def solution(mesh):
    placed = (
        P(("dp", "fsdp"), None),
        P(("dp", "fsdp")),
        P("dp"),
        P("dp", "fsdp"),
        P("dp", "fsdp"),
        P("dp", "fsdp"),
        P("fsdp", "dp"),
        P("dp"),
        P("dp", "fsdp"),
        P("dp", "fsdp"),
        P("fsdp", "dp"),
        P(("dp", "fsdp"), None),
    )
    return jax.shard_map(
        on_device,
        mesh=mesh,
        in_specs=placed,
        out_specs=(
            P(("dp", "fsdp"), None),
            P(("dp", "fsdp"), None),
            P("dp"),
            P("dp", "fsdp"),
            P("dp", "fsdp"),
            P("dp", "fsdp"),
            P("fsdp", "dp"),
            P("dp"),
            P("dp", "fsdp"),
            P("dp", "fsdp"),
            P("fsdp", "dp"),
        ),
        check_vma=False,
    )
```

```python
import functools
import math

import jax
import jax.numpy as jnp
import numpy as np
from jax import lax
from jax.experimental import pallas as pl
from jax.experimental.pallas import tpu as pltpu
from jax.sharding import PartitionSpec as P

HEAD_DIM = 64
EPSILON = 1e-05
ROPE_BASE = 10000.0
LOW = jnp.bfloat16
WIDE = jnp.float32
LANES = 128


def ring_order(n):
    return list(range(0, n, 2)) + list(range(n - 1, 0, -2))


def ring_perms(n):
    order = ring_order(n)
    forward = [(order[i], order[(i + 1) % n]) for i in range(n)]
    return forward, [(b, a) for a, b in forward]


def ring_tables(n):
    order = ring_order(n)
    place = [order.index(j) for j in range(n)]
    sources = [[order[(place[i] + s) % n] for s in range(n)] for i in range(n)]
    offsets = [[(place[j] - place[i]) % n for j in range(n)] for i in range(n)]
    return np.array(sources, np.int32), np.array(offsets, np.int32)


class Line:
    def __init__(self, token):
        self.token = token

    def after(self, *values):
        out = lax.optimization_barrier((*values, self.token))
        return out[0] if len(values) == 1 else out[:-1]

    def passed(self, *values):
        out = lax.optimization_barrier((*values, self.token))
        self.token = out[-1]
        return out[0] if len(values) == 1 else out[:-1]

    def run(self, work, *values):
        result = work(*lax.optimization_barrier((*values, self.token))[:-1])
        if isinstance(result, (tuple, list)):
            return self.passed(*result)
        return self.passed(result)

    def send(self, value, axis, pairs):
        return lax.ppermute(self.after(value), axis, pairs)


class RingGather:
    def __init__(self, line, own, n, split, part):
        self.line, self.n, self.split, self.part = line, n, split, part
        self.chunks = {0: own}
        self.flying = None

    def start(self, hop):
        n, pairs = self.n, ring_perms(self.n)
        ahead, behind = self.chunks[(n - hop + 1) % n], self.chunks[hop - 1]
        if hop == n // 2:
            ahead, behind = ahead[:, : self.split], behind[:, self.split :]
        self.flying = (self.line.send(ahead, "dp", pairs[0]), self.line.send(behind, "dp", pairs[1]))

    def wait(self, hop):
        ahead, behind = self.line.passed(*self.flying)
        if hop == self.n // 2:
            self.far = (ahead, behind)
        else:
            self.chunks[self.n - hop], self.chunks[hop] = ahead, behind

    def panel(self):
        n, part = self.n, self.part
        near = [self.chunks[s] for s in range(n) if s != n // 2]
        if part % LANES == 0:
            return [*near, *self.far]
        far = jnp.concatenate(self.far, axis=1)
        return [jnp.concatenate([v[:part] for v in (*near[: n // 2], far, *near[n // 2 :])], axis=0)]

    def extra(self, count):
        n, part = self.n, self.part
        chunks = [self.far[0] if s == n // 2 else self.chunks[s] for s in range(n)]
        return jnp.concatenate([c[part : part + count, :part] for c in chunks], axis=1)


class RingReduce:
    def __init__(self, line, products, n, split):
        self.line, self.products, self.n, self.split = line, products, n, split
        self.came = ()

    def grown(self, away):
        k = len(self.products)
        return self.line.run(
            lambda *v: grow(v[:k], v[k:], self.n, away, self.split), *self.products, *self.came
        )

    def start(self, hop):
        n, pairs = self.n, ring_perms(self.n)
        if hop == 1:
            part = self.products[0].shape[0] // n
            far = [v[n // 2 * part : (n // 2 + 1) * part] for v in self.products]
            if len(far) == 1:
                far = [far[0][:, : self.split], far[0][:, self.split :]]
            ahead, behind = far
        else:
            ahead, behind = self.grown(n // 2 - hop + 1)
        self.came = (self.line.send(ahead, "dp", pairs[0]), self.line.send(behind, "dp", pairs[1]))

    def wait(self, hop):
        self.came = self.line.passed(*self.came)

    def total(self):
        return self.grown(0)


CORE = [(i, i ^ 1) for i in range(4)]
PAIR = [(i, i ^ 2) for i in range(4)]


class GroupGather:
    def __init__(self, line, own):
        self.line, self.own = line, own
        self.pair = line.send(own, "fsdp", PAIR)

    def relay(self):
        self.pair = self.line.passed(self.pair)
        half = self.pair.shape[0] // 2
        upper = self.line.send(self.pair[:half], "fsdp", CORE)
        lower = self.line.send(self.pair[half:], "fsdp", CORE)
        return self.line.passed(upper, lower)

    def blocks(self):
        core = self.line.send(self.own, "fsdp", CORE)
        upper, lower = self.relay()
        return [self.own, self.pair, self.line.passed(core), upper, lower]


class GroupReduce:
    def __init__(self, line, blocks):
        self.line, self.blocks = line, blocks
        half = blocks[3].shape[0] // 2
        self.upper = line.send(blocks[3][:half], "fsdp", CORE)
        self.lower = line.send(blocks[3][half:], "fsdp", CORE)

    def relay(self):
        far = self.line.passed(self.upper, self.lower)
        self.sent = self.line.send(self.line.run(plus, self.blocks[1], *far), "fsdp", PAIR)
        self.near = self.line.send(self.blocks[2], "fsdp", CORE)

    def terms(self):
        self.near, self.sent = self.line.passed(self.near, self.sent)
        return self.blocks[0], self.near, self.sent


def dot(a, b):
    return jnp.dot(a, b, preferred_element_type=WIDE)


def dot_rows(a, b):
    return lax.dot_general(a, b, (((1,), (1,)), ((), ())), preferred_element_type=WIDE)


def dot_firsts(a, b):
    return lax.dot_general(a, b, (((0,), (0,)), ((), ())), preferred_element_type=WIDE)


def by_rows(rows, width):
    return pl.BlockSpec((rows, width), lambda i: (i, 0))


def whole(value):
    zeros = (0,) * value.ndim
    return pl.BlockSpec(value.shape, lambda i: zeros, pipeline_mode=pl.Buffered(1))


def shaped(shape, kind):
    return jax.ShapeDtypeStruct(shape, kind)


def times_chunks(value, chunks):
    total, at = None, 0
    for chunk in chunks:
        size = chunk.shape[0]
        term = dot(value[:, at : at + size], chunk[...])
        total = term if total is None else total + term
        at += size
    return total


def into_chunks(out_ref, values, chunk_sets):
    at = 0
    for row in zip(*chunk_sets):
        size = row[0].shape[0]
        total = None
        for value, chunk in zip(values, row):
            term = dot_rows(value, chunk[...])
            total = term if total is None else total + term
        out_ref[:, at : at + size] = total.astype(out_ref.dtype)
        at += size


def pieces_of(panel, split, depth):
    if len(panel) == 1:
        chunk = panel[0]
        return [chunk.at[:, :split]], [chunk.at[:, split:]]
    part = depth // (len(panel) - 1)
    near, far = panel[:-2], [chunk.at[:part, :] for chunk in panel[-2:]]
    left = [chunk.at[:part, :split] for chunk in near]
    right = [chunk.at[:part, split:] for chunk in near]
    at = (len(near) + 1) // 2
    return left[:at] + [far[0]] + left[at:], right[:at] + [far[1]] + right[at:]


def turn(values, first_half):
    width = values.shape[-1]
    left = pltpu.roll(values, width - HEAD_DIM // 2, 1)
    right = pltpu.roll(values, HEAD_DIM // 2, 1)
    return jnp.where(first_half, -left, right)


def lane_ids(rows, width):
    return lax.broadcasted_iota(jnp.int32, (rows, width), 1)


def allowed_pairs(column, row):
    rows = column.shape[0]
    later = lax.broadcasted_iota(jnp.int32, (rows, rows), 0)
    earlier = lax.broadcasted_iota(jnp.int32, (rows, rows), 1)
    return (column == row) & (later >= earlier)


def normalize(hidden, gain):
    inverse = lax.rsqrt(jnp.mean(hidden * hidden, axis=-1, keepdims=True) + EPSILON)
    return (hidden * inverse * gain).astype(LOW)


def attention_forward(count, *refs):
    x_ref, gain_ref, cos_ref, sin_ref, col_ref, row_ref = refs[:6]
    turned_ref, q_ref, kv_ref, o_ref, lse_ref = refs[6 + count : 11 + count]
    branch_refs, qkv_ref = refs[11 + count : 15 + count], refs[15 + count]
    q_chunks, o_chunks = pieces_of(refs[6 : 6 + count], qkv_ref.shape[1], gain_ref.shape[1])
    depth = gain_ref.shape[1]
    rows, width = q_ref.shape
    pairs = width // LANES
    normed = normalize(x_ref[:, :depth].astype(WIDE), gain_ref[...])
    turned_ref[...] = normed.T
    qkv_ref[...] = times_chunks(normed, q_chunks)
    cosine, sine = cos_ref[...], sin_ref[...]
    lanes = lane_ids(rows, LANES)
    even = lanes < HEAD_DIM
    first = (lanes % HEAD_DIM) < HEAD_DIM // 2
    keyval = qkv_ref[:, width:]
    keyval_rot = keyval * cosine + turn(keyval, first) * sine
    keyval = jnp.where(even, keyval_rot, keyval)
    kv_ref[...] = keyval.astype(LOW)
    other = pltpu.roll(keyval, HEAD_DIM, 1)
    keys = jnp.where(even, keyval, other).astype(LOW)
    vals = jnp.where(even, other, keyval).astype(LOW)
    allowed = allowed_pairs(col_ref[...], row_ref[0])
    log_sums = jnp.zeros((rows, LANES), WIDE)
    for pair in range(pairs):
        piece = qkv_ref[:, pair * LANES : (pair + 1) * LANES]
        piece = (piece * cosine + turn(piece, first) * sine).astype(LOW)
        q_ref[:, pair * LANES : (pair + 1) * LANES] = piece
        mixed = []
        for side in range(2):
            chosen = jnp.where(even if side == 0 else ~even, piece, jnp.zeros_like(piece))
            scores = dot_rows(chosen, keys) * (HEAD_DIM ** -0.5)
            scores = jnp.where(allowed, scores, -1e30)
            peak = jnp.max(scores, axis=1, keepdims=True)
            powers = jnp.exp(scores - peak)
            total = jnp.sum(powers, axis=1, keepdims=True)
            soft = (powers / total).astype(LOW)
            mixed.append(dot(soft, vals))
            log_sums = jnp.where(lanes == 2 * pair + side, peak + jnp.log(total), log_sums)
        o_ref[:, pair * LANES : (pair + 1) * LANES] = jnp.where(even, mixed[0], mixed[1]).astype(LOW)
    lse_ref[...] = log_sums
    for block, branch_ref in enumerate(branch_refs):

        @pl.when(pl.program_id(0) == block)
        def _(branch_ref=branch_ref):
            into_chunks(branch_ref, [o_ref[...]], [o_chunks])


def fixed(rows, width):
    return pl.BlockSpec((rows, width), lambda i: (0, 0))


def attend(x, gain, cosine, sine, column, row, panel, width, rows):
    total, depth = x.shape[0], gain.shape[1]
    return pl.pallas_call(
        functools.partial(attention_forward, len(panel)),
        grid=(total // rows,),
        in_specs=[
            by_rows(rows, x.shape[1]),
            whole(gain),
            by_rows(rows, LANES),
            by_rows(rows, LANES),
            by_rows(rows, 1),
            pl.BlockSpec((1, 1, rows), lambda i: (i, 0, 0)),
        ]
        + [whole(v) for v in panel],
        out_specs=[
            pl.BlockSpec((depth, rows), lambda i: (0, i)),
            by_rows(rows, width),
            by_rows(rows, LANES),
            by_rows(rows, width),
            by_rows(rows, LANES),
        ]
        + [fixed(rows, depth)] * 4,
        out_shape=[
            shaped((depth, total), LOW),
            shaped((total, width), LOW),
            shaped((total, LANES), LOW),
            shaped((total, width), LOW),
            shaped((total, LANES), WIDE),
        ]
        + [shaped((rows, depth), LOW)] * 4,
        scratch_shapes=[pltpu.VMEM((rows, width + LANES), WIDE)],
        name="attend",
    )(x, gain, cosine, sine, column, row, *panel)


def attention_backward(sizes, count, *refs):
    dh_refs, refs = refs[: sum(sizes)], refs[sum(sizes) :]
    q_ref, kv_ref, lse_ref, cos_ref, sin_ref, col_ref, row_ref = refs[:7]
    panel, refs = refs[7 : 7 + count], refs[-len(sizes) - 2 :]
    grad_ref, part_refs, do_ref = refs[0], refs[1:-1], refs[-1]
    q_chunks, o_chunks = pieces_of(panel, grad_ref.shape[1], dh_refs[0].shape[1])
    rows, width = q_ref.shape
    pairs = width // LANES
    scale = HEAD_DIM ** -0.5
    for block, size in enumerate(sizes):

        @pl.when(pl.program_id(0) == block)
        def _(mine=dh_refs[sum(sizes[:block]) : sum(sizes[: block + 1])]):
            at = 0
            for ref in mine:
                end = at + ref.shape[0]
                do_ref[at:end, :] = times_chunks(ref, o_chunks).astype(LOW)
                at = end

    cosine, sine = cos_ref[...], sin_ref[...]
    lanes = lane_ids(rows, LANES)
    even = lanes < HEAD_DIM
    first = (lanes % HEAD_DIM) < HEAD_DIM // 2
    keyval = kv_ref[...].astype(WIDE)
    other = pltpu.roll(keyval, HEAD_DIM, 1)
    keys = jnp.where(even, keyval, other).astype(LOW)
    vals = jnp.where(even, other, keyval).astype(LOW)
    allowed = allowed_pairs(col_ref[...], row_ref[0])
    log_sums = lse_ref[...]
    grad_keys = jnp.zeros((rows, LANES), WIDE)
    grad_vals = jnp.zeros((rows, LANES), WIDE)
    for pair in range(pairs):
        piece = q_ref[:, pair * LANES : (pair + 1) * LANES]
        grads = do_ref[:, pair * LANES : (pair + 1) * LANES]
        turned = []
        for side in range(2):
            mine = even if side == 0 else ~even
            chosen = jnp.where(mine, piece, jnp.zeros_like(piece))
            chosen_grad = jnp.where(mine, grads, jnp.zeros_like(grads))
            head = 2 * pair + side
            log_sum = log_sums[:, head : head + 1]
            scores = jnp.where(allowed, dot_rows(chosen, keys) * scale, -1e30)
            soft = jnp.exp(scores - log_sum)
            grad_soft = dot_rows(chosen_grad, vals)
            delta = jnp.sum(soft * grad_soft, axis=1, keepdims=True)
            grad_scores = (soft * (grad_soft - delta)).astype(LOW)
            grad_vals = grad_vals + dot_firsts(soft.astype(LOW), chosen_grad)
            grad_keys = grad_keys + dot_firsts(grad_scores, chosen)
            turned.append(dot(grad_scores, keys))
        grad_q = jnp.where(even, turned[0], turned[1]) * scale
        grad_q = grad_q * cosine - turn(grad_q, first) * sine
        grad_ref[:, pair * LANES : (pair + 1) * LANES] = grad_q.astype(LOW)
    grad_keys = (grad_keys + pltpu.roll(grad_keys, HEAD_DIM, 1)) * scale
    grad_keys = grad_keys * cosine - turn(grad_keys, first) * sine
    grad_vals = grad_vals + pltpu.roll(grad_vals, HEAD_DIM, 1)
    grad_ref[:, width:] = jnp.where(even, grad_keys, grad_vals).astype(LOW)
    for block, part_ref in enumerate(part_refs):

        @pl.when(pl.program_id(0) == block)
        def _(part_ref=part_ref):
            into_chunks(part_ref, [grad_ref[...]], [q_chunks])


def attend_back(blocks, groups, query, keyval, log_sums, cosine, sine, column, row, panel, rows, before=None):
    total, width = query.shape
    depth = groups[0][0].shape[1]
    first, step = blocks[0], blocks[1] - blocks[0]
    flat = [v for group in groups for v in group]

    def chosen(wide):
        return pl.BlockSpec((rows, wide), lambda i: (first + step * i, 0))

    operands = [*flat, query, keyval, log_sums, cosine, sine, column, row, *panel]
    in_specs = [whole(v) for v in flat]
    in_specs += [chosen(width), chosen(LANES), chosen(LANES), chosen(LANES), chosen(LANES), chosen(1)]
    in_specs += [pl.BlockSpec((1, 1, rows), lambda i: (first + step * i, 0, 0))]
    in_specs += [whole(v) for v in panel]
    aliases = {}
    if before is not None:
        aliases = {len(operands): 0}
        operands.append(before)
        in_specs.append(pl.BlockSpec(memory_space=pl.ANY))
    return pl.pallas_call(
        functools.partial(attention_backward, [len(group) for group in groups], len(panel)),
        grid=(len(groups),),
        in_specs=in_specs,
        out_specs=[chosen(width + LANES)] + [fixed(rows, depth)] * len(groups),
        out_shape=[shaped((total, width + LANES), LOW)] + [shaped((rows, depth), LOW)] * len(groups),
        scratch_shapes=[pltpu.VMEM((rows, width), LOW)],
        input_output_aliases=aliases,
        name="attend_back",
    )(*operands)


def plus_kernel(value_ref, upper_ref, lower_ref, out_ref):
    rows = upper_ref.shape[0]
    out_ref[:rows, :] = value_ref[:rows, :] + upper_ref[...]
    out_ref[rows:, :] = value_ref[rows:, :] + lower_ref[...]


def plus(value, upper, lower):
    rows, depth = value.shape
    step = depth // 2

    def columns(size):
        return pl.BlockSpec((size, step), lambda i: (0, i))

    return pl.pallas_call(
        plus_kernel,
        grid=(2,),
        in_specs=[columns(rows), columns(rows // 2), columns(rows // 2)],
        out_specs=columns(rows),
        out_shape=shaped(value.shape, value.dtype),
        name="plus",
    )(value, upper, lower)


def gathered_kernel(with_all, own, pair, core, upper, lower, *outs):
    all_ref = outs[0] if with_all else None
    turned_ref = outs[-1] if len(outs) == 2 or not with_all else None
    for block, refs in enumerate(((own,), (pair,), (core,), (upper, lower))):

        @pl.when(pl.program_id(0) == block)
        def _(refs=refs):
            at = 0
            for ref in refs:
                value = ref[...]
                end = at + value.shape[0]
                if all_ref is not None:
                    all_ref[at:end, :] = value
                if turned_ref is not None:
                    turned_ref[:, at:end] = value.T
                at = end


def gathered(blocks, with_all=True, with_turned=True):
    rows, depth = blocks[0].shape
    out_specs, out_shape = [], []
    if with_all:
        out_specs.append(by_rows(rows, depth))
        out_shape.append(shaped((4 * rows, depth), LOW))
    if with_turned:
        out_specs.append(pl.BlockSpec((depth, rows), lambda i: (0, i)))
        out_shape.append(shaped((depth, 4 * rows), LOW))
    out = pl.pallas_call(
        functools.partial(gathered_kernel, with_all),
        grid=(4,),
        in_specs=[whole(v) for v in blocks],
        out_specs=out_specs,
        out_shape=out_shape,
        name="gathered",
    )(*blocks)
    return tuple(out) if len(out) == 2 else out[0]


def added(refs):
    total = refs[0][...].astype(WIDE)
    for ref in refs[1:]:
        total = total + ref[...].astype(WIDE)
    return total


def join_kernel(x_ref, own_ref, near_ref, sent_ref, gain_ref, hidden_ref, normed_ref):
    hidden = added((x_ref, own_ref, near_ref, sent_ref))
    hidden_ref[...] = hidden
    normed_ref[...] = normalize(hidden, gain_ref[...])


def join(x, gain, *parts):
    rows, depth = x.shape
    step = rows // 2
    return pl.pallas_call(
        join_kernel,
        grid=(2,),
        in_specs=[by_rows(step, depth)] * 4 + [whole(gain)],
        out_specs=[by_rows(step, depth)] * 2,
        out_shape=[shaped((rows, depth), WIDE), shaped((rows, depth), LOW)],
        name="join",
    )(x, *parts, gain)


def feed_kernel(count, *refs):
    x_ref = refs[0]
    act_ref, slope_ref, silu_ref = refs[1 + count :]
    g_chunks, u_chunks = pieces_of(refs[1 : 1 + count], act_ref.shape[1], x_ref.shape[1])
    gate = times_chunks(x_ref, g_chunks)
    up = times_chunks(x_ref, u_chunks)
    sigmoid = 1.0 / (1.0 + jnp.exp(-gate))
    silu = gate * sigmoid
    act_ref[...] = (silu * up).astype(LOW)
    silu_ref[...] = silu.astype(LOW)
    slope_ref[...] = (up * sigmoid * (1.0 + gate * (1.0 - sigmoid))).astype(LOW)


def feed(x, panel, wide):
    total, depth = x.shape
    step = total // 4
    return pl.pallas_call(
        functools.partial(feed_kernel, len(panel)),
        grid=(4,),
        in_specs=[by_rows(step, depth)] + [whole(v) for v in panel],
        out_specs=[by_rows(step, wide)] * 3,
        out_shape=[shaped((total, wide), LOW)] * 3,
        name="feed",
    )(x, *panel)


def feed_back_kernel(count, split, *refs):
    dy_ref, slope_ref, silu_ref = refs[:3]
    (out_ref,) = refs[3 + count :]
    wide = slope_ref.shape[1]
    at = 0
    for chunks in pieces_of(refs[3 : 3 + count], split, dy_ref.shape[1]):
        end = at + chunks[0].shape[1]
        grads = times_chunks(dy_ref, chunks)
        out_ref[:, at:end] = (grads * slope_ref[:, at:end].astype(WIDE)).astype(LOW)
        out_ref[:, wide + at : wide + end] = (grads * silu_ref[:, at:end].astype(WIDE)).astype(LOW)
        at = end


def feed_back(grads, slope, silu, panel, split):
    total, depth = grads.shape
    wide = slope.shape[1]
    step = total // 4
    return pl.pallas_call(
        functools.partial(feed_back_kernel, len(panel), split),
        grid=(4,),
        in_specs=[by_rows(step, depth), by_rows(step, wide), by_rows(step, wide)]
        + [whole(v) for v in panel],
        out_specs=by_rows(step, 2 * wide),
        out_shape=shaped((total, 2 * wide), LOW),
        name="feed_back",
    )(grads, slope, silu, *panel)


def spread_kernel(count, split, *refs):
    value, out_refs = refs[0], refs[1 + count :]
    left, right = pieces_of(refs[1 : 1 + count], split, out_refs[0].shape[1])
    rows = out_refs[0].shape[0]
    each = value.shape[0] // rows
    for block, out_ref in enumerate(out_refs):
        inside = block % each

        @pl.when(pl.program_id(0) == block // each)
        def _(out_ref=out_ref, at=inside * rows):
            pieces = [value[at : at + rows, :split], value[at : at + rows, split:]]
            into_chunks(out_ref, pieces, [left, right])


def spread(value, panel, split, rows):
    total, wide = value.shape
    n = len(panel)
    depth = panel[0].shape[0] * max(1, n - 1)
    return pl.pallas_call(
        functools.partial(spread_kernel, n, split),
        grid=(4,),
        in_specs=[by_rows(total // 4, wide)] + [whole(c) for c in panel],
        out_specs=[fixed(rows, depth)] * 4,
        out_shape=[shaped((rows, depth), LOW)] * 4,
        name="spread",
    )(value, *panel)


def product_kernel(left, right, out):
    out[...] = dot(left[...], right[...]).astype(LOW)


def product(left, right):
    depth, total = left.shape
    wide = right.shape[1]
    step = depth // 8
    return pl.pallas_call(
        product_kernel,
        grid=(8,),
        in_specs=[by_rows(step, total), whole(right)],
        out_specs=by_rows(step, wide),
        out_shape=shaped((depth, wide), LOW),
        name="product",
    )(left, right)


def grow_kernel(split, narrow, count, *refs):
    ahead_terms, behind_terms = refs[:count], refs[count : 2 * count]
    ahead, behind, ahead_out, behind_out = refs[2 * count :]
    at = 0
    for ahead_term, behind_term in zip(ahead_terms, behind_terms):
        width = ahead_term.shape[1]
        cuts = [0, split - at, width] if at < split < at + width else [0, width]
        for low, high in zip(cuts[:-1], cuts[1:]):
            start, end = at + low, at + high
            first, second = ahead_term[:, low:high], behind_term[:, low:high]
            if not narrow or end <= split:
                first = first + ahead[:, start:end]
            if not narrow:
                second = second + behind[:, start:end]
            elif start >= split:
                second = second + behind[:, start - split : end - split]
            ahead_out[:, start:end] = first
            behind_out[:, start:end] = second
        at += width


def last_kernel(count, *refs):
    ahead, behind, out = refs[count:]
    at = 0
    for term in refs[:count]:
        end = at + term.shape[1]
        out[:, at:end] = term[...].astype(WIDE) + ahead[:, at:end].astype(WIDE) + behind[:, at:end].astype(WIDE)
        at = end


def grow(products, came, n, away, split):
    part = products[0].shape[0] // n
    wide = sum(v.shape[1] for v in products)
    narrow = away == n // 2 - 1
    step = part // 2
    came_specs = [by_rows(step, v.shape[1]) for v in came]

    def rows_at(offset):
        return [pl.BlockSpec((step, v.shape[1]), lambda i: (2 * offset + i, 0)) for v in products]

    if away == 0:
        return pl.pallas_call(
            functools.partial(last_kernel, len(products)),
            grid=(2,),
            in_specs=rows_at(0) + came_specs,
            out_specs=by_rows(step, wide),
            out_shape=shaped((part, wide), WIDE),
            name="last",
        )(*products, *came)
    return tuple(
        pl.pallas_call(
            functools.partial(grow_kernel, split, narrow, len(products)),
            grid=(2,),
            in_specs=rows_at(away) + rows_at(n - away) + came_specs,
            out_specs=[by_rows(step, wide)] * 2,
            out_shape=[shaped((part, wide), LOW)] * 2,
            name="grow",
        )(*products, *products, *came)
    )


def norm_back_kernel(hidden_ref, gain_ref, rest_ref, own_ref, near_ref, sent_ref, grads_ref, low_ref, terms_ref):
    hidden = hidden_ref[...].astype(WIDE)
    grad_normed = added((own_ref, near_ref, sent_ref))
    inverse = lax.rsqrt(jnp.mean(hidden * hidden, axis=-1, keepdims=True) + EPSILON)
    unit = hidden * inverse
    scaled = grad_normed * gain_ref[...]
    grads = rest_ref[...].astype(WIDE) + inverse * (
        scaled - unit * jnp.mean(scaled * unit, axis=-1, keepdims=True)
    )
    grads_ref[...] = grads
    low_ref[...] = grads.astype(LOW)

    @pl.when(pl.program_id(0) == 0)
    def _():
        terms_ref[...] = jnp.zeros_like(terms_ref)

    terms_ref[...] += jnp.sum(grad_normed * unit, axis=0, keepdims=True)


def norm_back(hidden, gain, rest, *parts):
    rows, depth = hidden.shape
    step = rows // 2
    return pl.pallas_call(
        norm_back_kernel,
        grid=(2,),
        in_specs=[by_rows(step, depth), whole(gain)] + [by_rows(step, depth)] * 4,
        out_specs=[by_rows(step, depth), by_rows(step, depth), pl.BlockSpec((1, depth), lambda i: (0, 0))],
        out_shape=[shaped((rows, depth), WIDE), shaped((rows, depth), LOW), shaped((1, depth), WIDE)],
        name="norm_back",
    )(hidden, gain, rest, *parts)


def shuffle_kernel(n, order_ref, *refs):
    out_ref = refs[-1]
    part = out_ref.shape[1] // n
    for s in range(n):
        at = pl.multiple_of(order_ref[s] * part, part)
        if len(refs) == 2:
            piece = refs[0][:, pl.ds(at, part)]
        else:
            piece = refs[0][:, pl.ds(at, part)]
            for ref in refs[1:-1]:
                piece = piece + ref[:, pl.ds(at, part)].astype(WIDE)
        out_ref[:, s * part : (s + 1) * part] = piece.astype(out_ref.dtype)


def shuffle(order, n, *values):
    rows, depth = values[0].shape
    part = depth // n
    if part % LANES:
        total = values[0]
        for v in values[1:]:
            total = total + v.astype(WIDE)
        pieces = [lax.dynamic_slice(total, (0, order[s] * part), (rows, part)) for s in range(n)]
        return jnp.concatenate(pieces, axis=1).astype(LOW)
    step = rows // 2
    return pl.pallas_call(
        functools.partial(shuffle_kernel, n),
        grid_spec=pltpu.PrefetchScalarGridSpec(
            num_scalar_prefetch=1,
            grid=(2,),
            in_specs=[pl.BlockSpec((step, depth), lambda i, order: (i, 0))] * len(values),
            out_specs=pl.BlockSpec((step, depth), lambda i, order: (i, 0)),
        ),
        out_shape=shaped((rows, depth), LOW),
        name="shuffle",
    )(order, *values)


def tables(segment_block):
    rows = segment_block.shape[0]
    places = jnp.arange(rows, dtype=jnp.int32)
    same = segment_block[:, None] == segment_block[None, :]
    first_index = jnp.min(jnp.where(same, places[None, :], rows), axis=1)
    offsets = (places - first_index).astype(WIDE)
    half = HEAD_DIM // 2
    frequencies = jnp.exp(jnp.arange(half, dtype=WIDE) * (-2.0 * math.log(ROPE_BASE) / HEAD_DIM))
    angles = offsets[:, None] * frequencies[None, :]
    cosine, sine = jnp.cos(angles), jnp.sin(angles)
    return jnp.concatenate([cosine] * 4, axis=1), jnp.concatenate([sine] * 4, axis=1)


def on_device(
    tokens, segments, gain_attn, w_query, w_key, w_value, w_out, gain_mlp, w_gate, w_up, w_down, cotangent
):
    n = lax.axis_size("dp")
    rows, depth = tokens.shape
    part = depth // n
    hops = n // 2
    me = lax.axis_index("dp")
    sources, offsets = [lax.dynamic_index_in_dim(jnp.asarray(t), me, keepdims=False) for t in ring_tables(n)]
    line = Line(jnp.zeros((8, LANES), WIDE))

    heads_wide, hidden_wide = w_query.shape[1], w_gate.shape[1]
    qkv_wide = heads_wide + w_key.shape[1] + w_value.shape[1]
    split = -(-hidden_wide // (2 * LANES)) * LANES
    attn_own = jnp.concatenate([w_query, w_key, w_value, w_out.T], axis=1).astype(LOW)
    gains = jnp.stack([gain_attn, gain_mlp]).astype(LOW)
    gains = jnp.pad(gains, ((0, 14), (0, attn_own.shape[1] - part)))
    attn = RingGather(line, jnp.concatenate([attn_own, gains], axis=0), n, qkv_wide, part)
    feedw = RingGather(line, jnp.concatenate([w_gate, w_up], axis=1).astype(LOW), n, hidden_wide, part)
    down = RingGather(line, w_down.T.astype(LOW), n, split, part)

    attn.start(1)
    own_tokens = shuffle(sources, n, tokens)
    marks = jnp.broadcast_to(segments.astype(LOW)[:, None], (rows, LANES))
    x = GroupGather(line, jnp.concatenate([own_tokens, marks], axis=1))
    attn.wait(1)
    attn.start(2)
    own_grads = line.run(lambda *v: shuffle(v[0], n, v[1]), sources, cotangent)
    for hop in range(2, hops - 1):
        attn.wait(hop)
        attn.start(hop + 1)
    attn.wait(hops - 1)
    attn.start(hops)
    token_rows = line.run(lambda *v: gathered(v, with_turned=False), *x.blocks())
    attn.wait(hops)
    feedw.start(1)
    y = GroupGather(line, own_grads)
    segment_blocks = token_rows[:, depth].astype(jnp.int32).reshape(-1, rows)
    column, row = segment_blocks.reshape(-1, 1), segment_blocks[:, None, :]
    cosine, sine = line.run(lambda v: jax.vmap(tables)(v), segment_blocks)
    cosine, sine = cosine.reshape(-1, LANES), sine.reshape(-1, LANES)
    gains = attn.extra(2).astype(WIDE)
    gain_one, gain_two = gains[0:1], gains[1:2]

    attn_panel = attn.panel()
    normed_turned, query, keyval, mixed, log_sums, *branch = line.run(
        lambda *v: attend(*v[:6], v[6:], heads_wide, rows),
        token_rows, gain_one, cosine, sine, column, row, *attn_panel,
    )
    feedw.wait(1)
    feedw.start(2)
    branch = GroupReduce(line, branch)
    grads_all, grads_turned = line.run(lambda *v: gathered(v), *y.blocks())
    branch.relay()
    for hop in range(2, hops - 1):
        feedw.wait(hop)
        feedw.start(hop + 1)
    hidden, normed_own = line.run(join, own_tokens, gain_two, *branch.terms())
    z = GroupGather(line, normed_own)
    feedw.wait(hops - 1)
    feedw.start(hops)
    normed_mlp, mlp_turned = line.run(lambda *v: gathered(v), *z.blocks())

    feedw.wait(hops)
    down.start(1)
    feed_panel = feedw.panel()
    activation, slope, silu = line.run(lambda a, *v: feed(a, v, hidden_wide), normed_mlp, *feed_panel)
    for hop in range(1, hops):
        down.wait(hop)
        down.start(hop + 1)
        if hop == 1:
            down_terms = line.run(lambda a, b: product(a, b), grads_turned, activation)
            r_down = RingReduce(line, [down_terms], n, split)
    r_down.start(1)
    down.wait(hops)
    down_panel = down.panel()
    r_down.wait(1)
    r_down.start(2)

    grad_feed = line.run(
        lambda a, b, c, *v: feed_back(a, b, c, v, split), grads_all, slope, silu, *down_panel
    )
    for hop in range(2, hops - 1):
        r_down.wait(hop)
        r_down.start(hop + 1)
    feed_terms = line.run(lambda a, b: product(a, b), mlp_turned, grad_feed)
    r_feed = RingReduce(line, [feed_terms], n, hidden_wide)
    r_down.wait(hops - 1)
    r_down.start(hops)
    r_feed.start(1)
    grad_normed = line.run(lambda a, *v: spread(a, v, hidden_wide, rows), grad_feed, *feed_panel)
    r_down.wait(hops)
    r_feed.wait(1)
    r_feed.start(2)
    grad_normed = GroupReduce(line, grad_normed)
    grad_normed.relay()
    grad_down = r_down.total()
    layer_part = line.run(lambda a, *v: spread(a, v, split, rows), activation, *down_panel)
    for hop in range(2, hops - 1):
        r_feed.wait(hop)
        r_feed.start(hop + 1)
    grad_hidden, grad_branch, gain_mlp_terms = line.run(
        norm_back, hidden, gain_two, own_grads, *grad_normed.terms()
    )
    b = GroupGather(line, grad_branch)
    b_core = line.passed(line.send(b.own, "fsdp", CORE))
    extras = (query, keyval, log_sums, cosine, sine, column, row)

    def backward(blocks, groups, before=None):
        sizes = [len(group) for group in groups]
        flat = [v for group in groups for v in group]
        k = len(flat)

        def work(*v):
            split_groups = [v[sum(sizes[:i]) : sum(sizes[: i + 1])] for i in range(len(sizes))]
            last = len(v) if before is None else len(v) - 1
            return attend_back(
                blocks, split_groups, *v[k : k + 7], v[k + 7 : last], rows, None if before is None else v[-1]
            )

        return line.run(work, *flat, *extras, *attn_panel, *([] if before is None else [before]))

    grad_qkv, own, core = backward((0, 2), [[b.own], [b_core]])
    r_feed.wait(hops - 1)
    r_feed.start(hops)
    upper, lower = b.relay()
    grad_qkv, pair, diagonal = backward((1, 3), [[b.pair], [upper, lower]], grad_qkv)
    grad_input_sum = GroupReduce(line, [own, pair, core, diagonal])
    grad_input_sum.relay()
    branch_turned = line.run(
        lambda *v: gathered(v, with_all=False), b.own, b.pair, b_core, upper, lower
    )
    out_terms = line.run(product, branch_turned, mixed)
    attn_terms = line.run(product, normed_turned, grad_qkv)
    r_attn = RingReduce(line, [attn_terms, out_terms], n, qkv_wide)
    r_feed.wait(hops)
    r_attn.start(1)
    grad_w_feed = r_feed.total()
    r_attn.wait(1)
    r_attn.start(2)
    _, grad_tokens, gain_attn_terms = line.run(
        norm_back, own_tokens, gain_one, grad_hidden, *grad_input_sum.terms()
    )
    gain_terms = jnp.concatenate([gain_attn_terms, gain_mlp_terms], axis=0).reshape(2, n, part)
    gain_terms = jnp.take(gain_terms, offsets, axis=1).reshape(2, depth)
    gain_steps = [("fsdp", 4, 1), ("fsdp", 4, 2)] + [("dp", n, 1 << i) for i in range((n - 1).bit_length())]
    flying = []

    def gain_send():
        if gain_steps:
            axis, size, bit = gain_steps.pop(0)
            flying.append(line.send(gain_terms, axis, [(i, i ^ bit) for i in range(size)]))

    def gain_take(value):
        return line.run(jnp.add, value, line.passed(flying.pop())) if flying else value

    for _ in range(2):
        gain_send()
        gain_terms = gain_take(gain_terms)
    for hop in range(2, hops - 1):
        r_attn.wait(hop)
        r_attn.start(hop + 1)
    gain_send()
    layer_sum = GroupReduce(line, layer_part)
    layer_sum.relay()
    grad_tokens = line.run(lambda at, v: shuffle(at, n, v), offsets, grad_tokens)
    r_attn.wait(hops - 1)
    r_attn.start(hops)
    while len(gain_steps) > 1:
        gain_terms = gain_take(gain_terms)
        gain_send()
    layer_own = line.run(lambda at, *v: shuffle(at, n, *v), offsets, hidden, *layer_sum.terms())
    r_attn.wait(hops)
    while flying:
        gain_terms = gain_take(gain_terms)
        gain_send()
    grad_attn = r_attn.total()
    gain_own = lax.dynamic_slice(gain_terms, (0, me * part), (2, part))

    value_at = heads_wide + w_key.shape[1]
    return (
        layer_own,
        grad_tokens,
        gain_own[0],
        grad_attn[:, :heads_wide],
        grad_attn[:, heads_wide:value_at],
        grad_attn[:, value_at:qkv_wide],
        grad_attn[:, qkv_wide:].T,
        gain_own[1],
        grad_w_feed[:, :hidden_wide],
        grad_w_feed[:, hidden_wide:],
        grad_down.T,
    )


def solution(mesh):
    placed = (
        P(("dp", "fsdp"), None),
        P(("dp", "fsdp")),
        P("dp"),
        P("dp", "fsdp"),
        P("dp", "fsdp"),
        P("dp", "fsdp"),
        P("fsdp", "dp"),
        P("dp"),
        P("dp", "fsdp"),
        P("dp", "fsdp"),
        P("fsdp", "dp"),
        P(("dp", "fsdp"), None),
    )
    return jax.shard_map(
        on_device,
        mesh=mesh,
        in_specs=placed,
        out_specs=(
            P(("dp", "fsdp"), None),
            P(("dp", "fsdp"), None),
            P("dp"),
            P("dp", "fsdp"),
            P("dp", "fsdp"),
            P("dp", "fsdp"),
            P("fsdp", "dp"),
            P("dp"),
            P("dp", "fsdp"),
            P("dp", "fsdp"),
            P("fsdp", "dp"),
        ),
        check_vma=False,
    )
```

```python
import functools
import math

import jax
import jax.numpy as jnp
import numpy as np
from jax import lax
from jax.experimental import pallas as pl
from jax.experimental.pallas import tpu as pltpu
from jax.sharding import PartitionSpec as P

HEAD_DIM = 64
EPSILON = 1e-05
ROPE_BASE = 10000.0
LOW = jnp.bfloat16
WIDE = jnp.float32
LANES = 128


def ring_order(n):
    return list(range(0, n, 2)) + list(range(n - 1, 0, -2))


def ring_perms(n):
    order = ring_order(n)
    forward = [(order[i], order[(i + 1) % n]) for i in range(n)]
    return forward, [(b, a) for a, b in forward]


def ring_tables(n):
    order = ring_order(n)
    place = [order.index(j) for j in range(n)]
    sources = [[order[(place[i] + s) % n] for s in range(n)] for i in range(n)]
    offsets = [[(place[j] - place[i]) % n for j in range(n)] for i in range(n)]
    return np.array(sources, np.int32), np.array(offsets, np.int32)


class Line:
    def __init__(self, token):
        self.token = token

    def after(self, *values):
        out = lax.optimization_barrier((*values, self.token))
        return out[0] if len(values) == 1 else out[:-1]

    def passed(self, *values):
        out = lax.optimization_barrier((*values, self.token))
        self.token = out[-1]
        return out[0] if len(values) == 1 else out[:-1]

    def run(self, work, *values):
        result = work(*lax.optimization_barrier((*values, self.token))[:-1])
        if not isinstance(result, (tuple, list)):
            return self.passed(result)
        out = lax.optimization_barrier((*result, self.token))
        self.token = out[-1]
        return out[:-1]

    def send(self, value, axis, pairs):
        return lax.ppermute(self.after(value), axis, pairs)


class RingGather:
    def __init__(self, line, own, n, split, part):
        self.line, self.n, self.split, self.part = line, n, split, part
        self.chunks = {0: own}
        self.flying = None

    def start(self, hop):
        n, pairs = self.n, ring_perms(self.n)
        ahead, behind = self.chunks[(n - hop + 1) % n], self.chunks[hop - 1]
        if hop == n // 2:
            ahead, behind = ahead[:, : self.split], behind[:, self.split :]
        self.flying = (self.line.send(ahead, "dp", pairs[0]), self.line.send(behind, "dp", pairs[1]))

    def wait(self, hop):
        ahead, behind = self.line.passed(*self.flying)
        if hop == self.n // 2:
            self.far = (ahead, behind)
        else:
            self.chunks[self.n - hop], self.chunks[hop] = ahead, behind

    def panel(self):
        n, part = self.n, self.part
        near = [self.chunks[s] for s in range(n) if s != n // 2]
        if part % LANES == 0:
            return [*near, *self.far]
        far = jnp.concatenate(self.far, axis=1)
        return [jnp.concatenate([v[:part] for v in (*near[: n // 2], far, *near[n // 2 :])], axis=0)]

    def extra(self, count):
        n, part = self.n, self.part
        chunks = [self.far[0] if s == n // 2 else self.chunks[s] for s in range(n)]
        return jnp.concatenate([c[part : part + count, :part] for c in chunks], axis=1)


class RingReduce:
    def __init__(self, line, products, far, n, split):
        self.line, self.products, self.far, self.n, self.split = line, products, far, n, split
        self.came = ()

    def start(self, hop):
        n, pairs = self.n, ring_perms(self.n)
        k = len(self.products)
        ahead, behind = self.far
        if hop > 1:
            away = n // 2 - hop + 1
            ahead, behind = self.line.run(
                lambda *v: grow(v[:k], v[k:], n, away, self.split), *self.products, *self.came
            )
        self.came = (self.line.send(ahead, "dp", pairs[0]), self.line.send(behind, "dp", pairs[1]))

    def wait(self, hop):
        self.came = self.line.passed(*self.came)

    def total(self, outputs):
        k = len(self.products)
        return self.line.run(lambda *v: last(v[:k], v[k:], self.n, outputs), *self.products, *self.came)


CORE = [(i, i ^ 1) for i in range(4)]
PAIR = [(i, i ^ 2) for i in range(4)]


class GroupGather:
    def __init__(self, line, own):
        self.line, self.own = line, own
        self.pair = line.send(own, "fsdp", PAIR)

    def relay(self):
        self.pair = self.line.passed(self.pair)
        half = self.pair.shape[0] // 2
        upper = self.line.send(self.pair[:half], "fsdp", CORE)
        lower = self.line.send(self.pair[half:], "fsdp", CORE)
        return self.line.passed(upper, lower)

    def blocks(self):
        core = self.line.send(self.own, "fsdp", CORE)
        upper, lower = self.relay()
        return [self.own, self.pair, self.line.passed(core), upper, lower]


class GroupReduce:
    def __init__(self, line, blocks):
        self.line, self.blocks = line, blocks
        half = blocks[3].shape[0] // 2
        self.upper = line.send(blocks[3][:half], "fsdp", CORE)
        self.lower = line.send(blocks[3][half:], "fsdp", CORE)

    def relay(self):
        far = self.line.passed(self.upper, self.lower)
        self.sent = self.line.send(self.line.run(plus, self.blocks[1], *far), "fsdp", PAIR)
        self.near = self.line.send(self.blocks[2], "fsdp", CORE)

    def terms(self):
        self.near, self.sent = self.line.passed(self.near, self.sent)
        return self.blocks[0], self.near, self.sent


def dot(a, b):
    return jnp.dot(a, b, preferred_element_type=WIDE)


def dot_rows(a, b):
    return lax.dot_general(a, b, (((1,), (1,)), ((), ())), preferred_element_type=WIDE)


def dot_firsts(a, b):
    return lax.dot_general(a, b, (((0,), (0,)), ((), ())), preferred_element_type=WIDE)


def by_rows(rows, width):
    return pl.BlockSpec((rows, width), lambda i: (i, 0))


def whole(value):
    zeros = (0,) * value.ndim
    return pl.BlockSpec(value.shape, lambda i: zeros, pipeline_mode=pl.Buffered(1))


def shaped(shape, kind):
    return jax.ShapeDtypeStruct(shape, kind)


def times_chunks(value, chunks):
    total, at = None, 0
    for chunk in chunks:
        size = chunk.shape[0]
        term = dot(value[:, at : at + size], chunk[...])
        total = term if total is None else total + term
        at += size
    return total


def into_chunks(out_ref, values, chunk_sets):
    at = 0
    for row in zip(*chunk_sets):
        size = row[0].shape[0]
        total = None
        for value, chunk in zip(values, row):
            term = dot_rows(value, chunk[...])
            total = term if total is None else total + term
        out_ref[:, at : at + size] = total.astype(out_ref.dtype)
        at += size


def pieces_of(panel, split, depth):
    if len(panel) == 1:
        chunk = panel[0]
        return [chunk.at[:, :split]], [chunk.at[:, split:]]
    part = depth // (len(panel) - 1)
    near, far = panel[:-2], [chunk.at[:part, :] for chunk in panel[-2:]]
    left = [chunk.at[:part, :split] for chunk in near]
    right = [chunk.at[:part, split:] for chunk in near]
    at = (len(near) + 1) // 2
    return left[:at] + [far[0]] + left[at:], right[:at] + [far[1]] + right[at:]


def into_block(out_refs, value_ref):
    for block, out_ref in enumerate(out_refs):

        @pl.when(pl.program_id(0) == block)
        def _(out_ref=out_ref):
            out_ref[...] = value_ref[...]


def turn(values, first_half):
    width = values.shape[-1]
    left = pltpu.roll(values, width - HEAD_DIM // 2, 1)
    right = pltpu.roll(values, HEAD_DIM // 2, 1)
    return jnp.where(first_half, -left, right)


def lane_ids(rows, width):
    return lax.broadcasted_iota(jnp.int32, (rows, width), 1)


def allowed_pairs(column, row):
    rows = column.shape[0]
    later = lax.broadcasted_iota(jnp.int32, (rows, rows), 0)
    earlier = lax.broadcasted_iota(jnp.int32, (rows, rows), 1)
    return (column == row) & (later >= earlier)


def normalize(hidden, gain):
    inverse = lax.rsqrt(jnp.mean(hidden * hidden, axis=-1, keepdims=True) + EPSILON)
    return (hidden * inverse * gain).astype(LOW)


def attention_forward(count, *refs):
    x_ref, gain_ref, cos_ref, sin_ref, col_ref, row_ref = refs[:6]
    turned_ref, q_ref, kv_ref, o_ref, lse_ref = refs[6 + count : 11 + count]
    branch_refs, qkv_ref, made_ref = refs[11 + count : 15 + count], refs[15 + count], refs[16 + count]
    q_chunks, o_chunks = pieces_of(refs[6 : 6 + count], qkv_ref.shape[1], gain_ref.shape[1])
    depth = gain_ref.shape[1]
    rows, width = q_ref.shape
    pairs = width // LANES
    normed = normalize(x_ref[:, :depth].astype(WIDE), gain_ref[...])
    turned_ref[...] = normed.T
    qkv_ref[...] = times_chunks(normed, q_chunks)
    cosine, sine = cos_ref[...], sin_ref[...]
    lanes = lane_ids(rows, LANES)
    even = lanes < HEAD_DIM
    first = (lanes % HEAD_DIM) < HEAD_DIM // 2
    keyval = qkv_ref[:, width:]
    keyval_rot = keyval * cosine + turn(keyval, first) * sine
    keyval = jnp.where(even, keyval_rot, keyval)
    kv_ref[...] = keyval.astype(LOW)
    other = pltpu.roll(keyval, HEAD_DIM, 1)
    keys = jnp.where(even, keyval, other).astype(LOW)
    vals = jnp.where(even, other, keyval).astype(LOW)
    allowed = allowed_pairs(col_ref[...], row_ref[0])
    log_sums = jnp.zeros((rows, LANES), WIDE)
    for pair in range(pairs):
        piece = qkv_ref[:, pair * LANES : (pair + 1) * LANES]
        piece = (piece * cosine + turn(piece, first) * sine).astype(LOW)
        q_ref[:, pair * LANES : (pair + 1) * LANES] = piece
        mixed = []
        for side in range(2):
            chosen = jnp.where(even if side == 0 else ~even, piece, jnp.zeros_like(piece))
            scores = dot_rows(chosen, keys) * (HEAD_DIM ** -0.5)
            scores = jnp.where(allowed, scores, -1e30)
            peak = jnp.max(scores, axis=1, keepdims=True)
            powers = jnp.exp(scores - peak)
            total = jnp.sum(powers, axis=1, keepdims=True)
            soft = (powers / total).astype(LOW)
            mixed.append(dot(soft, vals))
            log_sums = jnp.where(lanes == 2 * pair + side, peak + jnp.log(total), log_sums)
        o_ref[:, pair * LANES : (pair + 1) * LANES] = jnp.where(even, mixed[0], mixed[1]).astype(LOW)
    lse_ref[...] = log_sums
    into_chunks(made_ref, [o_ref[...]], [o_chunks])
    into_block(branch_refs, made_ref)


def fixed(rows, width):
    return pl.BlockSpec((rows, width), lambda i: (0, 0))


def attend(x, gain, cosine, sine, column, row, panel, width, rows):
    total, depth = x.shape[0], gain.shape[1]
    return pl.pallas_call(
        functools.partial(attention_forward, len(panel)),
        grid=(total // rows,),
        in_specs=[
            by_rows(rows, x.shape[1]),
            whole(gain),
            by_rows(rows, LANES),
            by_rows(rows, LANES),
            by_rows(rows, 1),
            pl.BlockSpec((1, 1, rows), lambda i: (i, 0, 0)),
        ]
        + [whole(v) for v in panel],
        out_specs=[
            pl.BlockSpec((depth, rows), lambda i: (0, i)),
            by_rows(rows, width),
            by_rows(rows, LANES),
            by_rows(rows, width),
            by_rows(rows, LANES),
        ]
        + [fixed(rows, depth)] * 4,
        out_shape=[
            shaped((depth, total), LOW),
            shaped((total, width), LOW),
            shaped((total, LANES), LOW),
            shaped((total, width), LOW),
            shaped((total, LANES), WIDE),
        ]
        + [shaped((rows, depth), LOW)] * 4,
        scratch_shapes=[pltpu.VMEM((rows, width + LANES), WIDE), pltpu.VMEM((rows, depth), LOW)],
        name="attend",
    )(x, gain, cosine, sine, column, row, *panel)


def attention_backward(sizes, count, *refs):
    dh_refs, refs = refs[: sum(sizes)], refs[sum(sizes) :]
    q_ref, kv_ref, lse_ref, cos_ref, sin_ref, col_ref, row_ref = refs[:7]
    panel, refs = refs[7 : 7 + count], refs[-len(sizes) - 3 :]
    grad_ref, part_refs, do_ref, made_ref = refs[0], refs[1:-2], refs[-2], refs[-1]
    q_chunks, o_chunks = pieces_of(panel, grad_ref.shape[1], dh_refs[0].shape[1])
    rows, width = q_ref.shape
    pairs = width // LANES
    scale = HEAD_DIM ** -0.5
    for block, size in enumerate(sizes):

        @pl.when(pl.program_id(0) == block)
        def _(mine=dh_refs[sum(sizes[:block]) : sum(sizes[: block + 1])]):
            at = 0
            for ref in mine:
                end = at + ref.shape[0]
                made_ref[at:end, :] = ref[...]
                at = end

    do_ref[...] = times_chunks(made_ref, o_chunks).astype(LOW)
    cosine, sine = cos_ref[...], sin_ref[...]
    lanes = lane_ids(rows, LANES)
    even = lanes < HEAD_DIM
    first = (lanes % HEAD_DIM) < HEAD_DIM // 2
    keyval = kv_ref[...].astype(WIDE)
    other = pltpu.roll(keyval, HEAD_DIM, 1)
    keys = jnp.where(even, keyval, other).astype(LOW)
    vals = jnp.where(even, other, keyval).astype(LOW)
    allowed = allowed_pairs(col_ref[...], row_ref[0])
    log_sums = lse_ref[...]

    def heads(pair, totals):
        grad_keys, grad_vals = totals
        span = pl.ds(pl.multiple_of(pair * LANES, LANES), LANES)
        piece = q_ref[:, span]
        grads = do_ref[:, span]
        turned = []
        for side in range(2):
            mine = even if side == 0 else ~even
            chosen = jnp.where(mine, piece, jnp.zeros_like(piece))
            chosen_grad = jnp.where(mine, grads, jnp.zeros_like(grads))
            own = jnp.where(lanes == 2 * pair + side, log_sums, 0.0)
            log_sum = jnp.sum(own, axis=1, keepdims=True)
            scores = jnp.where(allowed, dot_rows(chosen, keys) * scale, -1e30)
            soft = jnp.exp(scores - log_sum)
            grad_soft = dot_rows(chosen_grad, vals)
            delta = jnp.sum(soft * grad_soft, axis=1, keepdims=True)
            grad_scores = (soft * (grad_soft - delta)).astype(LOW)
            grad_vals = grad_vals + dot_firsts(soft.astype(LOW), chosen_grad)
            grad_keys = grad_keys + dot_firsts(grad_scores, chosen)
            turned.append(dot(grad_scores, keys))
        grad_q = jnp.where(even, turned[0], turned[1]) * scale
        grad_q = grad_q * cosine - turn(grad_q, first) * sine
        grad_ref[:, span] = grad_q.astype(LOW)
        return grad_keys, grad_vals

    nothing = jnp.zeros((rows, LANES), WIDE)
    grad_keys, grad_vals = lax.fori_loop(0, pairs, heads, (nothing, nothing), unroll=2)
    grad_keys = (grad_keys + pltpu.roll(grad_keys, HEAD_DIM, 1)) * scale
    grad_keys = grad_keys * cosine - turn(grad_keys, first) * sine
    grad_vals = grad_vals + pltpu.roll(grad_vals, HEAD_DIM, 1)
    grad_ref[:, width:] = jnp.where(even, grad_keys, grad_vals).astype(LOW)
    into_chunks(made_ref, [grad_ref[...]], [q_chunks])
    into_block(part_refs, made_ref)


def attend_back(blocks, groups, query, keyval, log_sums, cosine, sine, column, row, panel, rows, before=None):
    total, width = query.shape
    depth = groups[0][0].shape[1]
    first, step = blocks[0], blocks[1] - blocks[0]
    flat = [v for group in groups for v in group]

    def chosen(wide):
        return pl.BlockSpec((rows, wide), lambda i: (first + step * i, 0))

    operands = [*flat, query, keyval, log_sums, cosine, sine, column, row, *panel]
    in_specs = [whole(v) for v in flat]
    in_specs += [chosen(width), chosen(LANES), chosen(LANES), chosen(LANES), chosen(LANES), chosen(1)]
    in_specs += [pl.BlockSpec((1, 1, rows), lambda i: (first + step * i, 0, 0))]
    in_specs += [whole(v) for v in panel]
    aliases = {}
    if before is not None:
        aliases = {len(operands): 0}
        operands.append(before)
        in_specs.append(pl.BlockSpec(memory_space=pl.ANY))
    return pl.pallas_call(
        functools.partial(attention_backward, [len(group) for group in groups], len(panel)),
        grid=(len(groups),),
        in_specs=in_specs,
        out_specs=[chosen(width + LANES)] + [fixed(rows, depth)] * len(groups),
        out_shape=[shaped((total, width + LANES), LOW)] + [shaped((rows, depth), LOW)] * len(groups),
        scratch_shapes=[pltpu.VMEM((rows, width), LOW), pltpu.VMEM((rows, depth), LOW)],
        input_output_aliases=aliases,
        name="attend_back",
    )(*operands)


def plus_kernel(value_ref, upper_ref, lower_ref, out_ref):
    rows = upper_ref.shape[0]
    out_ref[:rows, :] = value_ref[:rows, :] + upper_ref[...]
    out_ref[rows:, :] = value_ref[rows:, :] + lower_ref[...]


def plus(value, upper, lower):
    rows, depth = value.shape
    step = depth // 2

    def columns(size):
        return pl.BlockSpec((size, step), lambda i: (0, i))

    return pl.pallas_call(
        plus_kernel,
        grid=(2,),
        in_specs=[columns(rows), columns(rows // 2), columns(rows // 2)],
        out_specs=columns(rows),
        out_shape=shaped(value.shape, value.dtype),
        name="plus",
    )(value, upper, lower)


def gathered_kernel(with_all, own, pair, core, upper, lower, *outs):
    all_ref = outs[0] if with_all else None
    turned_ref = outs[-1] if len(outs) == 2 or not with_all else None
    for block, refs in enumerate(((own,), (pair,), (core,), (upper, lower))):

        @pl.when(pl.program_id(0) == block)
        def _(refs=refs):
            at = 0
            for ref in refs:
                value = ref[...]
                end = at + value.shape[0]
                if all_ref is not None:
                    all_ref[at:end, :] = value
                if turned_ref is not None:
                    turned_ref[:, at:end] = value.T
                at = end


def gathered(blocks, with_all=True, with_turned=True):
    rows, depth = blocks[0].shape
    out_specs, out_shape = [], []
    if with_all:
        out_specs.append(by_rows(rows, depth))
        out_shape.append(shaped((4 * rows, depth), LOW))
    if with_turned:
        out_specs.append(pl.BlockSpec((depth, rows), lambda i: (0, i)))
        out_shape.append(shaped((depth, 4 * rows), LOW))
    out = pl.pallas_call(
        functools.partial(gathered_kernel, with_all),
        grid=(4,),
        in_specs=[whole(v) for v in blocks],
        out_specs=out_specs,
        out_shape=out_shape,
        name="gathered",
    )(*blocks)
    return tuple(out) if len(out) == 2 else out[0]


def added(refs):
    total = refs[0][...].astype(WIDE)
    for ref in refs[1:]:
        total = total + ref[...].astype(WIDE)
    return total


def join_kernel(x_ref, own_ref, near_ref, sent_ref, gain_ref, hidden_ref, normed_ref):
    hidden = added((x_ref, own_ref, near_ref, sent_ref))
    hidden_ref[...] = hidden
    normed_ref[...] = normalize(hidden, gain_ref[...])


def join(x, gain, *parts):
    rows, depth = x.shape
    step = rows // 2
    return pl.pallas_call(
        join_kernel,
        grid=(2,),
        in_specs=[by_rows(step, depth)] * 4 + [whole(gain)],
        out_specs=[by_rows(step, depth)] * 2,
        out_shape=[shaped((rows, depth), WIDE), shaped((rows, depth), LOW)],
        name="join",
    )(x, *parts, gain)


def feed_kernel(count, *refs):
    x_ref = refs[0]
    act_ref, slope_ref, silu_ref = refs[1 + count :]
    g_chunks, u_chunks = pieces_of(refs[1 : 1 + count], act_ref.shape[1], x_ref.shape[1])
    gate = times_chunks(x_ref, g_chunks)
    up = times_chunks(x_ref, u_chunks)
    sigmoid = 1.0 / (1.0 + jnp.exp(-gate))
    silu = gate * sigmoid
    act_ref[...] = (silu * up).astype(LOW)
    silu_ref[...] = silu.astype(LOW)
    slope_ref[...] = (up * sigmoid * (1.0 + gate * (1.0 - sigmoid))).astype(LOW)


def feed(x, panel, wide):
    total, depth = x.shape
    step = total // 8
    return pl.pallas_call(
        functools.partial(feed_kernel, len(panel)),
        grid=(8,),
        in_specs=[by_rows(step, depth)] + [whole(v) for v in panel],
        out_specs=[by_rows(step, wide)] * 3,
        out_shape=[shaped((total, wide), LOW)] * 3,
        name="feed",
    )(x, *panel)


def feed_back_kernel(count, split, *refs):
    dy_ref, slope_ref, silu_ref = refs[:3]
    (out_ref,) = refs[3 + count :]
    wide = slope_ref.shape[1]
    at = 0
    for chunks in pieces_of(refs[3 : 3 + count], split, dy_ref.shape[1]):
        end = at + chunks[0].shape[1]
        grads = times_chunks(dy_ref, chunks)
        out_ref[:, at:end] = (grads * slope_ref[:, at:end].astype(WIDE)).astype(LOW)
        out_ref[:, wide + at : wide + end] = (grads * silu_ref[:, at:end].astype(WIDE)).astype(LOW)
        at = end


def feed_back(grads, slope, silu, panel, split):
    total, depth = grads.shape
    wide = slope.shape[1]
    step = total // 4
    return pl.pallas_call(
        functools.partial(feed_back_kernel, len(panel), split),
        grid=(4,),
        in_specs=[by_rows(step, depth), by_rows(step, wide), by_rows(step, wide)]
        + [whole(v) for v in panel],
        out_specs=by_rows(step, 2 * wide),
        out_shape=shaped((total, 2 * wide), LOW),
        name="feed_back",
    )(grads, slope, silu, *panel)


def spread_kernel(count, split, *refs):
    value, out_refs, made_ref = refs[0], refs[1 + count : -1], refs[-1]
    left, right = pieces_of(refs[1 : 1 + count], split, made_ref.shape[1])
    into_chunks(made_ref, [value[:, :split], value[:, split:]], [left, right])
    into_block(out_refs, made_ref)


def spread(value, panel, split, rows):
    total, wide = value.shape
    n = len(panel)
    depth = panel[0].shape[0] * max(1, n - 1)
    return pl.pallas_call(
        functools.partial(spread_kernel, n, split),
        grid=(4,),
        in_specs=[by_rows(rows, wide)] + [whole(c) for c in panel],
        out_specs=[fixed(rows, depth)] * 4,
        out_shape=[shaped((rows, depth), LOW)] * 4,
        scratch_shapes=[pltpu.VMEM((rows, depth), LOW)],
        name="spread",
    )(value, *panel)


def product_kernel(left, right, out, *far_refs):
    total = dot(left[...], right[...]).astype(LOW)
    out[...] = total

    @pl.when(pl.program_id(0) == pl.num_programs(0) // 2)
    def _():
        at = 0
        for far_ref in far_refs:
            part, width = far_ref.shape
            far_ref[...] = total[:part, at : at + width]
            at += width


def product(left, right, n, widths):
    depth, total = left.shape
    wide = right.shape[1]
    step = depth // 8
    return pl.pallas_call(
        product_kernel,
        grid=(8,),
        in_specs=[by_rows(step, total), whole(right)],
        out_specs=[by_rows(step, wide)] + [fixed(depth // n, width) for width in widths],
        out_shape=[shaped((depth, wide), LOW)] + [shaped((depth // n, width), LOW) for width in widths],
        name="product",
    )(left, right)


def grow_kernel(split, narrow, count, *refs):
    ahead_terms, behind_terms = refs[:count], refs[count : 2 * count]
    ahead, behind, ahead_out, behind_out = refs[2 * count :]
    at = 0
    for ahead_term, behind_term in zip(ahead_terms, behind_terms):
        width = ahead_term.shape[1]
        cuts = [0, split - at, width] if at < split < at + width else [0, width]
        for low, high in zip(cuts[:-1], cuts[1:]):
            start, end = at + low, at + high
            first, second = ahead_term[:, low:high], behind_term[:, low:high]
            if not narrow or end <= split:
                first = first + ahead[:, start:end]
            if not narrow:
                second = second + behind[:, start:end]
            elif start >= split:
                second = second + behind[:, start - split : end - split]
            ahead_out[:, start:end] = first
            behind_out[:, start:end] = second
        at += width


def last_kernel(count, outputs, *refs):
    terms, (ahead, behind), outs = refs[:count], refs[count : count + 2], refs[count + 2 :]
    totals, at = [], 0
    for term in terms:
        end = at + term.shape[1]
        totals.append(term[...].astype(WIDE) + ahead[:, at:end].astype(WIDE) + behind[:, at:end].astype(WIDE))
        at = end
    which, at = 0, 0
    for (width, turned), out in zip(outputs, outs):
        if at == totals[which].shape[1]:
            which, at = which + 1, 0
        value = totals[which][:, at : at + width]
        out[...] = value.T if turned else value
        at += width


def last(products, came, n, outputs):
    part = products[0].shape[0] // n
    step = part // 2 if part // 2 % LANES == 0 else part
    specs, shapes = [], []
    for width, turned in outputs:
        if turned:
            specs.append(pl.BlockSpec((width, step), lambda i: (0, i)))
            shapes.append(shaped((width, part), WIDE))
        else:
            specs.append(by_rows(step, width))
            shapes.append(shaped((part, width), WIDE))
    return tuple(
        pl.pallas_call(
            functools.partial(last_kernel, len(products), outputs),
            grid=(part // step,),
            in_specs=[by_rows(step, v.shape[1]) for v in (*products, *came)],
            out_specs=specs,
            out_shape=shapes,
            name="last",
        )(*products, *came)
    )


def grow(products, came, n, away, split):
    part = products[0].shape[0] // n
    wide = sum(v.shape[1] for v in products)
    narrow = away == n // 2 - 1
    step = part // 2
    came_specs = [by_rows(step, v.shape[1]) for v in came]

    def rows_at(offset):
        return [pl.BlockSpec((step, v.shape[1]), lambda i: (2 * offset + i, 0)) for v in products]

    return tuple(
        pl.pallas_call(
            functools.partial(grow_kernel, split, narrow, len(products)),
            grid=(2,),
            in_specs=rows_at(away) + rows_at(n - away) + came_specs,
            out_specs=[by_rows(step, wide)] * 2,
            out_shape=[shaped((part, wide), LOW)] * 2,
            name="grow",
        )(*products, *products, *came)
    )


def norm_back_kernel(hidden_ref, gain_ref, rest_ref, own_ref, near_ref, sent_ref, grads_ref, low_ref, terms_ref):
    hidden = hidden_ref[...].astype(WIDE)
    grad_normed = added((own_ref, near_ref, sent_ref))
    inverse = lax.rsqrt(jnp.mean(hidden * hidden, axis=-1, keepdims=True) + EPSILON)
    unit = hidden * inverse
    scaled = grad_normed * gain_ref[...]
    grads = rest_ref[...].astype(WIDE) + inverse * (
        scaled - unit * jnp.mean(scaled * unit, axis=-1, keepdims=True)
    )
    grads_ref[...] = grads
    low_ref[...] = grads.astype(LOW)

    @pl.when(pl.program_id(0) == 0)
    def _():
        terms_ref[...] = jnp.zeros_like(terms_ref)

    terms_ref[...] += jnp.sum(grad_normed * unit, axis=0, keepdims=True)


def norm_back(hidden, gain, rest, *parts):
    rows, depth = hidden.shape
    step = rows // 2
    return pl.pallas_call(
        norm_back_kernel,
        grid=(2,),
        in_specs=[by_rows(step, depth), whole(gain)] + [by_rows(step, depth)] * 4,
        out_specs=[by_rows(step, depth), by_rows(step, depth), pl.BlockSpec((1, depth), lambda i: (0, 0))],
        out_shape=[shaped((rows, depth), WIDE), shaped((rows, depth), LOW), shaped((1, depth), WIDE)],
        name="norm_back",
    )(hidden, gain, rest, *parts)


def shuffle_kernel(n, order_ref, *refs):
    out_ref = refs[-1]
    part = out_ref.shape[1] // n
    for s in range(n):
        at = pl.multiple_of(order_ref[s] * part, part)
        if len(refs) == 2:
            piece = refs[0][:, pl.ds(at, part)]
        else:
            piece = refs[0][:, pl.ds(at, part)]
            for ref in refs[1:-1]:
                piece = piece + ref[:, pl.ds(at, part)].astype(WIDE)
        out_ref[:, s * part : (s + 1) * part] = piece.astype(out_ref.dtype)


def shuffle(order, n, *values):
    rows, depth = values[0].shape
    part = depth // n
    if part % LANES:
        total = values[0]
        for v in values[1:]:
            total = total + v.astype(WIDE)
        pieces = [lax.dynamic_slice(total, (0, order[s] * part), (rows, part)) for s in range(n)]
        return jnp.concatenate(pieces, axis=1).astype(LOW)
    step = rows // 2
    return pl.pallas_call(
        functools.partial(shuffle_kernel, n),
        grid_spec=pltpu.PrefetchScalarGridSpec(
            num_scalar_prefetch=1,
            grid=(2,),
            in_specs=[pl.BlockSpec((step, depth), lambda i, order: (i, 0))] * len(values),
            out_specs=pl.BlockSpec((step, depth), lambda i, order: (i, 0)),
        ),
        out_shape=shaped((rows, depth), LOW),
        name="shuffle",
    )(order, *values)


def tables(segment_block):
    rows = segment_block.shape[0]
    places = jnp.arange(rows, dtype=jnp.int32)
    same = segment_block[:, None] == segment_block[None, :]
    first_index = jnp.min(jnp.where(same, places[None, :], rows), axis=1)
    offsets = (places - first_index).astype(WIDE)
    half = HEAD_DIM // 2
    frequencies = jnp.exp(jnp.arange(half, dtype=WIDE) * (-2.0 * math.log(ROPE_BASE) / HEAD_DIM))
    angles = offsets[:, None] * frequencies[None, :]
    cosine, sine = jnp.cos(angles), jnp.sin(angles)
    return jnp.concatenate([cosine] * 4, axis=1), jnp.concatenate([sine] * 4, axis=1)


def on_device(
    tokens, segments, gain_attn, w_query, w_key, w_value, w_out, gain_mlp, w_gate, w_up, w_down, cotangent
):
    n = lax.axis_size("dp")
    rows, depth = tokens.shape
    part = depth // n
    hops = n // 2
    me = lax.axis_index("dp")
    sources, offsets = [lax.dynamic_index_in_dim(jnp.asarray(t), me, keepdims=False) for t in ring_tables(n)]
    line = Line(jnp.zeros((8, LANES), WIDE))

    heads_wide, hidden_wide = w_query.shape[1], w_gate.shape[1]
    qkv_wide = heads_wide + w_key.shape[1] + w_value.shape[1]
    split = -(-hidden_wide // (2 * LANES)) * LANES
    attn_own = jnp.concatenate([w_query, w_key, w_value, w_out.T], axis=1).astype(LOW)
    gains = jnp.stack([gain_attn, gain_mlp]).astype(LOW)
    gains = jnp.pad(gains, ((0, 14), (0, attn_own.shape[1] - part)))
    attn = RingGather(line, jnp.concatenate([attn_own, gains], axis=0), n, qkv_wide, part)
    feedw = RingGather(line, jnp.concatenate([w_gate, w_up], axis=1).astype(LOW), n, hidden_wide, part)
    down = RingGather(line, w_down.T.astype(LOW), n, split, part)

    attn.start(1)
    own_tokens = shuffle(sources, n, tokens)
    marks = jnp.broadcast_to(segments.astype(LOW)[:, None], (rows, LANES))
    x = GroupGather(line, jnp.concatenate([own_tokens, marks], axis=1))
    attn.wait(1)
    attn.start(2)
    own_grads = line.run(lambda *v: shuffle(v[0], n, v[1]), sources, cotangent)
    for hop in range(2, hops - 1):
        attn.wait(hop)
        attn.start(hop + 1)
    attn.wait(hops - 1)
    attn.start(hops)
    token_rows = line.run(lambda *v: gathered(v, with_turned=False), *x.blocks())
    attn.wait(hops)
    feedw.start(1)
    y = GroupGather(line, own_grads)
    segment_blocks = token_rows[:, depth].astype(jnp.int32).reshape(-1, rows)
    column, row = segment_blocks.reshape(-1, 1), segment_blocks[:, None, :]
    cosine, sine = line.run(lambda v: jax.vmap(tables)(v), segment_blocks)
    cosine, sine = cosine.reshape(-1, LANES), sine.reshape(-1, LANES)
    gains = attn.extra(2).astype(WIDE)
    gain_one, gain_two = gains[0:1], gains[1:2]

    attn_panel = attn.panel()
    normed_turned, query, keyval, mixed, log_sums, *branch = line.run(
        lambda *v: attend(*v[:6], v[6:], heads_wide, rows),
        token_rows, gain_one, cosine, sine, column, row, *attn_panel,
    )
    feedw.wait(1)
    feedw.start(2)
    branch = GroupReduce(line, branch)
    grads_all, grads_turned = line.run(lambda *v: gathered(v), *y.blocks())
    branch.relay()
    for hop in range(2, hops - 1):
        feedw.wait(hop)
        feedw.start(hop + 1)
    hidden, normed_own = line.run(join, own_tokens, gain_two, *branch.terms())
    z = GroupGather(line, normed_own)
    feedw.wait(hops - 1)
    feedw.start(hops)
    normed_mlp, mlp_turned = line.run(lambda *v: gathered(v), *z.blocks())

    feedw.wait(hops)
    down.start(1)
    feed_panel = feedw.panel()
    activation, slope, silu = line.run(lambda a, *v: feed(a, v, hidden_wide), normed_mlp, *feed_panel)
    for hop in range(1, hops):
        down.wait(hop)
        down.start(hop + 1)
        if hop == 1:
            down_terms, *far = line.run(
                lambda a, b: product(a, b, n, (split, hidden_wide - split)), grads_turned, activation
            )
            r_down = RingReduce(line, [down_terms], far, n, split)
    r_down.start(1)
    down.wait(hops)
    down_panel = down.panel()
    r_down.wait(1)
    r_down.start(2)

    grad_feed = line.run(
        lambda a, b, c, *v: feed_back(a, b, c, v, split), grads_all, slope, silu, *down_panel
    )
    for hop in range(2, hops - 1):
        r_down.wait(hop)
        r_down.start(hop + 1)
    feed_terms, *far = line.run(
        lambda a, b: product(a, b, n, (hidden_wide, hidden_wide)), mlp_turned, grad_feed
    )
    r_feed = RingReduce(line, [feed_terms], far, n, hidden_wide)
    r_down.wait(hops - 1)
    r_down.start(hops)
    r_feed.start(1)
    grad_normed = line.run(lambda a, *v: spread(a, v, hidden_wide, rows), grad_feed, *feed_panel)
    r_down.wait(hops)
    r_feed.wait(1)
    r_feed.start(2)
    grad_normed = GroupReduce(line, grad_normed)
    grad_normed.relay()
    (grad_down,) = r_down.total([(hidden_wide, True)])
    layer_part = line.run(lambda a, *v: spread(a, v, split, rows), activation, *down_panel)
    for hop in range(2, hops - 1):
        r_feed.wait(hop)
        r_feed.start(hop + 1)
    grad_hidden, grad_branch, gain_mlp_terms = line.run(
        norm_back, hidden, gain_two, own_grads, *grad_normed.terms()
    )
    b = GroupGather(line, grad_branch)
    b_core = line.passed(line.send(b.own, "fsdp", CORE))
    extras = (query, keyval, log_sums, cosine, sine, column, row)

    def backward(blocks, groups, before=None):
        sizes = [len(group) for group in groups]
        flat = [v for group in groups for v in group]
        k = len(flat)

        def work(*v):
            split_groups = [v[sum(sizes[:i]) : sum(sizes[: i + 1])] for i in range(len(sizes))]
            last = len(v) if before is None else len(v) - 1
            return attend_back(
                blocks, split_groups, *v[k : k + 7], v[k + 7 : last], rows, None if before is None else v[-1]
            )

        return line.run(work, *flat, *extras, *attn_panel, *([] if before is None else [before]))

    grad_qkv, own, core = backward((0, 2), [[b.own], [b_core]])
    r_feed.wait(hops - 1)
    r_feed.start(hops)
    upper, lower = b.relay()
    branch_turned = line.run(
        lambda *v: gathered(v, with_all=False), b.own, b.pair, b_core, upper, lower
    )
    out_terms, out_far = line.run(lambda a, b: product(a, b, n, (heads_wide,)), branch_turned, mixed)
    grad_qkv, pair, diagonal = backward((1, 3), [[b.pair], [upper, lower]], grad_qkv)
    grad_input_sum = GroupReduce(line, [own, pair, core, diagonal])
    grad_input_sum.relay()
    attn_terms, attn_far = line.run(lambda a, b: product(a, b, n, (qkv_wide,)), normed_turned, grad_qkv)
    r_attn = RingReduce(line, [attn_terms, out_terms], [attn_far, out_far], n, qkv_wide)
    r_feed.wait(hops)
    r_attn.start(1)
    grad_w_gate, grad_w_up = r_feed.total([(hidden_wide, False)] * 2)
    layer_sum = GroupReduce(line, layer_part)
    r_attn.wait(1)
    r_attn.start(2)
    _, grad_tokens, gain_attn_terms = line.run(
        norm_back, own_tokens, gain_one, grad_hidden, *grad_input_sum.terms()
    )
    gain_terms = jnp.concatenate([gain_attn_terms, gain_mlp_terms], axis=0).reshape(2, n, part)
    gain_terms = jnp.take(gain_terms, offsets, axis=1).reshape(2, depth)

    def gain_step(axis, bit):
        nonlocal gain_terms
        size = lax.axis_size(axis)
        other = line.passed(line.send(gain_terms, axis, [(i, i ^ bit) for i in range(size)]))
        gain_terms = line.run(jnp.add, gain_terms, other)

    gain_step("fsdp", 1)
    gain_step("fsdp", 2)
    steps = [1 << i for i in range((n - 1).bit_length())]
    for hop in range(2, hops):
        r_attn.wait(hop)
        r_attn.start(hop + 1)
        if hop == 2:
            layer_sum.relay()
            grad_tokens = line.run(lambda at, v: shuffle(at, n, v), offsets, grad_tokens)
        if len(steps) > 1:
            gain_step("dp", steps.pop(0))
    while len(steps) > 1:
        gain_step("dp", steps.pop(0))
    layer_own = line.run(lambda at, *v: shuffle(at, n, *v), offsets, hidden, *layer_sum.terms())
    gain_step("dp", steps.pop(0))
    r_attn.wait(hops)
    key_wide, value_wide = w_key.shape[1], w_value.shape[1]
    grad_w_attn = r_attn.total(
        [(heads_wide, False), (key_wide, True), (value_wide, True), (heads_wide, True)]
    )
    gain_own = lax.dynamic_slice(gain_terms, (0, me * part), (2, part))

    return (
        layer_own,
        grad_tokens,
        gain_own[0],
        grad_w_attn[0],
        grad_w_attn[1].T,
        grad_w_attn[2].T,
        grad_w_attn[3],
        gain_own[1],
        grad_w_gate,
        grad_w_up,
        grad_down,
    )


def solution(mesh):
    placed = (
        P(("dp", "fsdp"), None),
        P(("dp", "fsdp")),
        P("dp"),
        P("dp", "fsdp"),
        P("dp", "fsdp"),
        P("dp", "fsdp"),
        P("fsdp", "dp"),
        P("dp"),
        P("dp", "fsdp"),
        P("dp", "fsdp"),
        P("fsdp", "dp"),
        P(("dp", "fsdp"), None),
    )
    return jax.shard_map(
        on_device,
        mesh=mesh,
        in_specs=placed,
        out_specs=(
            P(("dp", "fsdp"), None),
            P(("dp", "fsdp"), None),
            P("dp"),
            P("dp", "fsdp"),
            P("dp", "fsdp"),
            P("dp", "fsdp"),
            P("fsdp", "dp"),
            P("dp"),
            P("dp", "fsdp"),
            P("dp", "fsdp"),
            P("fsdp", "dp"),
        ),
        check_vma=False,
    )
```

```python
import functools
import math

import jax
import jax.numpy as jnp
import numpy as np
from jax import lax
from jax.experimental import pallas as pl
from jax.experimental.pallas import tpu as pltpu
from jax.sharding import PartitionSpec as P

HEAD_DIM = 64
EPSILON = 1e-05
ROPE_BASE = 10000.0
LOW = jnp.bfloat16
WIDE = jnp.float32
LANES = 128


def ring_order(n):
    return list(range(0, n, 2)) + list(range(n - 1, 0, -2))


def ring_perms(n):
    order = ring_order(n)
    forward = [(order[i], order[(i + 1) % n]) for i in range(n)]
    return forward, [(b, a) for a, b in forward]


def ring_tables(n):
    order = ring_order(n)
    place = [order.index(j) for j in range(n)]
    sources = [[order[(place[i] + s) % n] for s in range(n)] for i in range(n)]
    offsets = [[(place[j] - place[i]) % n for j in range(n)] for i in range(n)]
    return np.array(sources, np.int32), np.array(offsets, np.int32)


class Line:
    def __init__(self, token):
        self.token = token

    def after(self, *values):
        out = lax.optimization_barrier((*values, self.token))
        return out[0] if len(values) == 1 else out[:-1]

    def passed(self, *values):
        out = lax.optimization_barrier((*values, self.token))
        self.token = out[-1]
        return out[0] if len(values) == 1 else out[:-1]

    def run(self, work, *values):
        result = work(*lax.optimization_barrier((*values, self.token))[:-1])
        if not isinstance(result, (tuple, list)):
            return self.passed(result)
        out = lax.optimization_barrier((*result, self.token))
        self.token = out[-1]
        return out[:-1]

    def send(self, value, axis, pairs):
        return lax.ppermute(self.after(value), axis, pairs)


class RingGather:
    def __init__(self, line, own, n, split, part):
        self.line, self.n, self.split, self.part = line, n, split, part
        self.chunks = {0: own}
        self.flying = None

    def start(self, hop):
        n, pairs = self.n, ring_perms(self.n)
        ahead, behind = self.chunks[(n - hop + 1) % n], self.chunks[hop - 1]
        if hop == n // 2:
            ahead, behind = ahead[:, : self.split], behind[:, self.split :]
        self.flying = (self.line.send(ahead, "dp", pairs[0]), self.line.send(behind, "dp", pairs[1]))

    def wait(self, hop):
        ahead, behind = self.line.passed(*self.flying)
        if hop == self.n // 2:
            self.far = (ahead, behind)
        else:
            self.chunks[self.n - hop], self.chunks[hop] = ahead, behind

    def panel(self):
        n, part = self.n, self.part
        near = [self.chunks[s] for s in range(n) if s != n // 2]
        if part % LANES == 0:
            return [*near, *self.far]
        far = jnp.concatenate(self.far, axis=1)
        return [jnp.concatenate([v[:part] for v in (*near[: n // 2], far, *near[n // 2 :])], axis=0)]

    def extra(self, count):
        n, part = self.n, self.part
        chunks = [self.far[0] if s == n // 2 else self.chunks[s] for s in range(n)]
        return jnp.concatenate([c[part : part + count, :part] for c in chunks], axis=1)


class RingReduce:
    def __init__(self, line, products, far, n, split):
        self.line, self.products, self.far, self.n, self.split = line, products, far, n, split
        self.came = ()

    def start(self, hop):
        n, pairs = self.n, ring_perms(self.n)
        k = len(self.products)
        ahead, behind = self.far
        if hop > 1:
            away = n // 2 - hop + 1
            ahead, behind = self.line.run(
                lambda *v: grow(v[:k], v[k:], n, away, self.split), *self.products, *self.came
            )
        self.came = (self.line.send(ahead, "dp", pairs[0]), self.line.send(behind, "dp", pairs[1]))

    def wait(self, hop):
        self.came = self.line.passed(*self.came)

    def total(self, outputs):
        k = len(self.products)
        return self.line.run(lambda *v: last(v[:k], v[k:], self.n, outputs), *self.products, *self.came)


CORE = [(i, i ^ 1) for i in range(4)]
PAIR = [(i, i ^ 2) for i in range(4)]


class GroupGather:
    def __init__(self, line, own):
        self.line, self.own = line, own
        self.pair = line.send(own, "fsdp", PAIR)

    def relay(self):
        self.pair = self.line.passed(self.pair)
        half = self.pair.shape[0] // 2
        upper = self.line.send(self.pair[:half], "fsdp", CORE)
        lower = self.line.send(self.pair[half:], "fsdp", CORE)
        return self.line.passed(upper, lower)

    def blocks(self):
        core = self.line.send(self.own, "fsdp", CORE)
        upper, lower = self.relay()
        return [self.own, self.pair, self.line.passed(core), upper, lower]


class GroupReduce:
    def __init__(self, line, blocks):
        self.line, self.blocks = line, blocks
        half = blocks[3].shape[0] // 2
        self.upper = line.send(blocks[3][:half], "fsdp", CORE)
        self.lower = line.send(blocks[3][half:], "fsdp", CORE)

    def relay(self):
        far = self.line.passed(self.upper, self.lower)
        self.sent = self.line.send(self.line.run(plus, self.blocks[1], *far), "fsdp", PAIR)
        self.near = self.line.send(self.blocks[2], "fsdp", CORE)

    def terms(self):
        self.near, self.sent = self.line.passed(self.near, self.sent)
        return self.blocks[0], self.near, self.sent


def dot(a, b):
    return jnp.dot(a, b, preferred_element_type=WIDE)


def dot_rows(a, b):
    return lax.dot_general(a, b, (((1,), (1,)), ((), ())), preferred_element_type=WIDE)


def dot_firsts(a, b):
    return lax.dot_general(a, b, (((0,), (0,)), ((), ())), preferred_element_type=WIDE)


def by_rows(rows, width):
    return pl.BlockSpec((rows, width), lambda i: (i, 0))


def whole(value):
    zeros = (0,) * value.ndim
    return pl.BlockSpec(value.shape, lambda i: zeros, pipeline_mode=pl.Buffered(1))


def shaped(shape, kind):
    return jax.ShapeDtypeStruct(shape, kind)


def times_chunks(value, chunks):
    total, at = None, 0
    for chunk in chunks:
        size = chunk.shape[0]
        term = dot(value[:, at : at + size], chunk[...])
        total = term if total is None else total + term
        at += size
    return total


def into_chunks(out_ref, values, chunk_sets):
    at = 0
    for row in zip(*chunk_sets):
        size = row[0].shape[0]
        total = None
        for value, chunk in zip(values, row):
            term = dot_rows(value, chunk[...])
            total = term if total is None else total + term
        out_ref[:, at : at + size] = total.astype(out_ref.dtype)
        at += size


def pieces_of(panel, split, depth):
    if len(panel) == 1:
        chunk = panel[0]
        return [chunk.at[:, :split]], [chunk.at[:, split:]]
    part = depth // (len(panel) - 1)
    near, far = panel[:-2], [chunk.at[:part, :] for chunk in panel[-2:]]
    left = [chunk.at[:part, :split] for chunk in near]
    right = [chunk.at[:part, split:] for chunk in near]
    at = (len(near) + 1) // 2
    return left[:at] + [far[0]] + left[at:], right[:at] + [far[1]] + right[at:]


def into_block(out_refs, value_ref):
    for block, out_ref in enumerate(out_refs):

        @pl.when(pl.program_id(0) == block)
        def _(out_ref=out_ref):
            out_ref[...] = value_ref[...]


def turn(values, first_half):
    width = values.shape[-1]
    left = pltpu.roll(values, width - HEAD_DIM // 2, 1)
    right = pltpu.roll(values, HEAD_DIM // 2, 1)
    return jnp.where(first_half, -left, right)


def lane_ids(rows, width):
    return lax.broadcasted_iota(jnp.int32, (rows, width), 1)


def allowed_pairs(column, row):
    rows = column.shape[0]
    later = lax.broadcasted_iota(jnp.int32, (rows, rows), 0)
    earlier = lax.broadcasted_iota(jnp.int32, (rows, rows), 1)
    return (column == row) & (later >= earlier)


def normalize(hidden, gain):
    inverse = lax.rsqrt(jnp.mean(hidden * hidden, axis=-1, keepdims=True) + EPSILON)
    return (hidden * inverse * gain).astype(LOW)


def attention_forward(count, *refs):
    x_ref, gain_ref, cos_ref, sin_ref, col_ref, row_ref = refs[:6]
    turned_ref, q_ref, kv_ref, o_ref, lse_ref = refs[6 + count : 11 + count]
    branch_refs, qkv_ref, made_ref = refs[11 + count : 15 + count], refs[15 + count], refs[16 + count]
    q_chunks, o_chunks = pieces_of(refs[6 : 6 + count], qkv_ref.shape[1], gain_ref.shape[1])
    depth = gain_ref.shape[1]
    rows, width = q_ref.shape
    pairs = width // LANES
    normed = normalize(x_ref[:, :depth].astype(WIDE), gain_ref[...])
    turned_ref[...] = normed.T
    qkv_ref[...] = times_chunks(normed, q_chunks)
    cosine, sine = cos_ref[...], sin_ref[...]
    lanes = lane_ids(rows, LANES)
    even = lanes < HEAD_DIM
    first = (lanes % HEAD_DIM) < HEAD_DIM // 2
    keyval = qkv_ref[:, width:]
    keyval_rot = keyval * cosine + turn(keyval, first) * sine
    keyval = jnp.where(even, keyval_rot, keyval)
    kv_ref[...] = keyval.astype(LOW)
    other = pltpu.roll(keyval, HEAD_DIM, 1)
    keys = jnp.where(even, keyval, other).astype(LOW)
    vals = jnp.where(even, other, keyval).astype(LOW)
    allowed = allowed_pairs(col_ref[...], row_ref[0])
    log_sums = jnp.zeros((rows, LANES), WIDE)
    for pair in range(pairs):
        piece = qkv_ref[:, pair * LANES : (pair + 1) * LANES]
        piece = (piece * cosine + turn(piece, first) * sine).astype(LOW)
        q_ref[:, pair * LANES : (pair + 1) * LANES] = piece
        mixed = []
        for side in range(2):
            chosen = jnp.where(even if side == 0 else ~even, piece, jnp.zeros_like(piece))
            scores = dot_rows(chosen, keys) * (HEAD_DIM ** -0.5)
            scores = jnp.where(allowed, scores, -1e30)
            peak = jnp.max(scores, axis=1, keepdims=True)
            powers = jnp.exp(scores - peak)
            total = jnp.sum(powers, axis=1, keepdims=True)
            soft = (powers / total).astype(LOW)
            mixed.append(dot(soft, vals))
            log_sums = jnp.where(lanes == 2 * pair + side, peak + jnp.log(total), log_sums)
        o_ref[:, pair * LANES : (pair + 1) * LANES] = jnp.where(even, mixed[0], mixed[1]).astype(LOW)
    lse_ref[...] = log_sums
    into_chunks(made_ref, [o_ref[...]], [o_chunks])
    into_block(branch_refs, made_ref)


def fixed(rows, width):
    return pl.BlockSpec((rows, width), lambda i: (0, 0))


def attend(x, gain, cosine, sine, column, row, panel, width, rows):
    total, depth = x.shape[0], gain.shape[1]
    return pl.pallas_call(
        functools.partial(attention_forward, len(panel)),
        grid=(total // rows,),
        in_specs=[
            by_rows(rows, x.shape[1]),
            whole(gain),
            by_rows(rows, LANES),
            by_rows(rows, LANES),
            by_rows(rows, 1),
            pl.BlockSpec((1, 1, rows), lambda i: (i, 0, 0)),
        ]
        + [whole(v) for v in panel],
        out_specs=[
            pl.BlockSpec((depth, rows), lambda i: (0, i)),
            by_rows(rows, width),
            by_rows(rows, LANES),
            by_rows(rows, width),
            by_rows(rows, LANES),
        ]
        + [fixed(rows, depth)] * 4,
        out_shape=[
            shaped((depth, total), LOW),
            shaped((total, width), LOW),
            shaped((total, LANES), LOW),
            shaped((total, width), LOW),
            shaped((total, LANES), WIDE),
        ]
        + [shaped((rows, depth), LOW)] * 4,
        scratch_shapes=[pltpu.VMEM((rows, width + LANES), WIDE), pltpu.VMEM((rows, depth), LOW)],
        name="attend",
    )(x, gain, cosine, sine, column, row, *panel)


def attention_backward(sizes, count, *refs):
    dh_refs, refs = refs[: sum(sizes)], refs[sum(sizes) :]
    q_ref, kv_ref, lse_ref, cos_ref, sin_ref, col_ref, row_ref = refs[:7]
    panel, refs = refs[7 : 7 + count], refs[-len(sizes) - 3 :]
    grad_ref, part_refs, do_ref, made_ref = refs[0], refs[1:-2], refs[-2], refs[-1]
    q_chunks, o_chunks = pieces_of(panel, grad_ref.shape[1], dh_refs[0].shape[1])
    rows, width = q_ref.shape
    pairs = width // LANES
    scale = HEAD_DIM ** -0.5
    for block, size in enumerate(sizes):

        @pl.when(pl.program_id(0) == block)
        def _(mine=dh_refs[sum(sizes[:block]) : sum(sizes[: block + 1])]):
            at = 0
            for ref in mine:
                end = at + ref.shape[0]
                made_ref[at:end, :] = ref[...]
                at = end

    do_ref[...] = times_chunks(made_ref, o_chunks).astype(LOW)
    cosine, sine = cos_ref[...], sin_ref[...]
    lanes = lane_ids(rows, LANES)
    even = lanes < HEAD_DIM
    first = (lanes % HEAD_DIM) < HEAD_DIM // 2
    keyval = kv_ref[...].astype(WIDE)
    other = pltpu.roll(keyval, HEAD_DIM, 1)
    keys = jnp.where(even, keyval, other).astype(LOW)
    vals = jnp.where(even, other, keyval).astype(LOW)
    allowed = allowed_pairs(col_ref[...], row_ref[0])
    log_sums = lse_ref[...]

    def heads(pair, totals):
        grad_keys, grad_vals = totals
        span = pl.ds(pl.multiple_of(pair * LANES, LANES), LANES)
        piece = q_ref[:, span]
        grads = do_ref[:, span]
        turned = []
        for side in range(2):
            mine = even if side == 0 else ~even
            chosen = jnp.where(mine, piece, jnp.zeros_like(piece))
            chosen_grad = jnp.where(mine, grads, jnp.zeros_like(grads))
            own = jnp.where(lanes == 2 * pair + side, log_sums, 0.0)
            log_sum = jnp.sum(own, axis=1, keepdims=True)
            scores = jnp.where(allowed, dot_rows(chosen, keys) * scale, -1e30)
            soft = jnp.exp(scores - log_sum)
            grad_soft = dot_rows(chosen_grad, vals)
            delta = jnp.sum(soft * grad_soft, axis=1, keepdims=True)
            grad_scores = (soft * (grad_soft - delta)).astype(LOW)
            grad_vals = grad_vals + dot_firsts(soft.astype(LOW), chosen_grad)
            grad_keys = grad_keys + dot_firsts(grad_scores, chosen)
            turned.append(dot(grad_scores, keys))
        grad_q = jnp.where(even, turned[0], turned[1]) * scale
        grad_q = grad_q * cosine - turn(grad_q, first) * sine
        grad_ref[:, span] = grad_q.astype(LOW)
        return grad_keys, grad_vals

    nothing = jnp.zeros((rows, LANES), WIDE)
    grad_keys, grad_vals = lax.fori_loop(0, pairs, heads, (nothing, nothing))
    grad_keys = (grad_keys + pltpu.roll(grad_keys, HEAD_DIM, 1)) * scale
    grad_keys = grad_keys * cosine - turn(grad_keys, first) * sine
    grad_vals = grad_vals + pltpu.roll(grad_vals, HEAD_DIM, 1)
    grad_ref[:, width:] = jnp.where(even, grad_keys, grad_vals).astype(LOW)
    into_chunks(made_ref, [grad_ref[...]], [q_chunks])
    into_block(part_refs, made_ref)


def attend_back(blocks, groups, query, keyval, log_sums, cosine, sine, column, row, panel, rows, before=None):
    total, width = query.shape
    depth = groups[0][0].shape[1]
    first, step = blocks[0], blocks[1] - blocks[0]
    flat = [v for group in groups for v in group]

    def chosen(wide):
        return pl.BlockSpec((rows, wide), lambda i: (first + step * i, 0))

    operands = [*flat, query, keyval, log_sums, cosine, sine, column, row, *panel]
    in_specs = [whole(v) for v in flat]
    in_specs += [chosen(width), chosen(LANES), chosen(LANES), chosen(LANES), chosen(LANES), chosen(1)]
    in_specs += [pl.BlockSpec((1, 1, rows), lambda i: (first + step * i, 0, 0))]
    in_specs += [whole(v) for v in panel]
    aliases = {}
    if before is not None:
        aliases = {len(operands): 0}
        operands.append(before)
        in_specs.append(pl.BlockSpec(memory_space=pl.ANY))
    return pl.pallas_call(
        functools.partial(attention_backward, [len(group) for group in groups], len(panel)),
        grid=(len(groups),),
        in_specs=in_specs,
        out_specs=[chosen(width + LANES)] + [fixed(rows, depth)] * len(groups),
        out_shape=[shaped((total, width + LANES), LOW)] + [shaped((rows, depth), LOW)] * len(groups),
        scratch_shapes=[pltpu.VMEM((rows, width), LOW), pltpu.VMEM((rows, depth), LOW)],
        input_output_aliases=aliases,
        name="attend_back",
    )(*operands)


def plus_kernel(value_ref, upper_ref, lower_ref, out_ref):
    rows = upper_ref.shape[0]
    out_ref[:rows, :] = value_ref[:rows, :] + upper_ref[...]
    out_ref[rows:, :] = value_ref[rows:, :] + lower_ref[...]


def plus(value, upper, lower):
    rows, depth = value.shape
    step = depth // 2

    def columns(size):
        return pl.BlockSpec((size, step), lambda i: (0, i))

    return pl.pallas_call(
        plus_kernel,
        grid=(2,),
        in_specs=[columns(rows), columns(rows // 2), columns(rows // 2)],
        out_specs=columns(rows),
        out_shape=shaped(value.shape, value.dtype),
        name="plus",
    )(value, upper, lower)


def gathered_kernel(with_all, own, pair, core, upper, lower, *outs):
    outs, made_ref = outs[:-1], outs[-1]
    for block, refs in enumerate(((own,), (pair,), (core,), (upper, lower))):

        @pl.when(pl.program_id(0) == block)
        def _(refs=refs):
            at = 0
            for ref in refs:
                end = at + ref.shape[0]
                made_ref[at:end, :] = ref[...]
                at = end

    if with_all:
        outs[0][...] = made_ref[...]
    if not with_all or len(outs) == 2:
        outs[-1][...] = made_ref[...].T


def gathered(blocks, with_all=True, with_turned=True):
    rows, depth = blocks[0].shape
    out_specs, out_shape = [], []
    if with_all:
        out_specs.append(by_rows(rows, depth))
        out_shape.append(shaped((4 * rows, depth), LOW))
    if with_turned:
        out_specs.append(pl.BlockSpec((depth, rows), lambda i: (0, i)))
        out_shape.append(shaped((depth, 4 * rows), LOW))
    out = pl.pallas_call(
        functools.partial(gathered_kernel, with_all),
        grid=(4,),
        in_specs=[whole(v) for v in blocks],
        out_specs=out_specs,
        out_shape=out_shape,
        scratch_shapes=[pltpu.VMEM((rows, depth), LOW)],
        name="gathered",
    )(*blocks)
    return tuple(out) if len(out) == 2 else out[0]


def added(refs):
    total = refs[0][...].astype(WIDE)
    for ref in refs[1:]:
        total = total + ref[...].astype(WIDE)
    return total


def join_kernel(x_ref, own_ref, near_ref, sent_ref, gain_ref, hidden_ref, normed_ref):
    hidden = added((x_ref, own_ref, near_ref, sent_ref))
    hidden_ref[...] = hidden
    normed_ref[...] = normalize(hidden, gain_ref[...])


def join(x, gain, *parts):
    rows, depth = x.shape
    step = rows // 2
    return pl.pallas_call(
        join_kernel,
        grid=(2,),
        in_specs=[by_rows(step, depth)] * 4 + [whole(gain)],
        out_specs=[by_rows(step, depth)] * 2,
        out_shape=[shaped((rows, depth), WIDE), shaped((rows, depth), LOW)],
        name="join",
    )(x, *parts, gain)


def feed_kernel(count, *refs):
    x_ref = refs[0]
    act_ref, slope_ref, silu_ref = refs[1 + count :]
    g_chunks, u_chunks = pieces_of(refs[1 : 1 + count], act_ref.shape[1], x_ref.shape[1])
    gate = times_chunks(x_ref, g_chunks)
    up = times_chunks(x_ref, u_chunks)
    sigmoid = 1.0 / (1.0 + jnp.exp(-gate))
    silu = gate * sigmoid
    act_ref[...] = (silu * up).astype(LOW)
    silu_ref[...] = silu.astype(LOW)
    slope_ref[...] = (up * sigmoid * (1.0 + gate * (1.0 - sigmoid))).astype(LOW)


def feed(x, panel, wide):
    total, depth = x.shape
    step = total // 8
    return pl.pallas_call(
        functools.partial(feed_kernel, len(panel)),
        grid=(8,),
        in_specs=[by_rows(step, depth)] + [whole(v) for v in panel],
        out_specs=[by_rows(step, wide)] * 3,
        out_shape=[shaped((total, wide), LOW)] * 3,
        name="feed",
    )(x, *panel)


def feed_back_kernel(count, split, *refs):
    dy_ref, slope_ref, silu_ref = refs[:3]
    (out_ref,) = refs[3 + count :]
    wide = slope_ref.shape[1]
    at = 0
    for chunks in pieces_of(refs[3 : 3 + count], split, dy_ref.shape[1]):
        end = at + chunks[0].shape[1]
        grads = times_chunks(dy_ref, chunks)
        out_ref[:, at:end] = (grads * slope_ref[:, at:end].astype(WIDE)).astype(LOW)
        out_ref[:, wide + at : wide + end] = (grads * silu_ref[:, at:end].astype(WIDE)).astype(LOW)
        at = end


def feed_back(grads, slope, silu, panel, split):
    total, depth = grads.shape
    wide = slope.shape[1]
    step = total // 4
    return pl.pallas_call(
        functools.partial(feed_back_kernel, len(panel), split),
        grid=(4,),
        in_specs=[by_rows(step, depth), by_rows(step, wide), by_rows(step, wide)]
        + [whole(v) for v in panel],
        out_specs=by_rows(step, 2 * wide),
        out_shape=shaped((total, 2 * wide), LOW),
        name="feed_back",
    )(grads, slope, silu, *panel)


def spread_kernel(count, split, *refs):
    value, out_refs, made_ref = refs[0], refs[1 + count : -1], refs[-1]
    left, right = pieces_of(refs[1 : 1 + count], split, made_ref.shape[1])
    into_chunks(made_ref, [value[:, :split], value[:, split:]], [left, right])
    into_block(out_refs, made_ref)


def spread(value, panel, split, rows):
    total, wide = value.shape
    n = len(panel)
    depth = panel[0].shape[0] * max(1, n - 1)
    return pl.pallas_call(
        functools.partial(spread_kernel, n, split),
        grid=(4,),
        in_specs=[by_rows(rows, wide)] + [whole(c) for c in panel],
        out_specs=[fixed(rows, depth)] * 4,
        out_shape=[shaped((rows, depth), LOW)] * 4,
        scratch_shapes=[pltpu.VMEM((rows, depth), LOW)],
        name="spread",
    )(value, *panel)


def product_kernel(left, right, out, *far_refs):
    total = dot(left[...], right[...]).astype(LOW)
    out[...] = total

    @pl.when(pl.program_id(0) == pl.num_programs(0) // 2)
    def _():
        at = 0
        for far_ref in far_refs:
            part, width = far_ref.shape
            far_ref[...] = total[:part, at : at + width]
            at += width


def product(left, right, n, widths):
    depth, total = left.shape
    wide = right.shape[1]
    step = depth // 8
    return pl.pallas_call(
        product_kernel,
        grid=(8,),
        in_specs=[by_rows(step, total), whole(right)],
        out_specs=[by_rows(step, wide)] + [fixed(depth // n, width) for width in widths],
        out_shape=[shaped((depth, wide), LOW)] + [shaped((depth // n, width), LOW) for width in widths],
        name="product",
    )(left, right)


def grow_kernel(split, narrow, count, *refs):
    ahead_terms, behind_terms = refs[:count], refs[count : 2 * count]
    ahead, behind, ahead_out, behind_out = refs[2 * count :]
    at = 0
    for ahead_term, behind_term in zip(ahead_terms, behind_terms):
        width = ahead_term.shape[1]
        cuts = [0, split - at, width] if at < split < at + width else [0, width]
        for low, high in zip(cuts[:-1], cuts[1:]):
            start, end = at + low, at + high
            first, second = ahead_term[:, low:high], behind_term[:, low:high]
            if not narrow or end <= split:
                first = first + ahead[:, start:end]
            if not narrow:
                second = second + behind[:, start:end]
            elif start >= split:
                second = second + behind[:, start - split : end - split]
            ahead_out[:, start:end] = first
            behind_out[:, start:end] = second
        at += width


def last_kernel(count, outputs, *refs):
    terms, (ahead, behind), outs = refs[:count], refs[count : count + 2], refs[count + 2 :]
    totals, at = [], 0
    for term in terms:
        end = at + term.shape[1]
        totals.append(term[...].astype(WIDE) + ahead[:, at:end].astype(WIDE) + behind[:, at:end].astype(WIDE))
        at = end
    which, at = 0, 0
    for (width, turned), out in zip(outputs, outs):
        if at == totals[which].shape[1]:
            which, at = which + 1, 0
        value = totals[which][:, at : at + width]
        out[...] = value.T if turned else value
        at += width


def last(products, came, n, outputs):
    part = products[0].shape[0] // n
    step = part // 2 if part // 2 % LANES == 0 else part
    specs, shapes = [], []
    for width, turned in outputs:
        if turned:
            specs.append(pl.BlockSpec((width, step), lambda i: (0, i)))
            shapes.append(shaped((width, part), WIDE))
        else:
            specs.append(by_rows(step, width))
            shapes.append(shaped((part, width), WIDE))
    return tuple(
        pl.pallas_call(
            functools.partial(last_kernel, len(products), outputs),
            grid=(part // step,),
            in_specs=[by_rows(step, v.shape[1]) for v in (*products, *came)],
            out_specs=specs,
            out_shape=shapes,
            name="last",
        )(*products, *came)
    )


def grow(products, came, n, away, split):
    part = products[0].shape[0] // n
    wide = sum(v.shape[1] for v in products)
    narrow = away == n // 2 - 1
    step = part // 2
    came_specs = [by_rows(step, v.shape[1]) for v in came]

    def rows_at(offset):
        return [pl.BlockSpec((step, v.shape[1]), lambda i: (2 * offset + i, 0)) for v in products]

    return tuple(
        pl.pallas_call(
            functools.partial(grow_kernel, split, narrow, len(products)),
            grid=(2,),
            in_specs=rows_at(away) + rows_at(n - away) + came_specs,
            out_specs=[by_rows(step, wide)] * 2,
            out_shape=[shaped((part, wide), LOW)] * 2,
            name="grow",
        )(*products, *products, *came)
    )


def norm_back_kernel(hidden_ref, gain_ref, rest_ref, own_ref, near_ref, sent_ref, grads_ref, low_ref, terms_ref):
    hidden = hidden_ref[...].astype(WIDE)
    grad_normed = added((own_ref, near_ref, sent_ref))
    inverse = lax.rsqrt(jnp.mean(hidden * hidden, axis=-1, keepdims=True) + EPSILON)
    unit = hidden * inverse
    scaled = grad_normed * gain_ref[...]
    grads = rest_ref[...].astype(WIDE) + inverse * (
        scaled - unit * jnp.mean(scaled * unit, axis=-1, keepdims=True)
    )
    grads_ref[...] = grads
    low_ref[...] = grads.astype(LOW)

    @pl.when(pl.program_id(0) == 0)
    def _():
        terms_ref[...] = jnp.zeros_like(terms_ref)

    terms_ref[...] += jnp.sum(grad_normed * unit, axis=0, keepdims=True)


def norm_back(hidden, gain, rest, *parts):
    rows, depth = hidden.shape
    step = rows // 2
    return pl.pallas_call(
        norm_back_kernel,
        grid=(2,),
        in_specs=[by_rows(step, depth), whole(gain)] + [by_rows(step, depth)] * 4,
        out_specs=[by_rows(step, depth), by_rows(step, depth), pl.BlockSpec((1, depth), lambda i: (0, 0))],
        out_shape=[shaped((rows, depth), WIDE), shaped((rows, depth), LOW), shaped((1, depth), WIDE)],
        name="norm_back",
    )(hidden, gain, rest, *parts)


def shuffle_kernel(n, order_ref, *refs):
    out_ref = refs[-1]
    part = out_ref.shape[1] // n
    for s in range(n):
        at = pl.multiple_of(order_ref[s] * part, part)
        if len(refs) == 2:
            piece = refs[0][:, pl.ds(at, part)]
        else:
            piece = refs[0][:, pl.ds(at, part)]
            for ref in refs[1:-1]:
                piece = piece + ref[:, pl.ds(at, part)].astype(WIDE)
        out_ref[:, s * part : (s + 1) * part] = piece.astype(out_ref.dtype)


def shuffle(order, n, *values):
    rows, depth = values[0].shape
    part = depth // n
    if part % LANES:
        total = values[0]
        for v in values[1:]:
            total = total + v.astype(WIDE)
        pieces = [lax.dynamic_slice(total, (0, order[s] * part), (rows, part)) for s in range(n)]
        return jnp.concatenate(pieces, axis=1).astype(LOW)
    step = rows // 2
    return pl.pallas_call(
        functools.partial(shuffle_kernel, n),
        grid_spec=pltpu.PrefetchScalarGridSpec(
            num_scalar_prefetch=1,
            grid=(2,),
            in_specs=[pl.BlockSpec((step, depth), lambda i, order: (i, 0))] * len(values),
            out_specs=pl.BlockSpec((step, depth), lambda i, order: (i, 0)),
        ),
        out_shape=shaped((rows, depth), LOW),
        name="shuffle",
    )(order, *values)


UNIT = 64


def angle_table(rows):
    half = HEAD_DIM // 2
    frequencies = np.exp(np.arange(half, dtype=np.float32) * np.float32(-2.0 * math.log(ROPE_BASE) / HEAD_DIM))
    angles = np.arange(rows, dtype=np.float32)[:, None] * frequencies[None, :].astype(np.float32)
    both = np.concatenate([np.cos(angles), np.sin(angles)], axis=1).astype(np.float32)
    return both.reshape(rows // UNIT, UNIT, HEAD_DIM)


def tables(segment_blocks):
    blocks, rows = segment_blocks.shape
    units = rows // UNIT
    marks = segment_blocks[:, ::UNIT]
    places = jnp.arange(units, dtype=jnp.int32)
    same = marks[:, :, None] == marks[:, None, :]
    first = jnp.min(jnp.where(same, places[None, None, :], units), axis=2)
    chosen = (places[None, :] - first).reshape(-1)
    both = jnp.take(jnp.asarray(angle_table(rows)), chosen, axis=0, mode="clip").reshape(-1, HEAD_DIM)
    half = HEAD_DIM // 2
    cosine, sine = both[:, :half], both[:, half:]
    return jnp.concatenate([cosine] * 4, axis=1), jnp.concatenate([sine] * 4, axis=1)


def on_device(
    tokens, segments, gain_attn, w_query, w_key, w_value, w_out, gain_mlp, w_gate, w_up, w_down, cotangent
):
    n = lax.axis_size("dp")
    rows, depth = tokens.shape
    part = depth // n
    hops = n // 2
    me = lax.axis_index("dp")
    sources, offsets = [lax.dynamic_index_in_dim(jnp.asarray(t), me, keepdims=False) for t in ring_tables(n)]
    line = Line(jnp.zeros((8, LANES), WIDE))

    heads_wide, hidden_wide = w_query.shape[1], w_gate.shape[1]
    qkv_wide = heads_wide + w_key.shape[1] + w_value.shape[1]
    split = -(-hidden_wide // (2 * LANES)) * LANES
    attn_own = jnp.concatenate([w_query, w_key, w_value, w_out.T], axis=1).astype(LOW)
    gains = jnp.stack([gain_attn, gain_mlp]).astype(LOW)
    gains = jnp.pad(gains, ((0, 14), (0, attn_own.shape[1] - part)))
    attn = RingGather(line, jnp.concatenate([attn_own, gains], axis=0), n, qkv_wide, part)
    feedw = RingGather(line, jnp.concatenate([w_gate, w_up], axis=1).astype(LOW), n, hidden_wide, part)
    down = RingGather(line, w_down.T.astype(LOW), n, split, part)

    attn.start(1)
    own_tokens = shuffle(sources, n, tokens)
    marks = jnp.broadcast_to(segments.astype(LOW)[:, None], (rows, LANES))
    x = GroupGather(line, jnp.concatenate([own_tokens, marks], axis=1))
    attn.wait(1)
    attn.start(2)
    own_grads = line.run(lambda *v: shuffle(v[0], n, v[1]), sources, cotangent)
    for hop in range(2, hops - 1):
        attn.wait(hop)
        attn.start(hop + 1)
    attn.wait(hops - 1)
    attn.start(hops)
    token_rows = line.run(lambda *v: gathered(v, with_turned=False), *x.blocks())
    attn.wait(hops)
    feedw.start(1)
    y = GroupGather(line, own_grads)
    segment_blocks = token_rows[:, depth].astype(jnp.int32).reshape(-1, rows)
    column, row = segment_blocks.reshape(-1, 1), segment_blocks[:, None, :]
    cosine, sine = line.run(tables, segment_blocks)
    gains = attn.extra(2).astype(WIDE)
    gain_one, gain_two = gains[0:1], gains[1:2]

    attn_panel = attn.panel()
    normed_turned, query, keyval, mixed, log_sums, *branch = line.run(
        lambda *v: attend(*v[:6], v[6:], heads_wide, rows),
        token_rows, gain_one, cosine, sine, column, row, *attn_panel,
    )
    feedw.wait(1)
    feedw.start(2)
    branch = GroupReduce(line, branch)
    grads_all, grads_turned = line.run(lambda *v: gathered(v), *y.blocks())
    branch.relay()
    for hop in range(2, hops - 1):
        feedw.wait(hop)
        feedw.start(hop + 1)
    hidden, normed_own = line.run(join, own_tokens, gain_two, *branch.terms())
    z = GroupGather(line, normed_own)
    feedw.wait(hops - 1)
    feedw.start(hops)
    normed_mlp, mlp_turned = line.run(lambda *v: gathered(v), *z.blocks())

    feedw.wait(hops)
    down.start(1)
    feed_panel = feedw.panel()
    activation, slope, silu = line.run(lambda a, *v: feed(a, v, hidden_wide), normed_mlp, *feed_panel)
    for hop in range(1, hops):
        down.wait(hop)
        down.start(hop + 1)
        if hop == 1:
            down_terms, *far = line.run(
                lambda a, b: product(a, b, n, (split, hidden_wide - split)), grads_turned, activation
            )
            r_down = RingReduce(line, [down_terms], far, n, split)
    r_down.start(1)
    down.wait(hops)
    down_panel = down.panel()
    r_down.wait(1)
    r_down.start(2)

    grad_feed = line.run(
        lambda a, b, c, *v: feed_back(a, b, c, v, split), grads_all, slope, silu, *down_panel
    )
    for hop in range(2, hops - 1):
        r_down.wait(hop)
        r_down.start(hop + 1)
    feed_terms, *far = line.run(
        lambda a, b: product(a, b, n, (hidden_wide, hidden_wide)), mlp_turned, grad_feed
    )
    r_feed = RingReduce(line, [feed_terms], far, n, hidden_wide)
    r_down.wait(hops - 1)
    r_down.start(hops)
    r_feed.start(1)
    grad_normed = line.run(lambda a, *v: spread(a, v, hidden_wide, rows), grad_feed, *feed_panel)
    r_down.wait(hops)
    r_feed.wait(1)
    r_feed.start(2)
    grad_normed = GroupReduce(line, grad_normed)
    grad_normed.relay()
    (grad_down,) = r_down.total([(hidden_wide, True)])
    layer_part = line.run(lambda a, *v: spread(a, v, split, rows), activation, *down_panel)
    for hop in range(2, hops - 1):
        r_feed.wait(hop)
        r_feed.start(hop + 1)
    grad_hidden, grad_branch, gain_mlp_terms = line.run(
        norm_back, hidden, gain_two, own_grads, *grad_normed.terms()
    )
    b = GroupGather(line, grad_branch)
    b_core = line.passed(line.send(b.own, "fsdp", CORE))
    extras = (query, keyval, log_sums, cosine, sine, column, row)

    def backward(blocks, groups, before=None):
        sizes = [len(group) for group in groups]
        flat = [v for group in groups for v in group]
        k = len(flat)

        def work(*v):
            split_groups = [v[sum(sizes[:i]) : sum(sizes[: i + 1])] for i in range(len(sizes))]
            last = len(v) if before is None else len(v) - 1
            return attend_back(
                blocks, split_groups, *v[k : k + 7], v[k + 7 : last], rows, None if before is None else v[-1]
            )

        return line.run(work, *flat, *extras, *attn_panel, *([] if before is None else [before]))

    grad_qkv, own, core = backward((0, 2), [[b.own], [b_core]])
    r_feed.wait(hops - 1)
    r_feed.start(hops)
    upper, lower = b.relay()
    branch_turned = line.run(
        lambda *v: gathered(v, with_all=False), b.own, b.pair, b_core, upper, lower
    )
    out_terms, out_far = line.run(lambda a, b: product(a, b, n, (heads_wide,)), branch_turned, mixed)
    grad_qkv, pair, diagonal = backward((1, 3), [[b.pair], [upper, lower]], grad_qkv)
    grad_input_sum = GroupReduce(line, [own, pair, core, diagonal])
    grad_input_sum.relay()
    attn_terms, attn_far = line.run(lambda a, b: product(a, b, n, (qkv_wide,)), normed_turned, grad_qkv)
    r_attn = RingReduce(line, [attn_terms, out_terms], [attn_far, out_far], n, qkv_wide)
    r_feed.wait(hops)
    r_attn.start(1)
    grad_w_gate, grad_w_up = r_feed.total([(hidden_wide, False)] * 2)
    layer_sum = GroupReduce(line, layer_part)
    r_attn.wait(1)
    r_attn.start(2)
    _, grad_tokens, gain_attn_terms = line.run(
        norm_back, own_tokens, gain_one, grad_hidden, *grad_input_sum.terms()
    )
    gain_terms = jnp.concatenate([gain_attn_terms, gain_mlp_terms], axis=0).reshape(2, n, part)
    gain_terms = jnp.take(gain_terms, offsets, axis=1).reshape(2, depth)

    def gain_step(axis, bit):
        nonlocal gain_terms
        size = lax.axis_size(axis)
        other = line.passed(line.send(gain_terms, axis, [(i, i ^ bit) for i in range(size)]))
        gain_terms = line.run(jnp.add, gain_terms, other)

    gain_step("fsdp", 1)
    gain_step("fsdp", 2)
    layer_sum.relay()
    steps = [1 << i for i in range((n - 1).bit_length())]
    for hop in range(2, hops):
        r_attn.wait(hop)
        r_attn.start(hop + 1)
        if hop == 2:
            grad_tokens = line.run(lambda at, v: shuffle(at, n, v), offsets, grad_tokens)
        if hop < hops - 1 and len(steps) > 1:
            gain_step("dp", steps.pop(0))
    layer_own = line.run(lambda at, *v: shuffle(at, n, *v), offsets, hidden, *layer_sum.terms())
    while len(steps) > 1:
        gain_step("dp", steps.pop(0))
    flying = line.send(gain_terms, "dp", [(i, i ^ steps[0]) for i in range(n)])
    r_attn.wait(hops)
    key_wide, value_wide = w_key.shape[1], w_value.shape[1]
    grad_w_attn = r_attn.total(
        [(heads_wide, False), (key_wide, True), (value_wide, True), (heads_wide, True)]
    )
    gain_terms = gain_terms + line.passed(flying)
    gain_own = lax.dynamic_slice(gain_terms, (0, me * part), (2, part))

    return (
        layer_own,
        grad_tokens,
        gain_own[0],
        grad_w_attn[0],
        grad_w_attn[1].T,
        grad_w_attn[2].T,
        grad_w_attn[3],
        gain_own[1],
        grad_w_gate,
        grad_w_up,
        grad_down,
    )


def solution(mesh):
    placed = (
        P(("dp", "fsdp"), None),
        P(("dp", "fsdp")),
        P("dp"),
        P("dp", "fsdp"),
        P("dp", "fsdp"),
        P("dp", "fsdp"),
        P("fsdp", "dp"),
        P("dp"),
        P("dp", "fsdp"),
        P("dp", "fsdp"),
        P("fsdp", "dp"),
        P(("dp", "fsdp"), None),
    )
    return jax.shard_map(
        on_device,
        mesh=mesh,
        in_specs=placed,
        out_specs=(
            P(("dp", "fsdp"), None),
            P(("dp", "fsdp"), None),
            P("dp"),
            P("dp", "fsdp"),
            P("dp", "fsdp"),
            P("dp", "fsdp"),
            P("fsdp", "dp"),
            P("dp"),
            P("dp", "fsdp"),
            P("dp", "fsdp"),
            P("fsdp", "dp"),
        ),
        check_vma=False,
    )
```

```python
import functools
import math

import jax
import jax.numpy as jnp
import numpy as np
from jax import lax
from jax.experimental import pallas as pl
from jax.experimental.pallas import tpu as pltpu
from jax.sharding import PartitionSpec as P

HEAD_DIM = 64
EPSILON = 1e-05
ROPE_BASE = 10000.0
LOW = jnp.bfloat16
WIDE = jnp.float32
LANES = 128


def ring_order(n):
    return list(range(0, n, 2)) + list(range(n - 1, 0, -2))


def ring_perms(n):
    order = ring_order(n)
    forward = [(order[i], order[(i + 1) % n]) for i in range(n)]
    return forward, [(b, a) for a, b in forward]


def ring_tables(n):
    order = ring_order(n)
    place = [order.index(j) for j in range(n)]
    sources = [[order[(place[i] + s) % n] for s in range(n)] for i in range(n)]
    offsets = [[(place[j] - place[i]) % n for j in range(n)] for i in range(n)]
    return np.array(sources, np.int32), np.array(offsets, np.int32)


class Line:
    def __init__(self, token):
        self.token = token

    def after(self, *values):
        out = lax.optimization_barrier((*values, self.token))
        return out[0] if len(values) == 1 else out[:-1]

    def passed(self, *values):
        out = lax.optimization_barrier((*values, self.token))
        self.token = out[-1]
        return out[0] if len(values) == 1 else out[:-1]

    def run(self, work, *values):
        result = work(*lax.optimization_barrier((*values, self.token))[:-1])
        if not isinstance(result, (tuple, list)):
            return self.passed(result)
        out = lax.optimization_barrier((*result, self.token))
        self.token = out[-1]
        return out[:-1]

    def send(self, value, axis, pairs):
        return lax.ppermute(self.after(value), axis, pairs)


class RingGather:
    def __init__(self, line, own, n, split, part):
        self.line, self.n, self.split, self.part = line, n, split, part
        self.chunks = {0: own}
        self.flying = None

    def start(self, hop):
        n, pairs = self.n, ring_perms(self.n)
        ahead, behind = self.chunks[(n - hop + 1) % n], self.chunks[hop - 1]
        if hop == n // 2:
            ahead, behind = ahead[:, : self.split], behind[:, self.split :]
        self.flying = (self.line.send(ahead, "dp", pairs[0]), self.line.send(behind, "dp", pairs[1]))

    def wait(self, hop):
        ahead, behind = self.line.passed(*self.flying)
        if hop == self.n // 2:
            self.far = (ahead, behind)
        else:
            self.chunks[self.n - hop], self.chunks[hop] = ahead, behind

    def panel(self):
        n, part = self.n, self.part
        near = [self.chunks[s] for s in range(n) if s != n // 2]
        if part % LANES == 0:
            return [*near, *self.far]
        far = jnp.concatenate(self.far, axis=1)
        return [jnp.concatenate([v[:part] for v in (*near[: n // 2], far, *near[n // 2 :])], axis=0)]

    def extra(self, count):
        n, part = self.n, self.part
        chunks = [self.far[0] if s == n // 2 else self.chunks[s] for s in range(n)]
        return jnp.concatenate([c[part : part + count, :part] for c in chunks], axis=1)


class RingReduce:
    def __init__(self, line, products, far, n, split):
        self.line, self.products, self.far, self.n, self.split = line, products, far, n, split
        self.came = ()

    def start(self, hop):
        n, pairs = self.n, ring_perms(self.n)
        k = len(self.products)
        ahead, behind = self.far
        if hop > 1:
            away = n // 2 - hop + 1
            ahead, behind = self.line.run(
                lambda *v: grow(v[:k], v[k:], n, away, self.split), *self.products, *self.came
            )
        self.came = (self.line.send(ahead, "dp", pairs[0]), self.line.send(behind, "dp", pairs[1]))

    def wait(self, hop):
        self.came = self.line.passed(*self.came)

    def total(self, outputs):
        k = len(self.products)
        return self.line.run(lambda *v: last(v[:k], v[k:], self.n, outputs), *self.products, *self.came)


CORE = [(i, i ^ 1) for i in range(4)]
PAIR = [(i, i ^ 2) for i in range(4)]


class GroupGather:
    def __init__(self, line, own):
        self.line, self.own = line, own
        self.pair = line.send(own, "fsdp", PAIR)

    def relay(self):
        self.pair = self.line.passed(self.pair)
        half = self.pair.shape[0] // 2
        upper = self.line.send(self.pair[:half], "fsdp", CORE)
        lower = self.line.send(self.pair[half:], "fsdp", CORE)
        return self.line.passed(upper, lower)

    def blocks(self):
        core = self.line.send(self.own, "fsdp", CORE)
        upper, lower = self.relay()
        return [self.own, self.pair, self.line.passed(core), upper, lower]


class GroupReduce:
    def __init__(self, line, blocks):
        self.line, self.blocks = line, blocks
        half = blocks[3].shape[0] // 2
        self.upper = line.send(blocks[3][:half], "fsdp", CORE)
        self.lower = line.send(blocks[3][half:], "fsdp", CORE)

    def relay(self):
        far = self.line.passed(self.upper, self.lower)
        self.sent = self.line.send(self.line.run(plus, self.blocks[1], *far), "fsdp", PAIR)
        self.near = self.line.send(self.blocks[2], "fsdp", CORE)

    def terms(self):
        self.near, self.sent = self.line.passed(self.near, self.sent)
        return self.blocks[0], self.near, self.sent


def dot(a, b):
    return jnp.dot(a, b, preferred_element_type=WIDE)


def dot_rows(a, b):
    return lax.dot_general(a, b, (((1,), (1,)), ((), ())), preferred_element_type=WIDE)


def dot_firsts(a, b):
    return lax.dot_general(a, b, (((0,), (0,)), ((), ())), preferred_element_type=WIDE)


def by_rows(rows, width):
    return pl.BlockSpec((rows, width), lambda i: (i, 0))


def whole(value):
    zeros = (0,) * value.ndim
    return pl.BlockSpec(value.shape, lambda i: zeros, pipeline_mode=pl.Buffered(1))


def shaped(shape, kind):
    return jax.ShapeDtypeStruct(shape, kind)


def times_chunks(value, chunks):
    total, at = None, 0
    for chunk in chunks:
        size = chunk.shape[0]
        term = dot(value[:, at : at + size], chunk[...])
        total = term if total is None else total + term
        at += size
    return total


def into_chunks(out_ref, values, chunk_sets):
    at = 0
    for row in zip(*chunk_sets):
        size = row[0].shape[0]
        total = None
        for value, chunk in zip(values, row):
            term = dot_rows(value, chunk[...])
            total = term if total is None else total + term
        out_ref[:, at : at + size] = total.astype(out_ref.dtype)
        at += size


def pieces_of(panel, split, depth):
    if len(panel) == 1:
        chunk = panel[0]
        return [chunk.at[:, :split]], [chunk.at[:, split:]]
    part = depth // (len(panel) - 1)
    near, far = panel[:-2], [chunk.at[:part, :] for chunk in panel[-2:]]
    left = [chunk.at[:part, :split] for chunk in near]
    right = [chunk.at[:part, split:] for chunk in near]
    at = (len(near) + 1) // 2
    return left[:at] + [far[0]] + left[at:], right[:at] + [far[1]] + right[at:]


def into_block(out_refs, value_ref):
    for block, out_ref in enumerate(out_refs):

        @pl.when(pl.program_id(0) == block)
        def _(out_ref=out_ref):
            out_ref[...] = value_ref[...]


def turn(values, first_half):
    width = values.shape[-1]
    left = pltpu.roll(values, width - HEAD_DIM // 2, 1)
    right = pltpu.roll(values, HEAD_DIM // 2, 1)
    return jnp.where(first_half, -left, right)


def lane_ids(rows, width):
    return lax.broadcasted_iota(jnp.int32, (rows, width), 1)


def allowed_pairs(column, row):
    rows = column.shape[0]
    later = lax.broadcasted_iota(jnp.int32, (rows, rows), 0)
    earlier = lax.broadcasted_iota(jnp.int32, (rows, rows), 1)
    return (column == row) & (later >= earlier)


def normalize(hidden, gain):
    inverse = lax.rsqrt(jnp.mean(hidden * hidden, axis=-1, keepdims=True) + EPSILON)
    return (hidden * inverse * gain).astype(LOW)


def attention_forward(count, *refs):
    x_ref, gain_ref, cos_ref, sin_ref, col_ref, row_ref = refs[:6]
    turned_ref, q_ref, kv_ref, o_ref, lse_ref = refs[6 + count : 11 + count]
    branch_refs, qkv_ref, made_ref = refs[11 + count : 15 + count], refs[15 + count], refs[16 + count]
    q_chunks, o_chunks = pieces_of(refs[6 : 6 + count], qkv_ref.shape[1], gain_ref.shape[1])
    depth = gain_ref.shape[1]
    rows, width = q_ref.shape
    pairs = width // LANES
    normed = normalize(x_ref[:, :depth].astype(WIDE), gain_ref[...])
    turned_ref[...] = normed.T
    qkv_ref[...] = times_chunks(normed, q_chunks)
    cosine, sine = cos_ref[...], sin_ref[...]
    lanes = lane_ids(rows, LANES)
    even = lanes < HEAD_DIM
    first = (lanes % HEAD_DIM) < HEAD_DIM // 2
    keyval = qkv_ref[:, width:]
    keyval_rot = keyval * cosine + turn(keyval, first) * sine
    keyval = jnp.where(even, keyval_rot, keyval)
    kv_ref[...] = keyval.astype(LOW)
    other = pltpu.roll(keyval, HEAD_DIM, 1)
    keys = jnp.where(even, keyval, other).astype(LOW)
    vals = jnp.where(even, other, keyval).astype(LOW)
    allowed = allowed_pairs(col_ref[...], row_ref[0])
    log_sums = jnp.zeros((rows, LANES), WIDE)
    for pair in range(pairs):
        piece = qkv_ref[:, pair * LANES : (pair + 1) * LANES]
        piece = (piece * cosine + turn(piece, first) * sine).astype(LOW)
        q_ref[:, pair * LANES : (pair + 1) * LANES] = piece
        mixed = []
        for side in range(2):
            chosen = jnp.where(even if side == 0 else ~even, piece, jnp.zeros_like(piece))
            scores = dot_rows(chosen, keys) * (HEAD_DIM ** -0.5)
            scores = jnp.where(allowed, scores, -1e30)
            peak = jnp.max(scores, axis=1, keepdims=True)
            powers = jnp.exp(scores - peak)
            total = jnp.sum(powers, axis=1, keepdims=True)
            soft = (powers / total).astype(LOW)
            mixed.append(dot(soft, vals))
            log_sums = jnp.where(lanes == 2 * pair + side, peak + jnp.log(total), log_sums)
        o_ref[:, pair * LANES : (pair + 1) * LANES] = jnp.where(even, mixed[0], mixed[1]).astype(LOW)
    lse_ref[...] = log_sums
    into_chunks(made_ref, [o_ref[...]], [o_chunks])
    into_block(branch_refs, made_ref)


def fixed(rows, width):
    return pl.BlockSpec((rows, width), lambda i: (0, 0))


def attend(x, gain, cosine, sine, column, row, panel, width, rows):
    total, depth = x.shape[0], gain.shape[1]
    return pl.pallas_call(
        functools.partial(attention_forward, len(panel)),
        grid=(total // rows,),
        in_specs=[
            by_rows(rows, x.shape[1]),
            whole(gain),
            by_rows(rows, LANES),
            by_rows(rows, LANES),
            by_rows(rows, 1),
            pl.BlockSpec((1, 1, rows), lambda i: (i, 0, 0)),
        ]
        + [whole(v) for v in panel],
        out_specs=[
            pl.BlockSpec((depth, rows), lambda i: (0, i)),
            by_rows(rows, width),
            by_rows(rows, LANES),
            by_rows(rows, width),
            by_rows(rows, LANES),
        ]
        + [fixed(rows, depth)] * 4,
        out_shape=[
            shaped((depth, total), LOW),
            shaped((total, width), LOW),
            shaped((total, LANES), LOW),
            shaped((total, width), LOW),
            shaped((total, LANES), WIDE),
        ]
        + [shaped((rows, depth), LOW)] * 4,
        scratch_shapes=[pltpu.VMEM((rows, width + LANES), WIDE), pltpu.VMEM((rows, depth), LOW)],
        name="attend",
    )(x, gain, cosine, sine, column, row, *panel)


def attention_backward(sizes, count, *refs):
    dh_refs, refs = refs[: sum(sizes)], refs[sum(sizes) :]
    q_ref, kv_ref, lse_ref, cos_ref, sin_ref, col_ref, row_ref = refs[:7]
    panel, refs = refs[7 : 7 + count], refs[-len(sizes) - 3 :]
    grad_ref, part_refs, do_ref, made_ref = refs[0], refs[1:-2], refs[-2], refs[-1]
    q_chunks, o_chunks = pieces_of(panel, grad_ref.shape[1], dh_refs[0].shape[1])
    rows, width = q_ref.shape
    pairs = width // LANES
    scale = HEAD_DIM ** -0.5
    for block, size in enumerate(sizes):

        @pl.when(pl.program_id(0) == block)
        def _(mine=dh_refs[sum(sizes[:block]) : sum(sizes[: block + 1])]):
            at = 0
            for ref in mine:
                end = at + ref.shape[0]
                made_ref[at:end, :] = ref[...]
                at = end

    do_ref[...] = times_chunks(made_ref, o_chunks).astype(LOW)
    cosine, sine = cos_ref[...], sin_ref[...]
    lanes = lane_ids(rows, LANES)
    even = lanes < HEAD_DIM
    first = (lanes % HEAD_DIM) < HEAD_DIM // 2
    keyval = kv_ref[...].astype(WIDE)
    other = pltpu.roll(keyval, HEAD_DIM, 1)
    keys = jnp.where(even, keyval, other).astype(LOW)
    vals = jnp.where(even, other, keyval).astype(LOW)
    allowed = allowed_pairs(col_ref[...], row_ref[0])
    log_sums = lse_ref[...]

    def heads(pair, totals):
        grad_keys, grad_vals = totals
        span = pl.ds(pl.multiple_of(pair * LANES, LANES), LANES)
        piece = q_ref[:, span]
        grads = do_ref[:, span]
        turned = []
        for side in range(2):
            mine = even if side == 0 else ~even
            chosen = jnp.where(mine, piece, jnp.zeros_like(piece))
            chosen_grad = jnp.where(mine, grads, jnp.zeros_like(grads))
            own = jnp.where(lanes == 2 * pair + side, log_sums, 0.0)
            log_sum = jnp.sum(own, axis=1, keepdims=True)
            scores = jnp.where(allowed, dot_rows(chosen, keys) * scale, -1e30)
            soft = jnp.exp(scores - log_sum)
            grad_soft = dot_rows(chosen_grad, vals)
            delta = jnp.sum(soft * grad_soft, axis=1, keepdims=True)
            grad_scores = (soft * (grad_soft - delta)).astype(LOW)
            grad_vals = grad_vals + dot_firsts(soft.astype(LOW), chosen_grad)
            grad_keys = grad_keys + dot_firsts(grad_scores, chosen)
            turned.append(dot(grad_scores, keys))
        grad_q = jnp.where(even, turned[0], turned[1]) * scale
        grad_q = grad_q * cosine - turn(grad_q, first) * sine
        grad_ref[:, span] = grad_q.astype(LOW)
        return grad_keys, grad_vals

    nothing = jnp.zeros((rows, LANES), WIDE)
    grad_keys, grad_vals = lax.fori_loop(0, pairs, heads, (nothing, nothing))
    grad_keys = (grad_keys + pltpu.roll(grad_keys, HEAD_DIM, 1)) * scale
    grad_keys = grad_keys * cosine - turn(grad_keys, first) * sine
    grad_vals = grad_vals + pltpu.roll(grad_vals, HEAD_DIM, 1)
    grad_ref[:, width:] = jnp.where(even, grad_keys, grad_vals).astype(LOW)
    into_chunks(made_ref, [grad_ref[...]], [q_chunks])
    into_block(part_refs, made_ref)


def attend_back(blocks, groups, query, keyval, log_sums, cosine, sine, column, row, panel, rows, before=None):
    total, width = query.shape
    depth = groups[0][0].shape[1]
    first, step = blocks[0], blocks[1] - blocks[0]
    flat = [v for group in groups for v in group]

    def chosen(wide):
        return pl.BlockSpec((rows, wide), lambda i: (first + step * i, 0))

    operands = [*flat, query, keyval, log_sums, cosine, sine, column, row, *panel]
    in_specs = [whole(v) for v in flat]
    in_specs += [chosen(width), chosen(LANES), chosen(LANES), chosen(LANES), chosen(LANES), chosen(1)]
    in_specs += [pl.BlockSpec((1, 1, rows), lambda i: (first + step * i, 0, 0))]
    in_specs += [whole(v) for v in panel]
    aliases = {}
    if before is not None:
        aliases = {len(operands): 0}
        operands.append(before)
        in_specs.append(pl.BlockSpec(memory_space=pl.ANY))
    return pl.pallas_call(
        functools.partial(attention_backward, [len(group) for group in groups], len(panel)),
        grid=(len(groups),),
        in_specs=in_specs,
        out_specs=[chosen(width + LANES)] + [fixed(rows, depth)] * len(groups),
        out_shape=[shaped((total, width + LANES), LOW)] + [shaped((rows, depth), LOW)] * len(groups),
        scratch_shapes=[pltpu.VMEM((rows, width), LOW), pltpu.VMEM((rows, depth), LOW)],
        input_output_aliases=aliases,
        name="attend_back",
    )(*operands)


def plus_kernel(value_ref, upper_ref, lower_ref, out_ref):
    rows = upper_ref.shape[0]
    out_ref[:rows, :] = value_ref[:rows, :] + upper_ref[...]
    out_ref[rows:, :] = value_ref[rows:, :] + lower_ref[...]


def plus(value, upper, lower):
    rows, depth = value.shape
    step = depth // 2

    def columns(size):
        return pl.BlockSpec((size, step), lambda i: (0, i))

    return pl.pallas_call(
        plus_kernel,
        grid=(2,),
        in_specs=[columns(rows), columns(rows // 2), columns(rows // 2)],
        out_specs=columns(rows),
        out_shape=shaped(value.shape, value.dtype),
        name="plus",
    )(value, upper, lower)


def gathered_kernel(with_all, own, pair, core, upper, lower, *outs):
    outs, made_ref = outs[:-1], outs[-1]
    for block, refs in enumerate(((own,), (pair,), (core,), (upper, lower))):

        @pl.when(pl.program_id(0) == block)
        def _(refs=refs):
            at = 0
            for ref in refs:
                end = at + ref.shape[0]
                made_ref[at:end, :] = ref[...]
                at = end

    if with_all:
        outs[0][...] = made_ref[...]
    if not with_all or len(outs) == 2:
        outs[-1][...] = made_ref[...].T


def gathered(blocks, with_all=True, with_turned=True):
    rows, depth = blocks[0].shape
    out_specs, out_shape = [], []
    if with_all:
        out_specs.append(by_rows(rows, depth))
        out_shape.append(shaped((4 * rows, depth), LOW))
    if with_turned:
        out_specs.append(pl.BlockSpec((depth, rows), lambda i: (0, i)))
        out_shape.append(shaped((depth, 4 * rows), LOW))
    out = pl.pallas_call(
        functools.partial(gathered_kernel, with_all),
        grid=(4,),
        in_specs=[whole(v) for v in blocks],
        out_specs=out_specs,
        out_shape=out_shape,
        scratch_shapes=[pltpu.VMEM((rows, depth), LOW)],
        name="gathered",
    )(*blocks)
    return tuple(out) if len(out) == 2 else out[0]


def added(refs):
    total = refs[0][...].astype(WIDE)
    for ref in refs[1:]:
        total = total + ref[...].astype(WIDE)
    return total


def join_kernel(x_ref, own_ref, near_ref, sent_ref, gain_ref, hidden_ref, normed_ref):
    hidden = added((x_ref, own_ref, near_ref, sent_ref))
    hidden_ref[...] = hidden
    normed_ref[...] = normalize(hidden, gain_ref[...])


def join(x, gain, *parts):
    rows, depth = x.shape
    step = rows // 2
    return pl.pallas_call(
        join_kernel,
        grid=(2,),
        in_specs=[by_rows(step, depth)] * 4 + [whole(gain)],
        out_specs=[by_rows(step, depth)] * 2,
        out_shape=[shaped((rows, depth), WIDE), shaped((rows, depth), LOW)],
        name="join",
    )(x, *parts, gain)


def feed_kernel(count, *refs):
    x_ref = refs[0]
    act_ref, slope_ref, silu_ref = refs[1 + count :]
    g_chunks, u_chunks = pieces_of(refs[1 : 1 + count], act_ref.shape[1], x_ref.shape[1])
    gate = times_chunks(x_ref, g_chunks)
    up = times_chunks(x_ref, u_chunks)
    sigmoid = 1.0 / (1.0 + jnp.exp(-gate))
    silu = gate * sigmoid
    act_ref[...] = (silu * up).astype(LOW)
    silu_ref[...] = silu.astype(LOW)
    slope_ref[...] = (up * sigmoid * (1.0 + gate * (1.0 - sigmoid))).astype(LOW)


def feed(x, panel, wide):
    total, depth = x.shape
    step = total // 8
    return pl.pallas_call(
        functools.partial(feed_kernel, len(panel)),
        grid=(8,),
        in_specs=[by_rows(step, depth)] + [whole(v) for v in panel],
        out_specs=[by_rows(step, wide)] * 3,
        out_shape=[shaped((total, wide), LOW)] * 3,
        name="feed",
    )(x, *panel)


def feed_back_kernel(count, split, *refs):
    dy_ref, slope_ref, silu_ref = refs[:3]
    (out_ref,) = refs[3 + count :]
    wide = slope_ref.shape[1]
    at = 0
    for chunks in pieces_of(refs[3 : 3 + count], split, dy_ref.shape[1]):
        end = at + chunks[0].shape[1]
        grads = times_chunks(dy_ref, chunks)
        out_ref[:, at:end] = (grads * slope_ref[:, at:end].astype(WIDE)).astype(LOW)
        out_ref[:, wide + at : wide + end] = (grads * silu_ref[:, at:end].astype(WIDE)).astype(LOW)
        at = end


def feed_back(grads, slope, silu, panel, split):
    total, depth = grads.shape
    wide = slope.shape[1]
    step = total // 4
    return pl.pallas_call(
        functools.partial(feed_back_kernel, len(panel), split),
        grid=(4,),
        in_specs=[by_rows(step, depth), by_rows(step, wide), by_rows(step, wide)]
        + [whole(v) for v in panel],
        out_specs=by_rows(step, 2 * wide),
        out_shape=shaped((total, 2 * wide), LOW),
        name="feed_back",
    )(grads, slope, silu, *panel)


def spread_kernel(count, split, *refs):
    value, out_refs, made_ref = refs[0], refs[1 + count : -1], refs[-1]
    left, right = pieces_of(refs[1 : 1 + count], split, made_ref.shape[1])
    into_chunks(made_ref, [value[:, :split], value[:, split:]], [left, right])
    into_block(out_refs, made_ref)


def spread(value, panel, split, rows):
    total, wide = value.shape
    n = len(panel)
    depth = panel[0].shape[0] * max(1, n - 1)
    return pl.pallas_call(
        functools.partial(spread_kernel, n, split),
        grid=(4,),
        in_specs=[by_rows(rows, wide)] + [whole(c) for c in panel],
        out_specs=[fixed(rows, depth)] * 4,
        out_shape=[shaped((rows, depth), LOW)] * 4,
        scratch_shapes=[pltpu.VMEM((rows, depth), LOW)],
        name="spread",
    )(value, *panel)


def product_kernel(left, right, out, *far_refs):
    total = dot(left[...], right[...]).astype(LOW)
    out[...] = total

    @pl.when(pl.program_id(0) == pl.num_programs(0) // 2)
    def _():
        at = 0
        for far_ref in far_refs:
            part, width = far_ref.shape
            far_ref[...] = total[:part, at : at + width]
            at += width


def product(left, right, n, widths):
    depth, total = left.shape
    wide = right.shape[1]
    step = depth // 8
    return pl.pallas_call(
        product_kernel,
        grid=(8,),
        in_specs=[by_rows(step, total), whole(right)],
        out_specs=[by_rows(step, wide)] + [fixed(depth // n, width) for width in widths],
        out_shape=[shaped((depth, wide), LOW)] + [shaped((depth // n, width), LOW) for width in widths],
        name="product",
    )(left, right)


def grow_kernel(split, narrow, count, *refs):
    ahead_terms, behind_terms = refs[:count], refs[count : 2 * count]
    ahead, behind, ahead_out, behind_out = refs[2 * count :]
    step = ahead_out.shape[0]
    rows = pl.ds(pl.multiple_of(pl.program_id(0) * step, step), step)
    ahead, behind = ahead.at[rows, :], behind.at[rows, :]
    at = 0
    for ahead_term, behind_term in zip(ahead_terms, behind_terms):
        width = ahead_term.shape[1]
        cuts = [0, split - at, width] if at < split < at + width else [0, width]
        for low, high in zip(cuts[:-1], cuts[1:]):
            start, end = at + low, at + high
            first, second = ahead_term[:, low:high], behind_term[:, low:high]
            if not narrow or end <= split:
                first = first + ahead[:, start:end]
            if not narrow:
                second = second + behind[:, start:end]
            elif start >= split:
                second = second + behind[:, start - split : end - split]
            ahead_out[:, start:end] = first
            behind_out[:, start:end] = second
        at += width


def last_kernel(count, outputs, *refs):
    terms, (ahead, behind), outs = refs[:count], refs[count : count + 2], refs[count + 2 :]
    totals, at = [], 0
    for term in terms:
        end = at + term.shape[1]
        totals.append(term[...].astype(WIDE) + ahead[:, at:end].astype(WIDE) + behind[:, at:end].astype(WIDE))
        at = end
    which, at = 0, 0
    for (width, turned), out in zip(outputs, outs):
        if at == totals[which].shape[1]:
            which, at = which + 1, 0
        value = totals[which][:, at : at + width]
        out[...] = value.T if turned else value
        at += width


def last(products, came, n, outputs):
    part = products[0].shape[0] // n
    step = part // 2 if part // 2 % LANES == 0 else part
    specs, shapes = [], []
    for width, turned in outputs:
        if turned:
            specs.append(pl.BlockSpec((width, step), lambda i: (0, i)))
            shapes.append(shaped((width, part), WIDE))
        else:
            specs.append(by_rows(step, width))
            shapes.append(shaped((part, width), WIDE))
    return tuple(
        pl.pallas_call(
            functools.partial(last_kernel, len(products), outputs),
            grid=(part // step,),
            in_specs=[by_rows(step, v.shape[1]) for v in (*products, *came)],
            out_specs=specs,
            out_shape=shapes,
            name="last",
        )(*products, *came)
    )


def grow(products, came, n, away, split):
    part = products[0].shape[0] // n
    wide = sum(v.shape[1] for v in products)
    narrow = away == n // 2 - 1
    step = part // 2
    came_specs = [pl.BlockSpec(memory_space=pltpu.VMEM) for _ in came]

    def rows_at(offset):
        return [pl.BlockSpec((step, v.shape[1]), lambda i: (2 * offset + i, 0)) for v in products]

    return tuple(
        pl.pallas_call(
            functools.partial(grow_kernel, split, narrow, len(products)),
            grid=(2,),
            in_specs=rows_at(away) + rows_at(n - away) + came_specs,
            out_specs=[by_rows(step, wide)] * 2,
            out_shape=[shaped((part, wide), LOW)] * 2,
            name="grow",
        )(*products, *products, *came)
    )


def norm_back_kernel(hidden_ref, gain_ref, rest_ref, own_ref, near_ref, sent_ref, grads_ref, low_ref, terms_ref):
    hidden = hidden_ref[...].astype(WIDE)
    grad_normed = added((own_ref, near_ref, sent_ref))
    inverse = lax.rsqrt(jnp.mean(hidden * hidden, axis=-1, keepdims=True) + EPSILON)
    unit = hidden * inverse
    scaled = grad_normed * gain_ref[...]
    grads = rest_ref[...].astype(WIDE) + inverse * (
        scaled - unit * jnp.mean(scaled * unit, axis=-1, keepdims=True)
    )
    grads_ref[...] = grads
    low_ref[...] = grads.astype(LOW)

    @pl.when(pl.program_id(0) == 0)
    def _():
        terms_ref[...] = jnp.zeros_like(terms_ref)

    terms_ref[...] += jnp.sum(grad_normed * unit, axis=0, keepdims=True)


def norm_back(hidden, gain, rest, *parts):
    rows, depth = hidden.shape
    step = rows // 2
    return pl.pallas_call(
        norm_back_kernel,
        grid=(2,),
        in_specs=[by_rows(step, depth), whole(gain)] + [by_rows(step, depth)] * 4,
        out_specs=[by_rows(step, depth), by_rows(step, depth), pl.BlockSpec((1, depth), lambda i: (0, 0))],
        out_shape=[shaped((rows, depth), WIDE), shaped((rows, depth), LOW), shaped((1, depth), WIDE)],
        name="norm_back",
    )(hidden, gain, rest, *parts)


def shuffle_kernel(n, order_ref, *refs):
    out_ref = refs[-1]
    part = out_ref.shape[1] // n
    for s in range(n):
        at = pl.multiple_of(order_ref[s] * part, part)
        if len(refs) == 2:
            piece = refs[0][:, pl.ds(at, part)]
        else:
            piece = refs[0][:, pl.ds(at, part)]
            for ref in refs[1:-1]:
                piece = piece + ref[:, pl.ds(at, part)].astype(WIDE)
        out_ref[:, s * part : (s + 1) * part] = piece.astype(out_ref.dtype)


def shuffle(order, n, *values):
    rows, depth = values[0].shape
    part = depth // n
    if part % LANES:
        total = values[0]
        for v in values[1:]:
            total = total + v.astype(WIDE)
        pieces = [lax.dynamic_slice(total, (0, order[s] * part), (rows, part)) for s in range(n)]
        return jnp.concatenate(pieces, axis=1).astype(LOW)
    step = rows // 2
    return pl.pallas_call(
        functools.partial(shuffle_kernel, n),
        grid_spec=pltpu.PrefetchScalarGridSpec(
            num_scalar_prefetch=1,
            grid=(2,),
            in_specs=[pl.BlockSpec((step, depth), lambda i, order: (i, 0))] * len(values),
            out_specs=pl.BlockSpec((step, depth), lambda i, order: (i, 0)),
        ),
        out_shape=shaped((rows, depth), LOW),
        name="shuffle",
    )(order, *values)


UNIT = 64


def angle_table(rows):
    half = HEAD_DIM // 2
    frequencies = np.exp(np.arange(half, dtype=np.float32) * np.float32(-2.0 * math.log(ROPE_BASE) / HEAD_DIM))
    angles = np.arange(rows, dtype=np.float32)[:, None] * frequencies[None, :].astype(np.float32)
    both = np.concatenate([np.cos(angles), np.sin(angles)], axis=1).astype(np.float32)
    return both.reshape(rows // UNIT, UNIT, HEAD_DIM)


def tables(segment_blocks):
    blocks, rows = segment_blocks.shape
    units = rows // UNIT
    marks = segment_blocks[:, ::UNIT]
    places = jnp.arange(units, dtype=jnp.int32)
    same = marks[:, :, None] == marks[:, None, :]
    first = jnp.min(jnp.where(same, places[None, None, :], units), axis=2)
    chosen = (places[None, :] - first).reshape(-1)
    both = jnp.take(jnp.asarray(angle_table(rows)), chosen, axis=0, mode="clip").reshape(-1, HEAD_DIM)
    half = HEAD_DIM // 2
    cosine, sine = both[:, :half], both[:, half:]
    return jnp.concatenate([cosine] * 4, axis=1), jnp.concatenate([sine] * 4, axis=1)


def on_device(
    tokens, segments, gain_attn, w_query, w_key, w_value, w_out, gain_mlp, w_gate, w_up, w_down, cotangent
):
    n = lax.axis_size("dp")
    rows, depth = tokens.shape
    part = depth // n
    hops = n // 2
    me = lax.axis_index("dp")
    sources, offsets = [lax.dynamic_index_in_dim(jnp.asarray(t), me, keepdims=False) for t in ring_tables(n)]
    line = Line(jnp.zeros((8, LANES), WIDE))

    heads_wide, hidden_wide = w_query.shape[1], w_gate.shape[1]
    qkv_wide = heads_wide + w_key.shape[1] + w_value.shape[1]
    split = -(-hidden_wide // (2 * LANES)) * LANES
    attn_own = jnp.concatenate([w_query, w_key, w_value, w_out.T], axis=1).astype(LOW)
    gains = jnp.stack([gain_attn, gain_mlp]).astype(LOW)
    gains = jnp.pad(gains, ((0, 14), (0, attn_own.shape[1] - part)))
    attn = RingGather(line, jnp.concatenate([attn_own, gains], axis=0), n, qkv_wide, part)
    feedw = RingGather(line, jnp.concatenate([w_gate, w_up], axis=1).astype(LOW), n, hidden_wide, part)
    down = RingGather(line, w_down.T.astype(LOW), n, split, part)

    attn.start(1)
    own_tokens = shuffle(sources, n, tokens)
    marks = jnp.broadcast_to(segments.astype(LOW)[:, None], (rows, LANES))
    x = GroupGather(line, jnp.concatenate([own_tokens, marks], axis=1))
    attn.wait(1)
    attn.start(2)
    own_grads = line.run(lambda *v: shuffle(v[0], n, v[1]), sources, cotangent)
    for hop in range(2, hops - 1):
        attn.wait(hop)
        attn.start(hop + 1)
    attn.wait(hops - 1)
    attn.start(hops)
    token_rows = line.run(lambda *v: gathered(v, with_turned=False), *x.blocks())
    attn.wait(hops)
    feedw.start(1)
    y = GroupGather(line, own_grads)
    segment_blocks = token_rows[:, depth].astype(jnp.int32).reshape(-1, rows)
    column, row = segment_blocks.reshape(-1, 1), segment_blocks[:, None, :]
    cosine, sine = line.run(tables, segment_blocks)
    gains = attn.extra(2).astype(WIDE)
    gain_one, gain_two = gains[0:1], gains[1:2]

    attn_panel = attn.panel()
    normed_turned, query, keyval, mixed, log_sums, *branch = line.run(
        lambda *v: attend(*v[:6], v[6:], heads_wide, rows),
        token_rows, gain_one, cosine, sine, column, row, *attn_panel,
    )
    feedw.wait(1)
    feedw.start(2)
    branch = GroupReduce(line, branch)
    grads_all, grads_turned = line.run(lambda *v: gathered(v), *y.blocks())
    branch.relay()
    for hop in range(2, hops - 1):
        feedw.wait(hop)
        feedw.start(hop + 1)
    hidden, normed_own = line.run(join, own_tokens, gain_two, *branch.terms())
    z = GroupGather(line, normed_own)
    feedw.wait(hops - 1)
    feedw.start(hops)
    normed_mlp, mlp_turned = line.run(lambda *v: gathered(v), *z.blocks())

    feedw.wait(hops)
    down.start(1)
    feed_panel = feedw.panel()
    activation, slope, silu = line.run(lambda a, *v: feed(a, v, hidden_wide), normed_mlp, *feed_panel)
    for hop in range(1, hops):
        down.wait(hop)
        down.start(hop + 1)
        if hop == 1:
            down_terms, *far = line.run(
                lambda a, b: product(a, b, n, (split, hidden_wide - split)), grads_turned, activation
            )
            r_down = RingReduce(line, [down_terms], far, n, split)
    r_down.start(1)
    down.wait(hops)
    down_panel = down.panel()
    r_down.wait(1)
    r_down.start(2)

    grad_feed = line.run(
        lambda a, b, c, *v: feed_back(a, b, c, v, split), grads_all, slope, silu, *down_panel
    )
    for hop in range(2, hops - 1):
        r_down.wait(hop)
        r_down.start(hop + 1)
    feed_terms, *far = line.run(
        lambda a, b: product(a, b, n, (hidden_wide, hidden_wide)), mlp_turned, grad_feed
    )
    r_feed = RingReduce(line, [feed_terms], far, n, hidden_wide)
    r_down.wait(hops - 1)
    r_down.start(hops)
    r_feed.start(1)
    grad_normed = line.run(lambda a, *v: spread(a, v, hidden_wide, rows), grad_feed, *feed_panel)
    r_down.wait(hops)
    r_feed.wait(1)
    r_feed.start(2)
    grad_normed = GroupReduce(line, grad_normed)
    grad_normed.relay()
    (grad_down,) = r_down.total([(hidden_wide, True)])
    layer_part = line.run(lambda a, *v: spread(a, v, split, rows), activation, *down_panel)
    for hop in range(2, hops - 1):
        r_feed.wait(hop)
        r_feed.start(hop + 1)
    grad_hidden, grad_branch, gain_mlp_terms = line.run(
        norm_back, hidden, gain_two, own_grads, *grad_normed.terms()
    )
    b = GroupGather(line, grad_branch)
    b_core = line.passed(line.send(b.own, "fsdp", CORE))
    extras = (query, keyval, log_sums, cosine, sine, column, row)

    def backward(blocks, groups, before=None):
        sizes = [len(group) for group in groups]
        flat = [v for group in groups for v in group]
        k = len(flat)

        def work(*v):
            split_groups = [v[sum(sizes[:i]) : sum(sizes[: i + 1])] for i in range(len(sizes))]
            last = len(v) if before is None else len(v) - 1
            return attend_back(
                blocks, split_groups, *v[k : k + 7], v[k + 7 : last], rows, None if before is None else v[-1]
            )

        return line.run(work, *flat, *extras, *attn_panel, *([] if before is None else [before]))

    grad_qkv, own, core = backward((0, 2), [[b.own], [b_core]])
    r_feed.wait(hops - 1)
    r_feed.start(hops)
    upper, lower = b.relay()
    branch_turned = line.run(
        lambda *v: gathered(v, with_all=False), b.own, b.pair, b_core, upper, lower
    )
    out_terms, out_far = line.run(lambda a, b: product(a, b, n, (heads_wide,)), branch_turned, mixed)
    grad_qkv, pair, diagonal = backward((1, 3), [[b.pair], [upper, lower]], grad_qkv)
    grad_input_sum = GroupReduce(line, [own, pair, core, diagonal])
    grad_input_sum.relay()
    attn_terms, attn_far = line.run(lambda a, b: product(a, b, n, (qkv_wide,)), normed_turned, grad_qkv)
    r_attn = RingReduce(line, [attn_terms, out_terms], [attn_far, out_far], n, qkv_wide)
    r_feed.wait(hops)
    r_attn.start(1)
    grad_w_gate, grad_w_up = r_feed.total([(hidden_wide, False)] * 2)
    layer_sum = GroupReduce(line, layer_part)
    r_attn.wait(1)
    r_attn.start(2)
    _, grad_tokens, gain_attn_terms = line.run(
        norm_back, own_tokens, gain_one, grad_hidden, *grad_input_sum.terms()
    )
    gain_terms = jnp.concatenate([gain_attn_terms, gain_mlp_terms], axis=0).reshape(2, n, part)
    gain_terms = jnp.take(gain_terms, offsets, axis=1).reshape(2, depth)

    def gain_step(axis, bit):
        nonlocal gain_terms
        size = lax.axis_size(axis)
        other = line.passed(line.send(gain_terms, axis, [(i, i ^ bit) for i in range(size)]))
        gain_terms = line.run(jnp.add, gain_terms, other)

    gain_step("fsdp", 1)
    gain_step("fsdp", 2)
    layer_sum.relay()
    steps = [1 << i for i in range((n - 1).bit_length())]
    for hop in range(2, hops):
        r_attn.wait(hop)
        r_attn.start(hop + 1)
        if hop == 2:
            grad_tokens = line.run(lambda at, v: shuffle(at, n, v), offsets, grad_tokens)
        if hop < hops - 1 and len(steps) > 1:
            gain_step("dp", steps.pop(0))
    layer_own = line.run(lambda at, *v: shuffle(at, n, *v), offsets, hidden, *layer_sum.terms())
    while len(steps) > 1:
        gain_step("dp", steps.pop(0))
    flying = line.send(gain_terms, "dp", [(i, i ^ steps[0]) for i in range(n)])
    r_attn.wait(hops)
    key_wide, value_wide = w_key.shape[1], w_value.shape[1]
    grad_w_attn = r_attn.total(
        [(heads_wide, False), (key_wide, True), (value_wide, True), (heads_wide, True)]
    )
    gain_terms = gain_terms + line.passed(flying)
    gain_own = lax.dynamic_slice(gain_terms, (0, me * part), (2, part))

    return (
        layer_own,
        grad_tokens,
        gain_own[0],
        grad_w_attn[0],
        grad_w_attn[1].T,
        grad_w_attn[2].T,
        grad_w_attn[3],
        gain_own[1],
        grad_w_gate,
        grad_w_up,
        grad_down,
    )


def solution(mesh):
    placed = (
        P(("dp", "fsdp"), None),
        P(("dp", "fsdp")),
        P("dp"),
        P("dp", "fsdp"),
        P("dp", "fsdp"),
        P("dp", "fsdp"),
        P("fsdp", "dp"),
        P("dp"),
        P("dp", "fsdp"),
        P("dp", "fsdp"),
        P("fsdp", "dp"),
        P(("dp", "fsdp"), None),
    )
    return jax.shard_map(
        on_device,
        mesh=mesh,
        in_specs=placed,
        out_specs=(
            P(("dp", "fsdp"), None),
            P(("dp", "fsdp"), None),
            P("dp"),
            P("dp", "fsdp"),
            P("dp", "fsdp"),
            P("dp", "fsdp"),
            P("fsdp", "dp"),
            P("dp"),
            P("dp", "fsdp"),
            P("dp", "fsdp"),
            P("fsdp", "dp"),
        ),
        check_vma=False,
    )
```
